32 devices in a mesh: gx: 4 (over y, x), gy: 8 (over z, core).
Axes of the slice: x: 2, y: 2, z: 4, core: 2. Of those that a mesh axis runs over, the one named last changes fastest.
Arguments:
- inputs: bfloat16 [16, 16, 32, 512], P('gx', 'gy'), may hold values from -6 to 6
- cotangent: bfloat16 [16, 16, 32, 512], P('gx', 'gy'), may hold values from -6 to 6
- point_weight: bfloat16 [32, 32], replicated, may hold values from -1 to 1
- spectral_weight: bfloat16 [2304, 24, 2048], P(('gx', 'gy')), may hold values from -0.75 to 0.75
Outputs:
- grad_input: bfloat16 [16, 16, 32, 512], P('gx', 'gy')
- grad_spectral: float32 [2304, 24, 2048], P(('gx', 'gy'))
The draws below stay inside these ranges and needn't reach their ends.
All inputs are finite; a program needn't handle non-finite values.
Results may differ from the reference program's by a relative error of at most 0.034.
Values may be sent and summed in bfloat16 or wider, within the bound.
No kernel may reach another device: no remote copies, remote signals or barrier semaphores. Data moves between devices by JAX's collectives and lax.ppermute only.
A program may use at most 192 MiB of HBM per device.

```python
import math
import jax
import jax.numpy as jnp
from jax import lax

W = 32
NZ = 64
NT = 8
KX = 24
KY = 24
KZ = 12
KT = 8
NX = 16
NY = 16
MODES = 2304


def shard_levels(rng, dims, split, least, high):
    def one(axis_at, parts):
        draws = jax.random.uniform(jax.random.fold_in(jax.random.fold_in(rng, 6), axis_at), (parts,), jnp.float32, least / len(split), high / len(split))
        return jnp.repeat(jnp.exp(draws), dims[axis_at] // parts).reshape((-1,) + (1,) * (len(dims) - axis_at - 1))

    level = one(*split[0])
    for cut in split[1:]:
        level = level * one(*cut)
    return level


def noise(stream_key, shape, spread, limit, split=(), held_as=jnp.bfloat16):
    gain = shard_levels(stream_key, shape, split, -0.22, 0.18) if split else 1.0
    entries = jax.random.normal(stream_key, shape, jnp.float32) * spread * gain
    return jnp.minimum(jnp.maximum(entries, -limit), limit).astype(held_as)


def setup_inputs(seed: int = 0) -> dict:
    arg_keys = jax.random.split(jax.random.key(seed), 5)
    return {
        "inputs": noise(arg_keys[0], (NX, NY, W, NZ * NT), 1.0, 6.0, ((0, 4), (1, 8))),
        "cotangent": noise(arg_keys[1], (NX, NY, W, NZ * NT), 1.0, 6.0, ((0, 4), (1, 8))),
        "point_weight": noise(arg_keys[2], (W, W), W ** -0.5, 1.0),
        "spectral_weight": noise(arg_keys[3], (MODES, KY, 2 * W * W), (2 * W) ** -0.5, 0.75, ((0, 32),)),
    }


def kept_angles(positions, kept_count, length):
    index = jnp.arange(kept_count, dtype=jnp.int32)
    frequency = jnp.where(index < kept_count // 2, index, index - kept_count)
    turns = positions[:, None] * frequency[None, :] % length
    return turns.astype(jnp.float32) * (2.0 * math.pi / length)

def axis_tables(positions, kept_count, length):
    angles = kept_angles(positions, kept_count, length)
    return (jnp.cos(angles), jnp.sin(angles))

def depth_tables():
    angle_depth = kept_angles(jnp.arange(NZ, dtype=jnp.int32), KZ, NZ)
    angle_time = kept_angles(jnp.arange(NT, dtype=jnp.int32), KT, NT)
    angles = (angle_depth[:, None, :, None] + angle_time[None, :, None, :]).reshape(NZ * NT, KZ * KT)
    return (jnp.cos(angles), jnp.sin(angles))

def settle(values):
    return lax.optimization_barrier(values.astype(jnp.bfloat16))

def rotate(spectra, cosine_table, sine_table, pattern, turn_sign):
    half_width = spectra.shape[-1] // 2
    with_cosine = jnp.einsum(pattern, spectra, cosine_table, precision=lax.Precision.HIGHEST)
    with_sine = jnp.einsum(pattern, spectra, sine_table, precision=lax.Precision.HIGHEST)
    real_part = with_cosine[..., :half_width] + turn_sign * with_sine[..., half_width:]
    imag_part = with_cosine[..., half_width:] - turn_sign * with_sine[..., :half_width]
    return jnp.concatenate([real_part, imag_part], -1)

def depth_forward(field_in, tables, factor):
    widened = field_in.astype(jnp.float32)
    with_cosine = jnp.einsum('xycs,sk->kxyc', widened, tables[0], precision=lax.Precision.HIGHEST)
    with_sine = jnp.einsum('xycs,sk->kxyc', widened, tables[1], precision=lax.Precision.HIGHEST)
    return jnp.concatenate([with_cosine, -with_sine], -1) * factor

def depth_inverse(spectra, tables, factor):
    half_width = spectra.shape[-1] // 2
    with_cosine = jnp.einsum('kxyc,sk->xycs', spectra[..., :half_width], tables[0], precision=lax.Precision.HIGHEST)
    with_sine = jnp.einsum('kxyc,sk->xycs', spectra[..., half_width:], tables[1], precision=lax.Precision.HIGHEST)
    return (with_cosine - with_sine) * factor

def contract_in(left, right):
    return jnp.einsum('mkc,mkco->mko', left, right, precision=lax.Precision.HIGHEST)

def contract_out(left, right):
    return jnp.einsum('mko,mkco->mkc', left, right, precision=lax.Precision.HIGHEST)

def mix_modes(spectra, weight):
    half_width = spectra.shape[-1] // 2
    weight_wide = weight.astype(jnp.float32)
    weight_real, weight_imag = (weight_wide[..., :half_width], weight_wide[..., half_width:])
    real_in, imag_in = (spectra[..., :half_width], spectra[..., half_width:])
    real_out = contract_in(real_in, weight_real) - contract_in(imag_in, weight_imag)
    imag_out = contract_in(real_in, weight_imag) + contract_in(imag_in, weight_real)
    return jnp.concatenate([real_out, imag_out], -1)

def adjoint_modes(spectra, weight):
    half_width = spectra.shape[-1] // 2
    weight_wide = weight.astype(jnp.float32)
    weight_real, weight_imag = (weight_wide[..., :half_width], weight_wide[..., half_width:])
    real_in, imag_in = (spectra[..., :half_width], spectra[..., half_width:])
    real_out = contract_out(real_in, weight_real) + contract_out(imag_in, weight_imag)
    imag_out = contract_out(imag_in, weight_real) - contract_out(real_in, weight_imag)
    return jnp.concatenate([real_out, imag_out], -1)

def partial_outer(left, right):
    return jnp.einsum('mkc,mko->mkco', left, right, precision=lax.Precision.HIGHEST)

def weight_grad(spectra_in, spectra_back):
    half_width = spectra_in.shape[-1] // 2
    real_in, imag_in = (spectra_in[..., :half_width], spectra_in[..., half_width:])
    real_back, imag_back = (spectra_back[..., :half_width], spectra_back[..., half_width:])
    real_part = partial_outer(real_in, real_back) + partial_outer(imag_in, imag_back)
    imag_part = partial_outer(real_in, imag_back) - partial_outer(imag_in, real_back)
    return jnp.concatenate([real_part, imag_part], -1)

def exact_gelu(values):
    return jax.nn.gelu(values, approximate=False)

def reference(inputs, cotangent, point_weight, spectral_weight):
    weight_blocks = spectral_weight.reshape(MODES, KY, W, 2 * W)
    depth_pair = depth_tables()
    whole_x = axis_tables(jnp.arange(NX, dtype=jnp.int32), KX, NX)
    whole_y = axis_tables(jnp.arange(NY, dtype=jnp.int32), KY, NY)
    total_cells = NX * NY * NZ * NT
    kept_total = KX * KY * KZ * KT

    def to_modes(field_in, factor):
        depth_spec = settle(depth_forward(field_in, depth_pair, factor))
        first_spectra = rotate(depth_spec.astype(jnp.float32), whole_x[0], whole_x[1], 'rxyc,xk->rkyc', 1.0)
        first_spectra = settle(first_spectra).reshape(MODES, NY, 2 * W)
        return rotate(first_spectra.astype(jnp.float32), whole_y[0], whole_y[1], 'myc,yk->mkc', 1.0)

    def to_space(spectra, factor):
        back_rows = settle(rotate(spectra, whole_y[0], whole_y[1], 'mkc,yk->myc', -1.0))
        back_rows = back_rows.reshape(KZ * KT, KX, NY, 2 * W)
        back_depth = settle(rotate(back_rows.astype(jnp.float32), whole_x[0], whole_x[1], 'rkyc,xk->rxyc', -1.0))
        return depth_inverse(back_depth.astype(jnp.float32), depth_pair, factor)
    spectra_in = to_modes(inputs, 1.0 / math.sqrt(total_cells))
    mixed = mix_modes(spectra_in, weight_blocks)
    spectral_out = to_space(mixed, 1.0 / math.sqrt(kept_total))
    pointwise = jnp.einsum('xycs,co->xyos', inputs.astype(jnp.float32), point_weight.astype(jnp.float32), precision=lax.Precision.HIGHEST)
    before = spectral_out + pointwise
    unused_out, pullback = jax.vjp(exact_gelu, before)
    slope = settle(pullback(cotangent.astype(jnp.float32))[0])
    spectra_back = to_modes(slope, 1.0 / math.sqrt(kept_total))
    grad_spectral = weight_grad(spectra_in, spectra_back).reshape(MODES, KY, 2 * W * W)
    adjoint = adjoint_modes(spectra_back, weight_blocks)
    spectral_grad = to_space(adjoint, 1.0 / math.sqrt(total_cells))
    pointwise_grad = jnp.einsum('xyos,co->xycs', slope.astype(jnp.float32), point_weight.astype(jnp.float32), precision=lax.Precision.HIGHEST)
    grad_input = (pointwise_grad + spectral_grad).astype(jnp.bfloat16)
    return (grad_input, grad_spectral)
```

```python
import functools
import math

import jax
import jax.numpy as jnp
import numpy as np
from jax import lax
from jax.experimental import pallas as pl
from jax.experimental.pallas import tpu as pltpu
from jax.sharding import PartitionSpec as P

NZ = 64
NT = 8
KX = 24
KY = 24
KZ = 12
KT = 8
SLOTS = 8
GRID_AXES = ("gx", "gy")
VMEM_BYTES = 56 * 1024 * 1024


def table_angles(positions, kept_count, length):
    index = np.arange(kept_count)
    frequency = np.where(index < kept_count // 2, index, index - kept_count)
    turns = (np.asarray(positions)[:, None] * frequency[None, :]) % length
    return 2.0 * np.pi * turns / length


def depth_table(share):
    angles = (
        table_angles(np.arange(NZ), KZ, NZ)[:, None, :, None]
        + table_angles(np.arange(NT), KT, NT)[None, :, None, :]
    ).reshape(NZ * NT, KZ * KT)
    parts = np.stack([np.cos(angles), -np.sin(angles)], -1)
    owners = KZ * KT // share
    rows = np.zeros((owners, SLOTS, NZ * NT))
    rows[:, : 2 * share] = parts.reshape(NZ * NT, owners, 2 * share).transpose(1, 2, 0)
    return rows.reshape(owners * SLOTS, NZ * NT).astype(jnp.bfloat16)


def plane_tables(count_gx, count_gy, rows_x, rows_y):
    length_x, length_y = count_gx * rows_x, count_gy * rows_y
    angle_x = table_angles(np.arange(length_x), KX, length_x).T.reshape(KX, 1, count_gx, 1, rows_x, 1)
    angle_y = table_angles(np.arange(length_y), KY, length_y).T.reshape(1, KY, 1, count_gy, 1, rows_y)
    angles = (angle_x + angle_y).transpose(0, 1, 4, 5, 2, 3).reshape(KX * KY, length_x * length_y)
    forward = np.concatenate([np.cos(angles), np.sin(angles)], 1)
    inverse = np.concatenate([np.cos(angles.T), np.sin(angles.T)], 1)
    return forward.astype(jnp.bfloat16), inverse.astype(jnp.bfloat16)


def dot(left, right, left_dim=1, right_dim=0):
    return lax.dot_general(
        left, right, (((left_dim,), (right_dim,)), ((), ())), preferred_element_type=jnp.float32
    )


def depth_kernel(factor, table_ref, field_ref, sent_ref):
    spectra = dot(table_ref[...], field_ref[...], 1, 1)
    sent_ref[...] = (spectra * factor).astype(jnp.bfloat16)


def gather_cells(mode, wide_ref, channels):
    halves, rows, lanes = wide_ref.shape
    devices = rows // SLOTS
    parts = []
    for part in range(2):
        pieces = []
        for h in range(halves):
            piece = wide_ref[h, pl.ds(mode * 2 + part, devices, stride=SLOTS), :]
            pieces += [piece[:, c * channels : (c + 1) * channels] for c in range(lanes // channels)]
        parts.append(jnp.concatenate(pieces, 0))
    return parts


def scatter_cells(mode, spectra, out_ref, channels):
    halves, rows, lanes = out_ref.shape
    devices = rows // SLOTS
    each = lanes // channels
    for part in range(2):
        columns = slice(part * channels, (part + 1) * channels)
        for h in range(halves):
            pieces = [spectra[c * devices : (c + 1) * devices, columns] for c in range(h * each, (h + 1) * each)]
            out_ref[h, pl.ds(mode * 2 + part, devices, stride=SLOTS), :] = jnp.concatenate(pieces, 1)


def spread_matrix(channels):
    wide = 2 * channels
    row = lax.broadcasted_iota(jnp.int32, (wide, wide * wide), 0)
    column = lax.broadcasted_iota(jnp.int32, (wide, wide * wide), 1)
    return jnp.where(column // wide == row, 1.0, 0.0).astype(jnp.bfloat16)


def mix_kernel(
    channels, arrived_ref, weight_ref, forward_ref, inverse_ref, sent_ref, kept_ref,
    wide_ref, plane_ref, modes_ref, pair_ref, spread_ref, out_ref,
):
    mode, block = pl.program_id(0), pl.program_id(1)
    rows_x, rows_y, flat = weight_ref.shape
    block_rows = rows_x * rows_y
    plane = modes_ref.shape[0]
    tiles = flat // 128

    @pl.when((mode == 0) & (block == 0))
    def _():
        for h in range(wide_ref.shape[0]):
            wide_ref[h] = arrived_ref[:, h * 128 : (h + 1) * 128].astype(jnp.float32)
        out_ref[...] = jnp.zeros_like(out_ref)
        spread_ref[...] = spread_matrix(channels)

    @pl.when(block == 0)
    def _():
        real, imag = gather_cells(mode, wide_ref, channels)
        half = real.shape[0]
        plane_ref[:half, :] = jnp.concatenate([real, imag], 1).astype(jnp.bfloat16)
        plane_ref[half:, :] = jnp.concatenate([imag, -real], 1).astype(jnp.bfloat16)
        modes_ref[...] = dot(forward_ref[...], plane_ref[...])
        kept_ref[...] = modes_ref[...].astype(jnp.bfloat16)

    for r in range(rows_x):
        start = block * block_rows + r * rows_y
        start = pl.multiple_of(start, 8)
        entries = modes_ref[pl.ds(start, rows_y), :].astype(jnp.bfloat16)
        spread = dot(entries, spread_ref[...])
        weight = weight_ref[r].astype(jnp.float32)
        by_real = jnp.zeros((rows_y, 128), jnp.float32)
        by_imag = jnp.zeros((rows_y, 128), jnp.float32)
        for t in range(tiles):
            tile = weight[:, t * 128 : (t + 1) * 128]
            by_real += spread[:, t * 128 : (t + 1) * 128] * tile
            by_imag += spread[:, flat + t * 128 : flat + (t + 1) * 128] * tile
        pair_ref[pl.ds(start, rows_y), :] = jnp.concatenate([by_real, by_imag], 1)
        pair_ref[pl.ds(plane + start, rows_y), :] = jnp.concatenate([-by_imag, by_real], 1)

    @pl.when(block == pl.num_programs(1) - 1)
    def _():
        total = dot(inverse_ref[...], pair_ref[...].astype(jnp.bfloat16))
        first, second = total[:, :128], total[:, 128:]
        first = first[:, :64] + first[:, 64:]
        second = second[:, :64] + second[:, 64:]
        turned = jnp.concatenate([-second[:, channels:], second[:, :channels]], 1)
        scatter_cells(mode, first + turned, out_ref, channels)

    @pl.when((mode == pl.num_programs(0) - 1) & (block == pl.num_programs(1) - 1))
    def _():
        for h in range(out_ref.shape[0]):
            sent_ref[:, h * 128 : (h + 1) * 128] = out_ref[h].astype(jnp.bfloat16)


def adjoint_kernel(
    channels, arrived_ref, weight_ref, forward_ref, inverse_ref, sent_ref, kept_ref,
    wide_ref, plane_ref, modes_ref, pair_ref, sum_ref, product_ref, out_ref,
):
    mode, block = pl.program_id(0), pl.program_id(1)
    rows_x, rows_y, flat = weight_ref.shape
    block_rows = rows_x * rows_y
    plane = modes_ref.shape[0]
    tiles = flat // 128
    wide = 2 * channels

    @pl.when((mode == 0) & (block == 0))
    def _():
        for h in range(wide_ref.shape[0]):
            wide_ref[h] = arrived_ref[:, h * 128 : (h + 1) * 128].astype(jnp.float32)
        out_ref[...] = jnp.zeros_like(out_ref)
        row = lax.broadcasted_iota(jnp.int32, (2 * flat, 2 * wide), 0)
        column = lax.broadcasted_iota(jnp.int32, (2 * flat, 2 * wide), 1)
        own = (row % flat) // wide == column % channels
        slot = column // channels
        real = jnp.where(own & ((slot == 0) | (slot == 3)), 1.0, 0.0)
        imag = jnp.where(own & (slot == 1), 1.0, jnp.where(own & (slot == 2), -1.0, 0.0))
        sum_ref[...] = jnp.where(row < flat, real, imag).astype(jnp.bfloat16)

    @pl.when(block == 0)
    def _():
        real, imag = gather_cells(mode, wide_ref, channels)
        half = real.shape[0]
        once = jnp.concatenate([real, imag], 1)
        turn = jnp.concatenate([imag, -real], 1)
        plane_ref[:half, :] = jnp.concatenate([once, once, turn, turn], 1).astype(jnp.bfloat16)
        plane_ref[half:, :] = jnp.concatenate([turn, turn, -once, -once], 1).astype(jnp.bfloat16)
        modes_ref[...] = dot(forward_ref[...], plane_ref[...])
        kept_ref[...] = modes_ref[...].astype(jnp.bfloat16)

    for r in range(rows_x):
        start = block * block_rows + r * rows_y
        start = pl.multiple_of(start, 8)
        entries = modes_ref[pl.ds(start, rows_y), :].astype(jnp.bfloat16)
        here, turned = entries[:, :128], entries[:, 128:]
        weight = weight_ref[r]
        for t in range(tiles):
            tile = weight[:, t * 128 : (t + 1) * 128]
            product_ref[:, t * 128 : (t + 1) * 128] = here * tile
            product_ref[:, flat + t * 128 : flat + (t + 1) * 128] = turned * tile
        summed = dot(product_ref[...], sum_ref[...])
        pair_ref[pl.ds(start, rows_y), :] = summed[:, :wide]
        pair_ref[pl.ds(plane + start, rows_y), :] = summed[:, wide:]

    @pl.when(block == pl.num_programs(1) - 1)
    def _():
        total = dot(inverse_ref[...], pair_ref[...].astype(jnp.bfloat16))
        scatter_cells(mode, total, out_ref, channels)

    @pl.when((mode == pl.num_programs(0) - 1) & (block == pl.num_programs(1) - 1))
    def _():
        for h in range(out_ref.shape[0]):
            sent_ref[:, h * 128 : (h + 1) * 128] = out_ref[h].astype(jnp.bfloat16)


def outer_kernel(channels, in_ref, back_ref, grad_ref, spread_ref):
    rows_x, rows_y, flat = grad_ref.shape
    tiles = flat // 128

    @pl.when(pl.program_id(0) == 0)
    def _():
        spread_ref[...] = spread_matrix(channels)

    for r in range(rows_x):
        entries = in_ref[r * rows_y : (r + 1) * rows_y, :]
        back = back_ref[r * rows_y : (r + 1) * rows_y, :].astype(jnp.float32)
        here, turned = back[:, :128], back[:, 128:]
        spread = dot(entries, spread_ref[...])
        for t in range(tiles):
            grad_ref[r, :, t * 128 : (t + 1) * 128] = (
                spread[:, t * 128 : (t + 1) * 128] * here
                + spread[:, flat + t * 128 : flat + (t + 1) * 128] * turned
            )


def slope_kernel(
    cells, channels, factor, arrived_ref, table_ref, field_ref, cotangent_ref, point_ref, slope_ref, sent_ref
):
    spectral = dot(arrived_ref[...], table_ref[...], 0, 0)
    for c in range(cells):
        rows = slice(c * channels, (c + 1) * channels)
        before = spectral[rows] * factor + dot(point_ref[...], field_ref[rows, :], 0, 0)
        cumulative = 0.5 + 0.5 * lax.erf(before * math.sqrt(0.5))
        density = jnp.exp(-0.5 * before * before) * (1.0 / math.sqrt(2.0 * math.pi))
        slope = cotangent_ref[rows, :].astype(jnp.float32) * (cumulative + before * density)
        slope_ref[rows, :] = slope.astype(jnp.bfloat16)
    sent = dot(table_ref[...], slope_ref[...], 1, 1)
    sent_ref[...] = (sent * factor).astype(jnp.bfloat16)


def final_kernel(cells, channels, factor, arrived_ref, table_ref, slope_ref, point_ref, grad_ref):
    spectral = dot(arrived_ref[...], table_ref[...], 0, 0)
    for c in range(cells):
        rows = slice(c * channels, (c + 1) * channels)
        pointwise = dot(point_ref[...], slope_ref[rows, :])
        grad_ref[rows, :] = (pointwise + spectral[rows] * factor).astype(jnp.bfloat16)


def params(semantics=None):
    return pltpu.CompilerParams(dimension_semantics=semantics, vmem_limit_bytes=VMEM_BYTES)


def shape(dims, dtype=jnp.bfloat16):
    return jax.ShapeDtypeStruct(dims, dtype)


def per_device(inputs, cotangent, point_weight, spectral_weight):
    rows_x, rows_y, channels, depth = inputs.shape
    mode_rows, mode_cols, flat = spectral_weight.shape
    count_gx, count_gy = lax.axis_size("gx"), lax.axis_size("gy")
    devices = count_gx * count_gy
    share = mode_rows // KX
    cells = rows_x * rows_y
    lanes = cells * channels
    wide = 2 * channels
    plane = KX * KY
    points = cells * devices
    slots = devices * SLOTS
    inner = 1.0 / math.sqrt(points * depth)
    outer = 1.0 / math.sqrt(plane * KZ * KT)

    table = jnp.asarray(depth_table(share))
    forward, inverse = (jnp.asarray(t) for t in plane_tables(count_gx, count_gy, rows_x, rows_y))
    field = inputs.reshape(lanes, depth)
    seed = cotangent.reshape(lanes, depth)

    def exchange(sent):
        blocks = sent.reshape(devices, SLOTS, lanes)
        return lax.all_to_all(blocks, GRID_AXES, split_axis=0, concat_axis=0, tiled=True).reshape(slots, lanes)

    steps = 2
    block_x = KX // steps
    whole = lambda dims: pl.BlockSpec(dims, lambda k, b: (0,) * len(dims))
    weight_spec = pl.BlockSpec((block_x, mode_cols, flat), lambda k, b: (k * steps + b, 0, 0))

    sent = pl.pallas_call(
        functools.partial(depth_kernel, inner), out_shape=shape((slots, lanes)), compiler_params=params(),
        name="depth",
    )(table, field)
    arrived = exchange(sent)
    sent, kept_in = pl.pallas_call(
        functools.partial(mix_kernel, channels),
        grid=(share, steps),
        in_specs=[whole((slots, lanes)), weight_spec, whole((plane, 2 * points)), whole((points, 2 * plane))],
        out_specs=[whole((slots, lanes)), pl.BlockSpec((plane, wide), lambda k, b: (k, 0))],
        out_shape=[shape((slots, lanes)), shape((share * plane, wide))],
        scratch_shapes=[
            pltpu.VMEM((lanes // 128, slots, 128), jnp.float32),
            pltpu.VMEM((2 * points, wide), jnp.bfloat16),
            pltpu.VMEM((plane, wide), jnp.float32),
            pltpu.VMEM((2 * plane, 256), jnp.float32),
            pltpu.VMEM((wide, wide * wide), jnp.bfloat16),
            pltpu.VMEM((lanes // 128, slots, 128), jnp.float32),
        ],
        compiler_params=params(("arbitrary", "arbitrary")),
        name="mix",
    )(arrived, spectral_weight, forward, inverse)
    arrived = exchange(sent)
    slope, sent = pl.pallas_call(
        functools.partial(slope_kernel, cells, channels, outer),
        out_shape=[shape((lanes, depth)), shape((slots, lanes))], compiler_params=params(),
        name="slope",
    )(arrived, table, field, seed, point_weight)
    arrived = exchange(sent)
    sent, kept_back = pl.pallas_call(
        functools.partial(adjoint_kernel, channels),
        grid=(share, steps),
        in_specs=[whole((slots, lanes)), weight_spec, whole((plane, 2 * points)), whole((points, 2 * plane))],
        out_specs=[whole((slots, lanes)), pl.BlockSpec((plane, 256), lambda k, b: (k, 0))],
        out_shape=[shape((slots, lanes)), shape((share * plane, 256))],
        scratch_shapes=[
            pltpu.VMEM((lanes // 128, slots, 128), jnp.float32),
            pltpu.VMEM((2 * points, 256), jnp.bfloat16),
            pltpu.VMEM((plane, 256), jnp.float32),
            pltpu.VMEM((2 * plane, wide), jnp.float32),
            pltpu.VMEM((2 * flat, 2 * wide), jnp.bfloat16),
            pltpu.VMEM((mode_cols, 2 * flat), jnp.bfloat16),
            pltpu.VMEM((lanes // 128, slots, 128), jnp.float32),
        ],
        compiler_params=params(("arbitrary", "arbitrary")),
        name="adjoint",
    )(arrived, spectral_weight, forward, inverse)
    arrived = exchange(sent)
    grad_x = 6
    grad_spectral = pl.pallas_call(
        functools.partial(outer_kernel, channels),
        grid=(mode_rows // grad_x,),
        in_specs=[
            pl.BlockSpec((grad_x * mode_cols, wide), lambda i: (i, 0)),
            pl.BlockSpec((grad_x * mode_cols, 256), lambda i: (i, 0)),
        ],
        out_specs=pl.BlockSpec((grad_x, mode_cols, flat), lambda i: (i, 0, 0)),
        out_shape=shape((mode_rows, mode_cols, flat), jnp.float32),
        scratch_shapes=[pltpu.VMEM((wide, wide * wide), jnp.bfloat16)],
        compiler_params=params(("arbitrary",)),
        cost_estimate=pl.CostEstimate(flops=2 * mode_rows * mode_cols * flat * wide * 2, transcendentals=0,
                                      bytes_accessed=mode_rows * mode_cols * flat * 4),
        name="outer",
    )(kept_in, kept_back)
    grad_input = pl.pallas_call(
        functools.partial(final_kernel, cells, channels, inner), out_shape=shape((lanes, depth)),
        compiler_params=params(), name="final",
    )(arrived, table, slope, point_weight)
    return grad_input.reshape(inputs.shape), grad_spectral


def kept_angles(positions, kept_count, length):
    index = jnp.arange(kept_count, dtype=jnp.int32)
    frequency = jnp.where(index < kept_count // 2, index, index - kept_count)
    turns = positions[:, None] * frequency[None, :] % length
    return turns.astype(jnp.float32) * (2.0 * math.pi / length)


def axis_tables(positions, kept_count, length):
    angles = kept_angles(positions, kept_count, length)
    return (jnp.cos(angles), jnp.sin(angles))


def depth_tables():
    angle_depth = kept_angles(jnp.arange(NZ, dtype=jnp.int32), KZ, NZ)
    angle_time = kept_angles(jnp.arange(NT, dtype=jnp.int32), KT, NT)
    angles = (angle_depth[:, None, :, None] + angle_time[None, :, None, :]).reshape(
        NZ * NT, KZ * KT
    )
    return (jnp.cos(angles), jnp.sin(angles))


def settle(values):
    return lax.optimization_barrier(values.astype(jnp.bfloat16))


def rotate(spectra, cosine_table, sine_table, pattern, turn_sign):
    half_width = spectra.shape[-1] // 2
    with_cosine = jnp.einsum(pattern, spectra, cosine_table, precision=lax.Precision.HIGHEST)
    with_sine = jnp.einsum(pattern, spectra, sine_table, precision=lax.Precision.HIGHEST)
    real_part = with_cosine[..., :half_width] + turn_sign * with_sine[..., half_width:]
    imag_part = with_cosine[..., half_width:] - turn_sign * with_sine[..., :half_width]
    return jnp.concatenate([real_part, imag_part], -1)


def depth_forward(field_in, tables, factor):
    widened = field_in.astype(jnp.float32)
    with_cosine = jnp.einsum("xycs,sk->kxyc", widened, tables[0], precision=lax.Precision.HIGHEST)
    with_sine = jnp.einsum("xycs,sk->kxyc", widened, tables[1], precision=lax.Precision.HIGHEST)
    return jnp.concatenate([with_cosine, -with_sine], -1) * factor


def depth_inverse(spectra, tables, factor):
    half_width = spectra.shape[-1] // 2
    with_cosine = jnp.einsum(
        "kxyc,sk->xycs", spectra[..., :half_width], tables[0], precision=lax.Precision.HIGHEST
    )
    with_sine = jnp.einsum(
        "kxyc,sk->xycs", spectra[..., half_width:], tables[1], precision=lax.Precision.HIGHEST
    )
    return (with_cosine - with_sine) * factor


def contract_in(left, right):
    return jnp.einsum("mkc,mkco->mko", left, right, precision=lax.Precision.HIGHEST)


def contract_out(left, right):
    return jnp.einsum("mko,mkco->mkc", left, right, precision=lax.Precision.HIGHEST)


def partial_outer(left, right):
    return jnp.einsum("mkc,mko->mkco", left, right, precision=lax.Precision.HIGHEST)


def mix_modes(spectra, weight):
    half_width = spectra.shape[-1] // 2
    weight_wide = weight.astype(jnp.float32)
    weight_real, weight_imag = (weight_wide[..., :half_width], weight_wide[..., half_width:])
    real_in, imag_in = (spectra[..., :half_width], spectra[..., half_width:])
    real_out = contract_in(real_in, weight_real) - contract_in(imag_in, weight_imag)
    imag_out = contract_in(real_in, weight_imag) + contract_in(imag_in, weight_real)
    return jnp.concatenate([real_out, imag_out], -1)


def adjoint_modes(spectra, weight):
    half_width = spectra.shape[-1] // 2
    weight_wide = weight.astype(jnp.float32)
    weight_real, weight_imag = (weight_wide[..., :half_width], weight_wide[..., half_width:])
    real_in, imag_in = (spectra[..., :half_width], spectra[..., half_width:])
    real_out = contract_out(real_in, weight_real) + contract_out(imag_in, weight_imag)
    imag_out = contract_out(imag_in, weight_real) - contract_out(real_in, weight_imag)
    return jnp.concatenate([real_out, imag_out], -1)


def weight_grad(spectra_in, spectra_back):
    half_width = spectra_in.shape[-1] // 2
    real_in, imag_in = (spectra_in[..., :half_width], spectra_in[..., half_width:])
    real_back, imag_back = (spectra_back[..., :half_width], spectra_back[..., half_width:])
    real_part = partial_outer(real_in, real_back) + partial_outer(imag_in, imag_back)
    imag_part = partial_outer(real_in, imag_back) - partial_outer(imag_in, real_back)
    return jnp.concatenate([real_part, imag_part], -1)


def exact_gelu(values):
    return jax.nn.gelu(values, approximate=False)


def general_per_device(inputs, cotangent, point_weight, spectral_weight):
    rows_x, rows_y, channels, cells = inputs.shape
    mode_rows, mode_cols, flat_width = spectral_weight.shape
    weight_blocks = spectral_weight.reshape(mode_rows, mode_cols, channels, 2 * channels)
    count_gx = lax.axis_size("gx")
    count_gy = lax.axis_size("gy")
    length_x = rows_x * count_gx
    length_y = rows_y * count_gy
    depth_pair = depth_tables()
    own_x = lax.axis_index("gx") * rows_x + jnp.arange(rows_x, dtype=jnp.int32)
    local_x = axis_tables(own_x, KX, length_x)
    whole_y = axis_tables(jnp.arange(length_y, dtype=jnp.int32), KY, length_y)
    total_cells = length_x * length_y * cells
    kept_total = KX * KY * KZ * KT

    def to_modes(field_in, factor):
        depth_spec = settle(depth_forward(field_in, depth_pair, factor))
        share = depth_spec.shape[0] // count_gx
        first_spectra = lax.psum_scatter(
            rotate(
                depth_spec.astype(jnp.float32), local_x[0], local_x[1], "rxyc,xk->rkyc", 1.0
            ).astype(jnp.bfloat16),
            "gx",
            scatter_dimension=0,
            tiled=True,
        ).astype(jnp.float32)
        first_spectra = settle(first_spectra).reshape(share * KX, rows_y, 2 * channels)
        arrived_modes = lax.all_to_all(first_spectra, "gy", split_axis=0, concat_axis=1, tiled=True)
        return rotate(arrived_modes.astype(jnp.float32), whole_y[0], whole_y[1], "myc,yk->mkc", 1.0)

    def to_space(spectra, factor):
        back_rows = settle(rotate(spectra, whole_y[0], whole_y[1], "mkc,yk->myc", -1.0))
        returned = lax.all_to_all(back_rows, "gy", split_axis=1, concat_axis=0, tiled=True)
        share = returned.shape[0] // KX
        returned = returned.reshape(share, KX, rows_y, 2 * channels)
        back_depth = settle(
            rotate(
                lax.all_gather(returned, "gx", axis=0, tiled=True).astype(jnp.float32),
                local_x[0],
                local_x[1],
                "rkyc,xk->rxyc",
                -1.0,
            )
        )
        return depth_inverse(back_depth.astype(jnp.float32), depth_pair, factor)

    spectra_in = to_modes(inputs, 1.0 / math.sqrt(total_cells))
    mixed = mix_modes(spectra_in, weight_blocks)
    spectral_out = to_space(mixed, 1.0 / math.sqrt(kept_total))
    pointwise = jnp.einsum(
        "xycs,co->xyos", inputs, point_weight, preferred_element_type=jnp.float32
    )
    before = spectral_out + pointwise
    unused_out, pullback = jax.vjp(exact_gelu, before)
    slope = settle(pullback(cotangent.astype(jnp.float32))[0])
    spectra_back = to_modes(slope, 1.0 / math.sqrt(kept_total))
    grad_spectral = weight_grad(spectra_in, spectra_back).reshape(mode_rows, mode_cols, flat_width)
    adjoint = adjoint_modes(spectra_back, weight_blocks)
    spectral_grad = to_space(adjoint, 1.0 / math.sqrt(total_cells))
    pointwise_grad = jnp.einsum(
        "xyos,co->xycs", slope, point_weight, preferred_element_type=jnp.float32
    )
    grad_input = (pointwise_grad + spectral_grad).astype(jnp.bfloat16)
    return (grad_input, grad_spectral)


def solution(mesh):
    count_gx, count_gy = mesh.shape["gx"], mesh.shape["gy"]
    placed = (
        P("gx", "gy", None, None),
        P("gx", "gy", None, None),
        P(),
        P(("gx", "gy"), None, None),
    )

    def program(inputs, cotangent, point_weight, spectral_weight):
        cells = inputs.shape[0] * inputs.shape[1] // (count_gx * count_gy)
        whole_modes = KZ * KT % (count_gx * count_gy) == 0
        fits = whole_modes and 2 * KZ * KT // (count_gx * count_gy) <= SLOTS
        fits = fits and inputs.shape[2] == 32 and cells * inputs.shape[2] == 256
        return jax.shard_map(
            per_device if fits else general_per_device,
            mesh=mesh,
            in_specs=placed,
            out_specs=(P("gx", "gy", None, None), P(("gx", "gy"), None, None)),
            check_vma=False,
        )(inputs, cotangent, point_weight, spectral_weight)

    return program
```

```python
import functools
import math

import jax
import jax.numpy as jnp
import numpy as np
from jax import lax
from jax.experimental import pallas as pl
from jax.experimental.pallas import tpu as pltpu
from jax.sharding import PartitionSpec as P

NZ = 64
NT = 8
KX = 24
KY = 24
KZ = 12
KT = 8
SLOTS = 8
LANES = 128
GROUP = 4
ROWS = 16
READ_AHEAD_FLOPS = 10**11
GRID_AXES = ("gx", "gy")


def table_angles(positions, kept_count, length):
    index = np.arange(kept_count)
    frequency = np.where(index < kept_count // 2, index, index - kept_count)
    turns = (np.asarray(positions)[:, None] * frequency[None, :]) % length
    return 2.0 * np.pi * turns / length


def depth_table(share):
    angles = (
        table_angles(np.arange(NZ), KZ, NZ)[:, None, :, None]
        + table_angles(np.arange(NT), KT, NT)[None, :, None, :]
    ).reshape(NZ * NT, KZ * KT)
    parts = np.stack([np.cos(angles), -np.sin(angles)], -1)
    owners = KZ * KT // share
    rows = np.zeros((owners, SLOTS, NZ * NT))
    rows[:, : 2 * share] = parts.reshape(NZ * NT, owners, 2 * share).transpose(1, 2, 0)
    return rows.reshape(owners * SLOTS, NZ * NT).astype(jnp.bfloat16)


def plane_tables(count_gx, count_gy, rows_x, rows_y):
    length_x, length_y = count_gx * rows_x, count_gy * rows_y
    angle_x = table_angles(np.arange(length_x), KX, length_x).T.reshape(KX, 1, 1, 1, count_gx, 1, rows_x, 1)
    angle_y = table_angles(np.arange(length_y), KY, length_y).T.reshape(1, KY, 1, 1, 1, count_gy, 1, rows_y)
    angles = (angle_x + angle_y).transpose(0, 1, 2, 3, 6, 7, 4, 5).reshape(KX * KY, length_x * length_y)
    pad = ((0, -KX * KY % LANES), (0, 0))
    cosine, sine = np.pad(np.cos(angles), pad), np.pad(np.sin(angles), pad)
    forward = np.concatenate([cosine.T, sine.T], 0)
    inverse = np.concatenate([cosine.T, sine.T], 1)
    return forward.astype(jnp.bfloat16), inverse.astype(jnp.bfloat16)


def dot(left, right, left_dim=1, right_dim=0):
    return lax.dot_general(
        left, right, (((left_dim,), (right_dim,)), ((), ())), preferred_element_type=jnp.float32
    )


def depth_kernel(factor, table_ref, field_ref, sent_ref):
    spectra = dot(table_ref[...], field_ref[...], 1, 1)
    sent_ref[...] = (spectra * factor).astype(jnp.bfloat16)


def to_plane_modes(share, channels, arrived_ref, forward_ref, wide_ref, modes_ref):
    halves, rows, lanes = wide_ref.shape
    devices = rows // SLOTS
    for h in range(halves):
        wide_ref[h] = arrived_ref[:, h * LANES : (h + 1) * LANES].astype(jnp.float32)
    columns = []
    for slot in range(2 * share):
        pieces = []
        for h in range(halves):
            piece = wide_ref[h, pl.ds(slot, devices, stride=SLOTS), :]
            pieces += [piece[:, c * channels : (c + 1) * channels] for c in range(lanes // channels)]
        columns.append(jnp.concatenate(pieces, 0))
    cells = jnp.concatenate(columns, 1).T
    blocks = []
    for k in range(share):
        real = cells[2 * k * channels : (2 * k + 1) * channels]
        imag = cells[(2 * k + 1) * channels : (2 * k + 2) * channels]
        blocks += [jnp.concatenate([real, imag], 1), jnp.concatenate([imag, -real], 1)]
    modes = dot(jnp.concatenate(blocks, 0).astype(jnp.bfloat16), forward_ref[...])
    each = modes_ref.shape[0] // share
    for k in range(share):
        for j in range(each):
            modes_ref[k * each + j] = modes[2 * k * channels : (2 * k + 2) * channels, j * LANES : (j + 1) * LANES]


def store_pair(tile, share, channels, real, imag, pair_ref):
    pair_ref[tile, :channels, :LANES] = real.astype(jnp.bfloat16)
    pair_ref[tile, channels:, :LANES] = imag.astype(jnp.bfloat16)
    pair_ref[tile, :channels, LANES:] = (-imag).astype(jnp.bfloat16)
    pair_ref[tile, channels:, LANES:] = real.astype(jnp.bfloat16)


def to_cells(share, channels, pair_ref, inverse_ref, out_ref, sent_ref):
    halves, rows, lanes = out_ref.shape
    devices = rows // SLOTS
    each = pair_ref.shape[0] // share
    padded = each * LANES
    out_ref[...] = jnp.zeros_like(out_ref)
    spectra = []
    for k in range(share):
        cosine = jnp.concatenate([pair_ref[k * each + j, :, :LANES] for j in range(each)], 1)
        sine = jnp.concatenate([pair_ref[k * each + j, :, LANES:] for j in range(each)], 1)
        spectra.append(jnp.concatenate([cosine, sine], 1))
    total = dot(inverse_ref[...], jnp.concatenate(spectra, 0), 1, 1)
    per_half = lanes // channels
    for slot in range(2 * share):
        columns = slice(slot * channels, (slot + 1) * channels)
        for h in range(halves):
            pieces = [total[c * devices : (c + 1) * devices, columns] for c in range(h * per_half, (h + 1) * per_half)]
            out_ref[h, pl.ds(slot, devices, stride=SLOTS), :] = jnp.concatenate(pieces, 1)
    for h in range(halves):
        sent_ref[:, h * LANES : (h + 1) * LANES] = out_ref[h].astype(jnp.bfloat16)


def mix_kernel(
    share, channels, plane, arrived_ref, weight_ref, forward_ref, inverse_ref, sent_ref, modes_ref, turned_ref,
    wide_ref, pair_ref,
):
    to_plane_modes(share, channels, arrived_ref, forward_ref, wide_ref, modes_ref)
    wide = 2 * channels
    each = modes_ref.shape[0] // share

    @pl.loop(0, share)
    def _(k):
        for j in range(each):
            tile = k * each + j
            count = min(LANES, plane - j * LANES)
            rows = pl.ds(pl.multiple_of(k * plane + j * LANES, 64), count)
            by_real = jnp.zeros((wide, LANES), jnp.float32)
            by_imag = jnp.zeros((wide, LANES), jnp.float32)
            for first in range(0, channels, GROUP):
                real_sum, imag_sum = None, None
                for c in range(first, first + GROUP, LANES // wide):
                    block = weight_ref[rows, c * wide : c * wide + LANES].T
                    if count < LANES:
                        block = jnp.concatenate([block, jnp.zeros((LANES, LANES - count), jnp.bfloat16)], 1)
                    turned_ref[tile, c * wide : c * wide + LANES, :] = block
                    for h in range(LANES // wide):
                        weight = block[h * wide : (h + 1) * wide]
                        real = jnp.broadcast_to(modes_ref[tile, c + h : c + h + 1, :], (wide, LANES))
                        imag = jnp.broadcast_to(
                            modes_ref[tile, channels + c + h : channels + c + h + 1, :], (wide, LANES)
                        )
                        real, imag = real.astype(jnp.bfloat16) * weight, imag.astype(jnp.bfloat16) * weight
                        real_sum = real if real_sum is None else real_sum + real
                        imag_sum = imag if imag_sum is None else imag_sum + imag
                by_real += real_sum.astype(jnp.float32)
                by_imag += imag_sum.astype(jnp.float32)
            store_pair(
                tile, share, channels, by_real[:channels] - by_imag[channels:],
                by_real[channels:] + by_imag[:channels], pair_ref,
            )

    to_cells(share, channels, pair_ref, inverse_ref, wide_ref, sent_ref)


def adjoint_kernel(
    share, channels, arrived_ref, turned_ref, forward_ref, inverse_ref, sent_ref, modes_ref, wide_ref, pair_ref,
    part_ref,
):
    to_plane_modes(share, channels, arrived_ref, forward_ref, wide_ref, modes_ref)
    wide = 2 * channels
    tiles = modes_ref.shape[0]

    @pl.loop(0, tiles)
    def _(tile):
        real, imag = modes_ref[tile, :channels, :], modes_ref[tile, channels:, :]
        here = jnp.concatenate([real, imag], 0).astype(jnp.bfloat16)
        turn = jnp.concatenate([imag, -real], 0).astype(jnp.bfloat16)
        for c in range(channels):
            weight = turned_ref[tile, c * wide : (c + 1) * wide, :]
            for part, factor in enumerate((here, turn)):
                product = factor * weight
                while product.shape[0] > ROWS:
                    half = product.shape[0] // 2
                    product = product[:half] + product[half:]
                part_ref[tile, (part * channels + c) * ROWS : (part * channels + c + 1) * ROWS, :] = product

    row = lax.broadcasted_iota(jnp.int32, (wide, ROWS * wide), 0)
    column = lax.broadcasted_iota(jnp.int32, (wide, ROWS * wide), 1)
    groups = jnp.where(column // ROWS == row, 1.0, 0.0).astype(jnp.bfloat16)
    for tile in range(tiles):
        summed = dot(groups, part_ref[tile])
        store_pair(tile, share, channels, summed[:channels], summed[channels:], pair_ref)

    to_cells(share, channels, pair_ref, inverse_ref, wide_ref, sent_ref)


def outer_kernel(share, channels, plane, in_ref, back_ref, grad_ref, held_ref, sems):
    wide = 2 * channels
    each = in_ref.shape[0] // share
    per_block = LANES // wide

    def copy(k, j):
        rows = pl.ds(pl.multiple_of(k * plane + j * LANES, 64), min(LANES, plane - j * LANES))
        return pltpu.make_async_copy(held_ref.at[rows], grad_ref.at[rows], sems.at[k * each + j])

    @pl.loop(0, share)
    def _(k):
        for j in range(each):
            tile = k * each + j
            count = min(LANES, plane - j * LANES)
            rows = pl.ds(pl.multiple_of(k * plane + j * LANES, 64), count)
            real, imag = back_ref[tile, :channels, :], back_ref[tile, channels:, :]
            here = jnp.concatenate([real, imag], 0)
            turn = jnp.concatenate([imag, -real], 0)
            for c in range(0, channels, per_block):
                parts = [
                    in_ref[tile, c + h : c + h + 1, :] * here
                    + in_ref[tile, channels + c + h : channels + c + h + 1, :] * turn
                    for h in range(per_block)
                ]
                block = jnp.concatenate(parts, 0).T
                held_ref[rows, c * wide : c * wide + LANES] = block[:count]
            copy(k, j).start()

    @pl.loop(0, share)
    def _(k):
        for j in range(each):
            copy(k, j).wait()


def slope_kernel(
    cells, channels, factor, arrived_ref, table_ref, field_ref, cotangent_ref, point_ref, slope_ref, sent_ref
):
    spectral = dot(arrived_ref[...], table_ref[...], 0, 0)
    for c in range(cells):
        rows = slice(c * channels, (c + 1) * channels)
        before = spectral[rows] * factor + dot(point_ref[...], field_ref[rows, :], 0, 0)
        cumulative = 0.5 + 0.5 * lax.erf(before * math.sqrt(0.5))
        density = jnp.exp(-0.5 * before * before) * (1.0 / math.sqrt(2.0 * math.pi))
        slope = cotangent_ref[rows, :].astype(jnp.float32) * (cumulative + before * density)
        slope_ref[rows, :] = slope.astype(jnp.bfloat16)
    sent = dot(table_ref[...], slope_ref[...], 1, 1)
    sent_ref[...] = (sent * factor).astype(jnp.bfloat16)


def final_kernel(cells, channels, factor, arrived_ref, table_ref, slope_ref, point_ref, grad_ref):
    spectral = dot(arrived_ref[...], table_ref[...], 0, 0)
    for c in range(cells):
        rows = slice(c * channels, (c + 1) * channels)
        pointwise = dot(point_ref[...], slope_ref[rows, :])
        grad_ref[rows, :] = (pointwise + spectral[rows] * factor).astype(jnp.bfloat16)


def params(mebibytes, semantics=None):
    return pltpu.CompilerParams(dimension_semantics=semantics, vmem_limit_bytes=mebibytes * 1024 * 1024)


def on_chip(value):
    return pltpu.with_memory_space_constraint(value, pltpu.VMEM)


def off_chip(value):
    return pltpu.with_memory_space_constraint(value, pltpu.HBM)


IN_VMEM = pl.BlockSpec(memory_space=pltpu.VMEM)


def per_device(inputs, cotangent, point_weight, spectral_weight):
    rows_x, rows_y, channels, depth = inputs.shape
    mode_rows, mode_cols, flat = spectral_weight.shape
    count_gx, count_gy = lax.axis_size("gx"), lax.axis_size("gy")
    devices = count_gx * count_gy
    share = mode_rows // KX
    cells = rows_x * rows_y
    lanes = cells * channels
    wide = 2 * channels
    plane = KX * KY
    each = -(-plane // LANES)
    tiles = share * each
    points = cells * devices
    slots = devices * SLOTS
    inner = 1.0 / math.sqrt(points * depth)
    outer = 1.0 / math.sqrt(plane * KZ * KT)

    table = on_chip(jnp.asarray(depth_table(share)))
    forward, inverse = (on_chip(jnp.asarray(t)) for t in plane_tables(count_gx, count_gy, rows_x, rows_y))
    field = on_chip(inputs.reshape(lanes, depth))
    seed = on_chip(cotangent.reshape(lanes, depth))
    point = on_chip(point_weight)

    def exchange(sent):
        blocks = sent.reshape(devices, SLOTS, lanes)
        arrived = lax.all_to_all(blocks, GRID_AXES, split_axis=0, concat_axis=0, tiled=True)
        return on_chip(arrived.reshape(slots, lanes))

    packet = pltpu.VMEM((slots, lanes), jnp.bfloat16)
    spectra = pltpu.VMEM((tiles, wide, LANES), jnp.float32)

    sent = pl.pallas_call(
        functools.partial(depth_kernel, inner), in_specs=[IN_VMEM] * 2, out_specs=IN_VMEM, out_shape=packet,
        compiler_params=params(2),
        cost_estimate=pl.CostEstimate(flops=READ_AHEAD_FLOPS, transcendentals=0, bytes_accessed=0),
        name="depth",
    )(off_chip(jnp.asarray(depth_table(share))), off_chip(inputs.reshape(lanes, depth)))
    arrived = exchange(sent)
    scratch = [
        pltpu.VMEM((lanes // LANES, slots, LANES), jnp.float32),
        pltpu.VMEM((tiles, wide, 2 * LANES), jnp.bfloat16),
    ]
    sent, modes_in, turned = pl.pallas_call(
        functools.partial(mix_kernel, share, channels, plane),
        in_specs=[IN_VMEM] * 4, out_specs=[IN_VMEM] * 3,
        out_shape=[packet, spectra, pltpu.VMEM((tiles, flat, LANES), jnp.bfloat16)],
        scratch_shapes=scratch, compiler_params=params(6), name="mix",
    )(arrived, on_chip(spectral_weight.reshape(share * plane, flat)), forward, inverse)
    arrived = exchange(sent)
    slope, sent = pl.pallas_call(
        functools.partial(slope_kernel, cells, channels, outer),
        in_specs=[IN_VMEM] * 5, out_specs=[IN_VMEM] * 2, out_shape=[pltpu.VMEM((lanes, depth), jnp.bfloat16), packet],
        compiler_params=params(8), name="slope",
    )(arrived, table, field, seed, point)
    arrived = exchange(sent)
    sent, modes_back = pl.pallas_call(
        functools.partial(adjoint_kernel, share, channels),
        in_specs=[IN_VMEM] * 4, out_specs=[IN_VMEM] * 2, out_shape=[packet, spectra],
        scratch_shapes=scratch + [pltpu.VMEM((tiles, ROWS * wide, LANES), jnp.bfloat16)],
        compiler_params=params(12), name="adjoint",
    )(arrived, on_chip(turned), forward, inverse)
    arrived = exchange(sent)
    grad_spectral = pl.pallas_call(
        functools.partial(outer_kernel, share, channels, plane),
        in_specs=[IN_VMEM] * 2, out_specs=pl.BlockSpec(memory_space=pl.ANY),
        out_shape=jax.ShapeDtypeStruct((share * plane, flat), jnp.float32),
        scratch_shapes=[pltpu.VMEM((share * plane, flat), jnp.float32), pltpu.SemaphoreType.DMA((tiles,))],
        compiler_params=params(24),
        cost_estimate=pl.CostEstimate(
            flops=4 * share * plane * flat * wide, transcendentals=0, bytes_accessed=4 * share * plane * flat
        ),
        name="outer",
    )(on_chip(modes_in), on_chip(modes_back))
    grad_input = pl.pallas_call(
        functools.partial(final_kernel, cells, channels, inner),
        in_specs=[IN_VMEM] * 4, out_specs=IN_VMEM, out_shape=jax.ShapeDtypeStruct((lanes, depth), jnp.bfloat16),
        compiler_params=params(8), name="final",
    )(arrived, table, on_chip(slope), point)
    return grad_input.reshape(inputs.shape), grad_spectral.reshape(spectral_weight.shape)


def kept_angles(positions, kept_count, length):
    index = jnp.arange(kept_count, dtype=jnp.int32)
    frequency = jnp.where(index < kept_count // 2, index, index - kept_count)
    turns = positions[:, None] * frequency[None, :] % length
    return turns.astype(jnp.float32) * (2.0 * math.pi / length)


def axis_tables(positions, kept_count, length):
    angles = kept_angles(positions, kept_count, length)
    return (jnp.cos(angles), jnp.sin(angles))


def depth_tables():
    angle_depth = kept_angles(jnp.arange(NZ, dtype=jnp.int32), KZ, NZ)
    angle_time = kept_angles(jnp.arange(NT, dtype=jnp.int32), KT, NT)
    angles = (angle_depth[:, None, :, None] + angle_time[None, :, None, :]).reshape(
        NZ * NT, KZ * KT
    )
    return (jnp.cos(angles), jnp.sin(angles))


def settle(values):
    return lax.optimization_barrier(values.astype(jnp.bfloat16))


def rotate(spectra, cosine_table, sine_table, pattern, turn_sign):
    half_width = spectra.shape[-1] // 2
    with_cosine = jnp.einsum(pattern, spectra, cosine_table, precision=lax.Precision.HIGHEST)
    with_sine = jnp.einsum(pattern, spectra, sine_table, precision=lax.Precision.HIGHEST)
    real_part = with_cosine[..., :half_width] + turn_sign * with_sine[..., half_width:]
    imag_part = with_cosine[..., half_width:] - turn_sign * with_sine[..., :half_width]
    return jnp.concatenate([real_part, imag_part], -1)


def depth_forward(field_in, tables, factor):
    widened = field_in.astype(jnp.float32)
    with_cosine = jnp.einsum("xycs,sk->kxyc", widened, tables[0], precision=lax.Precision.HIGHEST)
    with_sine = jnp.einsum("xycs,sk->kxyc", widened, tables[1], precision=lax.Precision.HIGHEST)
    return jnp.concatenate([with_cosine, -with_sine], -1) * factor


def depth_inverse(spectra, tables, factor):
    half_width = spectra.shape[-1] // 2
    with_cosine = jnp.einsum(
        "kxyc,sk->xycs", spectra[..., :half_width], tables[0], precision=lax.Precision.HIGHEST
    )
    with_sine = jnp.einsum(
        "kxyc,sk->xycs", spectra[..., half_width:], tables[1], precision=lax.Precision.HIGHEST
    )
    return (with_cosine - with_sine) * factor


def contract_in(left, right):
    return jnp.einsum("mkc,mkco->mko", left, right, precision=lax.Precision.HIGHEST)


def contract_out(left, right):
    return jnp.einsum("mko,mkco->mkc", left, right, precision=lax.Precision.HIGHEST)


def partial_outer(left, right):
    return jnp.einsum("mkc,mko->mkco", left, right, precision=lax.Precision.HIGHEST)


def mix_modes(spectra, weight):
    half_width = spectra.shape[-1] // 2
    weight_wide = weight.astype(jnp.float32)
    weight_real, weight_imag = (weight_wide[..., :half_width], weight_wide[..., half_width:])
    real_in, imag_in = (spectra[..., :half_width], spectra[..., half_width:])
    real_out = contract_in(real_in, weight_real) - contract_in(imag_in, weight_imag)
    imag_out = contract_in(real_in, weight_imag) + contract_in(imag_in, weight_real)
    return jnp.concatenate([real_out, imag_out], -1)


def adjoint_modes(spectra, weight):
    half_width = spectra.shape[-1] // 2
    weight_wide = weight.astype(jnp.float32)
    weight_real, weight_imag = (weight_wide[..., :half_width], weight_wide[..., half_width:])
    real_in, imag_in = (spectra[..., :half_width], spectra[..., half_width:])
    real_out = contract_out(real_in, weight_real) + contract_out(imag_in, weight_imag)
    imag_out = contract_out(imag_in, weight_real) - contract_out(real_in, weight_imag)
    return jnp.concatenate([real_out, imag_out], -1)


def weight_grad(spectra_in, spectra_back):
    half_width = spectra_in.shape[-1] // 2
    real_in, imag_in = (spectra_in[..., :half_width], spectra_in[..., half_width:])
    real_back, imag_back = (spectra_back[..., :half_width], spectra_back[..., half_width:])
    real_part = partial_outer(real_in, real_back) + partial_outer(imag_in, imag_back)
    imag_part = partial_outer(real_in, imag_back) - partial_outer(imag_in, real_back)
    return jnp.concatenate([real_part, imag_part], -1)


def exact_gelu(values):
    return jax.nn.gelu(values, approximate=False)


def general_per_device(inputs, cotangent, point_weight, spectral_weight):
    rows_x, rows_y, channels, cells = inputs.shape
    mode_rows, mode_cols, flat_width = spectral_weight.shape
    weight_blocks = spectral_weight.reshape(mode_rows, mode_cols, channels, 2 * channels)
    count_gx = lax.axis_size("gx")
    count_gy = lax.axis_size("gy")
    length_x = rows_x * count_gx
    length_y = rows_y * count_gy
    depth_pair = depth_tables()
    own_x = lax.axis_index("gx") * rows_x + jnp.arange(rows_x, dtype=jnp.int32)
    local_x = axis_tables(own_x, KX, length_x)
    whole_y = axis_tables(jnp.arange(length_y, dtype=jnp.int32), KY, length_y)
    total_cells = length_x * length_y * cells
    kept_total = KX * KY * KZ * KT

    def to_modes(field_in, factor):
        depth_spec = settle(depth_forward(field_in, depth_pair, factor))
        share = depth_spec.shape[0] // count_gx
        first_spectra = lax.psum_scatter(
            rotate(
                depth_spec.astype(jnp.float32), local_x[0], local_x[1], "rxyc,xk->rkyc", 1.0
            ).astype(jnp.bfloat16),
            "gx",
            scatter_dimension=0,
            tiled=True,
        ).astype(jnp.float32)
        first_spectra = settle(first_spectra).reshape(share * KX, rows_y, 2 * channels)
        arrived_modes = lax.all_to_all(first_spectra, "gy", split_axis=0, concat_axis=1, tiled=True)
        return rotate(arrived_modes.astype(jnp.float32), whole_y[0], whole_y[1], "myc,yk->mkc", 1.0)

    def to_space(spectra, factor):
        back_rows = settle(rotate(spectra, whole_y[0], whole_y[1], "mkc,yk->myc", -1.0))
        returned = lax.all_to_all(back_rows, "gy", split_axis=1, concat_axis=0, tiled=True)
        share = returned.shape[0] // KX
        returned = returned.reshape(share, KX, rows_y, 2 * channels)
        back_depth = settle(
            rotate(
                lax.all_gather(returned, "gx", axis=0, tiled=True).astype(jnp.float32),
                local_x[0],
                local_x[1],
                "rkyc,xk->rxyc",
                -1.0,
            )
        )
        return depth_inverse(back_depth.astype(jnp.float32), depth_pair, factor)

    spectra_in = to_modes(inputs, 1.0 / math.sqrt(total_cells))
    mixed = mix_modes(spectra_in, weight_blocks)
    spectral_out = to_space(mixed, 1.0 / math.sqrt(kept_total))
    pointwise = jnp.einsum(
        "xycs,co->xyos", inputs, point_weight, preferred_element_type=jnp.float32
    )
    before = spectral_out + pointwise
    unused_out, pullback = jax.vjp(exact_gelu, before)
    slope = settle(pullback(cotangent.astype(jnp.float32))[0])
    spectra_back = to_modes(slope, 1.0 / math.sqrt(kept_total))
    grad_spectral = weight_grad(spectra_in, spectra_back).reshape(mode_rows, mode_cols, flat_width)
    adjoint = adjoint_modes(spectra_back, weight_blocks)
    spectral_grad = to_space(adjoint, 1.0 / math.sqrt(total_cells))
    pointwise_grad = jnp.einsum(
        "xyos,co->xycs", slope, point_weight, preferred_element_type=jnp.float32
    )
    grad_input = (pointwise_grad + spectral_grad).astype(jnp.bfloat16)
    return (grad_input, grad_spectral)


def solution(mesh):
    count_gx, count_gy = mesh.shape["gx"], mesh.shape["gy"]
    placed = (
        P("gx", "gy", None, None),
        P("gx", "gy", None, None),
        P(),
        P(("gx", "gy"), None, None),
    )

    def program(inputs, cotangent, point_weight, spectral_weight):
        cells = inputs.shape[0] * inputs.shape[1] // (count_gx * count_gy)
        whole_modes = KZ * KT % (count_gx * count_gy) == 0
        fits = whole_modes and 2 * KZ * KT // (count_gx * count_gy) <= SLOTS
        fits = fits and inputs.shape[2] == 32 and cells * inputs.shape[2] == 256
        return jax.shard_map(
            per_device if fits else general_per_device,
            mesh=mesh,
            in_specs=placed,
            out_specs=(P("gx", "gy", None, None), P(("gx", "gy"), None, None)),
            check_vma=False,
        )(inputs, cotangent, point_weight, spectral_weight)

    return program
```

```python
import functools
import math

import jax
import jax.numpy as jnp
import numpy as np
from jax import lax
from jax.experimental import pallas as pl
from jax.experimental.pallas import tpu as pltpu
from jax.sharding import PartitionSpec as P

NZ = 64
NT = 8
KX = 24
KY = 24
KZ = 12
KT = 8
SLOTS = 8
LANES = 128
LENGTH = 16
GROUP = 4
ROWS = 16
READ_AHEAD_FLOPS = 10**11
GRID_AXES = ("gx", "gy")


def table_angles(positions, kept_count, length):
    index = np.arange(kept_count)
    frequency = np.where(index < kept_count // 2, index, index - kept_count)
    turns = (np.asarray(positions)[:, None] * frequency[None, :]) % length
    return 2.0 * np.pi * turns / length


def depth_table(share):
    angles = (
        table_angles(np.arange(NZ), KZ, NZ)[:, None, :, None]
        + table_angles(np.arange(NT), KT, NT)[None, :, None, :]
    ).reshape(NZ * NT, KZ * KT)
    parts = np.stack([np.cos(angles), -np.sin(angles)], -1)
    owners = KZ * KT // share
    rows = np.zeros((owners, SLOTS, NZ * NT))
    rows[:, : 2 * share] = parts.reshape(NZ * NT, owners, 2 * share).transpose(1, 2, 0)
    return rows.reshape(owners * SLOTS, NZ * NT).astype(jnp.bfloat16)


def plane_tables(count_gx, count_gy, rows_x, rows_y):
    length_x, length_y = count_gx * rows_x, count_gy * rows_y
    turns_x = np.outer(np.arange(length_x), np.arange(length_x)) % length_x / length_x
    turns_y = np.outer(np.arange(length_y), np.arange(length_y)) % length_y / length_y
    turns_x = turns_x.reshape(length_x, 1, count_gx, 1, rows_x, 1)
    turns_y = turns_y.reshape(1, length_y, 1, count_gy, 1, rows_y)
    turns = (turns_x + turns_y).transpose(0, 1, 4, 5, 2, 3).reshape(length_x * length_y, length_x * length_y)
    cosine, sine = np.cos(2.0 * np.pi * turns), np.sin(2.0 * np.pi * turns)
    forward = np.concatenate([cosine.T, sine.T], 0)
    inverse = np.concatenate([cosine.T, sine.T], 1)
    return forward.astype(jnp.bfloat16), inverse.astype(jnp.bfloat16)


def residue_of(mode):
    return (mode if mode < KX // 2 else mode - KX) % LENGTH


def modes_of(residue):
    return [mode for mode in range(KX) if residue_of(mode) == residue]


def dot(left, right, left_dim=1, right_dim=0):
    return lax.dot_general(
        left, right, (((left_dim,), (right_dim,)), ((), ())), preferred_element_type=jnp.float32
    )


def depth_kernel(factor, table_ref, field_ref, sent_ref):
    spectra = dot(table_ref[...], field_ref[...], 1, 1)
    sent_ref[...] = (spectra * factor).astype(jnp.bfloat16)


def to_plane_modes(share, channels, arrived_ref, forward_ref, wide_ref, modes_ref):
    halves, rows, lanes = wide_ref.shape
    devices = rows // SLOTS
    for h in range(halves):
        wide_ref[h] = arrived_ref[:, h * LANES : (h + 1) * LANES].astype(jnp.float32)
    columns = []
    for slot in range(2 * share):
        pieces = []
        for h in range(halves):
            piece = wide_ref[h, pl.ds(slot, devices, stride=SLOTS), :]
            pieces += [piece[:, c * channels : (c + 1) * channels] for c in range(lanes // channels)]
        columns.append(jnp.concatenate(pieces, 0))
    cells = jnp.concatenate(columns, 1).T
    blocks = []
    for k in range(share):
        real = cells[2 * k * channels : (2 * k + 1) * channels]
        imag = cells[(2 * k + 1) * channels : (2 * k + 2) * channels]
        blocks += [jnp.concatenate([real, imag], 1), jnp.concatenate([imag, -real], 1)]
    modes = dot(jnp.concatenate(blocks, 0).astype(jnp.bfloat16), forward_ref[...])
    each = modes_ref.shape[0] // share
    for k in range(share):
        for j in range(each):
            modes_ref[k * each + j] = modes[2 * k * channels : (2 * k + 2) * channels, j * LANES : (j + 1) * LANES]


def store_pair(tile, share, channels, real, imag, pair_ref):
    pair_ref[tile, :channels, :LANES] = real.astype(jnp.bfloat16)
    pair_ref[tile, channels:, :LANES] = imag.astype(jnp.bfloat16)
    pair_ref[tile, :channels, LANES:] = (-imag).astype(jnp.bfloat16)
    pair_ref[tile, channels:, LANES:] = real.astype(jnp.bfloat16)


def to_cells(share, channels, pair_ref, inverse_ref, out_ref, sent_ref):
    halves, rows, lanes = out_ref.shape
    devices = rows // SLOTS
    each = pair_ref.shape[0] // share
    padded = each * LANES
    out_ref[...] = jnp.zeros_like(out_ref)
    spectra = []
    for k in range(share):
        cosine = jnp.concatenate([pair_ref[k * each + j, :, :LANES] for j in range(each)], 1)
        sine = jnp.concatenate([pair_ref[k * each + j, :, LANES:] for j in range(each)], 1)
        spectra.append(jnp.concatenate([cosine, sine], 1))
    total = dot(inverse_ref[...], jnp.concatenate(spectra, 0), 1, 1)
    per_half = lanes // channels
    for slot in range(2 * share):
        columns = slice(slot * channels, (slot + 1) * channels)
        for h in range(halves):
            pieces = [total[c * devices : (c + 1) * devices, columns] for c in range(h * per_half, (h + 1) * per_half)]
            out_ref[h, pl.ds(slot, devices, stride=SLOTS), :] = jnp.concatenate(pieces, 1)
    for h in range(halves):
        sent_ref[:, h * LANES : (h + 1) * LANES] = out_ref[h].astype(jnp.bfloat16)


def fold_rows(weight_ref, mode, first, count, columns):
    row = lax.broadcasted_iota(jnp.int32, (8, LANES), 0)
    low = jnp.where(row < 4, 1.0, 0.0)
    high = 1.0 - low
    folded = []
    for residue in range(first, first + count):
        total = None
        for kx in modes_of(residue):
            rows = pl.ds(pl.multiple_of((mode * KX + kx) * KY, 8), KY)
            block = weight_ref[rows, columns].astype(jnp.float32)
            total = block if total is None else total + block
        folded += [total[:8] + high * total[8:16], total[16:] + low * total[8:16]]
    return jnp.concatenate(folded, 0).astype(jnp.bfloat16)


def mix_kernel(
    share, channels, arrived_ref, weight_ref, forward_ref, inverse_ref, sent_ref, modes_ref, turned_ref,
    wide_ref, pair_ref,
):
    to_plane_modes(share, channels, arrived_ref, forward_ref, wide_ref, modes_ref)
    wide = 2 * channels
    each = modes_ref.shape[0] // share
    per_tile = LANES // LENGTH

    @pl.loop(0, share)
    def _(k):
        for j in range(each):
            tile = k * each + j
            by_real = jnp.zeros((wide, LANES), jnp.float32)
            by_imag = jnp.zeros((wide, LANES), jnp.float32)
            for first in range(0, channels, GROUP):
                real_sum, imag_sum = None, None
                for c in range(first, first + GROUP, LANES // wide):
                    columns = slice(c * wide, c * wide + LANES)
                    block = fold_rows(weight_ref, k, j * per_tile, per_tile, columns).T
                    turned_ref[tile, columns, :] = block
                    for h in range(LANES // wide):
                        weight = block[h * wide : (h + 1) * wide]
                        real = jnp.broadcast_to(modes_ref[tile, c + h : c + h + 1, :], (wide, LANES))
                        imag = jnp.broadcast_to(
                            modes_ref[tile, channels + c + h : channels + c + h + 1, :], (wide, LANES)
                        )
                        real, imag = real.astype(jnp.bfloat16) * weight, imag.astype(jnp.bfloat16) * weight
                        real_sum = real if real_sum is None else real_sum + real
                        imag_sum = imag if imag_sum is None else imag_sum + imag
                by_real += real_sum.astype(jnp.float32)
                by_imag += imag_sum.astype(jnp.float32)
            store_pair(
                tile, share, channels, by_real[:channels] - by_imag[channels:],
                by_real[channels:] + by_imag[:channels], pair_ref,
            )

    to_cells(share, channels, pair_ref, inverse_ref, wide_ref, sent_ref)


def adjoint_kernel(
    share, channels, arrived_ref, turned_ref, forward_ref, inverse_ref, sent_ref, modes_ref, wide_ref, pair_ref,
    part_ref,
):
    to_plane_modes(share, channels, arrived_ref, forward_ref, wide_ref, modes_ref)
    wide = 2 * channels
    tiles = modes_ref.shape[0]

    @pl.loop(0, tiles)
    def _(tile):
        real, imag = modes_ref[tile, :channels, :], modes_ref[tile, channels:, :]
        here = jnp.concatenate([real, imag], 0).astype(jnp.bfloat16)
        turn = jnp.concatenate([imag, -real], 0).astype(jnp.bfloat16)
        for c in range(channels):
            weight = turned_ref[tile, c * wide : (c + 1) * wide, :]
            for part, factor in enumerate((here, turn)):
                product = factor * weight
                while product.shape[0] > ROWS:
                    half = product.shape[0] // 2
                    product = product[:half] + product[half:]
                part_ref[tile, (part * channels + c) * ROWS : (part * channels + c + 1) * ROWS, :] = product

    row = lax.broadcasted_iota(jnp.int32, (wide, ROWS * wide), 0)
    column = lax.broadcasted_iota(jnp.int32, (wide, ROWS * wide), 1)
    groups = jnp.where(column // ROWS == row, 1.0, 0.0).astype(jnp.bfloat16)
    for tile in range(tiles):
        summed = dot(groups, part_ref[tile])
        store_pair(tile, share, channels, summed[:channels], summed[channels:], pair_ref)

    to_cells(share, channels, pair_ref, inverse_ref, wide_ref, sent_ref)


def outer_kernel(share, channels, in_ref, back_ref, grad_ref, held_ref, sems):
    wide = 2 * channels
    each = in_ref.shape[0] // share
    per_block = LANES // wide
    per_tile = LANES // LENGTH

    def runs(j):
        inside = [kx for kx in range(KX) if residue_of(kx) // per_tile == j]
        found = []
        for kx in inside:
            if found and found[-1][0] + found[-1][2] == kx and found[-1][1] + found[-1][2] == residue_of(kx):
                found[-1][2] += 1
            else:
                found.append([kx, residue_of(kx), 1])
        return found

    def copies(k, j):
        made = []
        for place, (mode, residue, count) in enumerate(runs(j)):
            source = pl.ds(pl.multiple_of((k * LENGTH + residue) * KY, 8), count * KY)
            target = pl.ds(pl.multiple_of((k * KX + mode) * KY, 8), count * KY)
            made.append(
                pltpu.make_async_copy(held_ref.at[source], grad_ref.at[target], sems.at[k * each + j, place])
            )
        return made

    low = lax.broadcasted_iota(jnp.int32, (8, LANES), 0) < 4

    @pl.loop(0, share)
    def _(k):
        for j in range(each):
            tile = k * each + j
            real, imag = back_ref[tile, :channels, :], back_ref[tile, channels:, :]
            here = jnp.concatenate([real, imag], 0)
            turn = jnp.concatenate([imag, -real], 0)
            for c in range(0, channels, per_block):
                parts = [
                    in_ref[tile, c + h : c + h + 1, :] * here
                    + in_ref[tile, channels + c + h : channels + c + h + 1, :] * turn
                    for h in range(per_block)
                ]
                block = jnp.concatenate(parts, 0).T
                for i in range(per_tile):
                    first = block[i * LENGTH : i * LENGTH + 8]
                    second = block[i * LENGTH + 8 : (i + 1) * LENGTH]
                    rows = pl.ds(pl.multiple_of((k * LENGTH + j * per_tile + i) * KY, 8), KY)
                    held_ref[rows, c * wide : c * wide + LANES] = jnp.concatenate(
                        [first, jnp.where(low, second, first), second], 0
                    )
            for copy in copies(k, j):
                copy.start()

    @pl.loop(0, share)
    def _(k):
        for j in range(each):
            for copy in copies(k, j):
                copy.wait()


def slope_kernel(
    cells, channels, factor, arrived_ref, table_ref, field_ref, cotangent_ref, point_ref, slope_ref, sent_ref
):
    spectral = dot(arrived_ref[...], table_ref[...], 0, 0)
    for c in range(cells):
        rows = slice(c * channels, (c + 1) * channels)
        before = spectral[rows] * factor + dot(point_ref[...], field_ref[rows, :], 0, 0)
        cumulative = 0.5 + 0.5 * lax.erf(before * math.sqrt(0.5))
        density = jnp.exp(-0.5 * before * before) * (1.0 / math.sqrt(2.0 * math.pi))
        slope = cotangent_ref[rows, :].astype(jnp.float32) * (cumulative + before * density)
        slope_ref[rows, :] = slope.astype(jnp.bfloat16)
    sent = dot(table_ref[...], slope_ref[...], 1, 1)
    sent_ref[...] = (sent * factor).astype(jnp.bfloat16)


def final_kernel(cells, channels, factor, arrived_ref, table_ref, slope_ref, point_ref, grad_ref):
    spectral = dot(arrived_ref[...], table_ref[...], 0, 0)
    for c in range(cells):
        rows = slice(c * channels, (c + 1) * channels)
        pointwise = dot(point_ref[...], slope_ref[rows, :])
        grad_ref[rows, :] = (pointwise + spectral[rows] * factor).astype(jnp.bfloat16)


def params(mebibytes, semantics=None):
    return pltpu.CompilerParams(dimension_semantics=semantics, vmem_limit_bytes=mebibytes * 1024 * 1024)


def on_chip(value):
    return pltpu.with_memory_space_constraint(value, pltpu.VMEM)


def off_chip(value):
    return pltpu.with_memory_space_constraint(value, pltpu.HBM)


IN_VMEM = pl.BlockSpec(memory_space=pltpu.VMEM)


def per_device(inputs, cotangent, point_weight, spectral_weight):
    rows_x, rows_y, channels, depth = inputs.shape
    mode_rows, mode_cols, flat = spectral_weight.shape
    count_gx, count_gy = lax.axis_size("gx"), lax.axis_size("gy")
    devices = count_gx * count_gy
    share = mode_rows // KX
    cells = rows_x * rows_y
    lanes = cells * channels
    wide = 2 * channels
    plane = KX * KY
    points = cells * devices
    each = points // LANES
    tiles = share * each
    slots = devices * SLOTS
    inner = 1.0 / math.sqrt(points * depth)
    outer = 1.0 / math.sqrt(plane * KZ * KT)

    table = on_chip(jnp.asarray(depth_table(share)))
    forward, inverse = (on_chip(jnp.asarray(t)) for t in plane_tables(count_gx, count_gy, rows_x, rows_y))
    field = on_chip(inputs.reshape(lanes, depth))
    seed = on_chip(cotangent.reshape(lanes, depth))
    point = on_chip(point_weight)

    def exchange(sent):
        blocks = sent.reshape(devices, SLOTS, lanes)
        arrived = lax.all_to_all(blocks, GRID_AXES, split_axis=0, concat_axis=0, tiled=True)
        return on_chip(arrived.reshape(slots, lanes))

    packet = pltpu.VMEM((slots, lanes), jnp.bfloat16)
    spectra = pltpu.VMEM((tiles, wide, LANES), jnp.float32)

    sent = pl.pallas_call(
        functools.partial(depth_kernel, inner), in_specs=[IN_VMEM] * 2, out_specs=IN_VMEM, out_shape=packet,
        compiler_params=params(2),
        cost_estimate=pl.CostEstimate(flops=READ_AHEAD_FLOPS, transcendentals=0, bytes_accessed=0),
        name="depth",
    )(off_chip(jnp.asarray(depth_table(share))), off_chip(inputs.reshape(lanes, depth)))
    arrived = exchange(sent)
    scratch = [
        pltpu.VMEM((lanes // LANES, slots, LANES), jnp.float32),
        pltpu.VMEM((tiles, wide, 2 * LANES), jnp.bfloat16),
    ]
    sent, modes_in, turned = pl.pallas_call(
        functools.partial(mix_kernel, share, channels),
        in_specs=[IN_VMEM] * 4, out_specs=[IN_VMEM] * 3,
        out_shape=[packet, spectra, pltpu.VMEM((tiles, flat, LANES), jnp.bfloat16)],
        scratch_shapes=scratch, compiler_params=params(6), name="mix",
    )(arrived, on_chip(spectral_weight.reshape(share * plane, flat)), forward, inverse)
    arrived = exchange(sent)
    slope, sent = pl.pallas_call(
        functools.partial(slope_kernel, cells, channels, outer),
        in_specs=[IN_VMEM] * 5, out_specs=[IN_VMEM] * 2, out_shape=[pltpu.VMEM((lanes, depth), jnp.bfloat16), packet],
        compiler_params=params(8), name="slope",
    )(arrived, table, field, seed, point)
    arrived = exchange(sent)
    sent, modes_back = pl.pallas_call(
        functools.partial(adjoint_kernel, share, channels),
        in_specs=[IN_VMEM] * 4, out_specs=[IN_VMEM] * 2, out_shape=[packet, spectra],
        scratch_shapes=scratch + [pltpu.VMEM((tiles, ROWS * wide, LANES), jnp.bfloat16)],
        compiler_params=params(12), name="adjoint",
    )(arrived, on_chip(turned), forward, inverse)
    arrived = exchange(sent)
    grad_spectral = pl.pallas_call(
        functools.partial(outer_kernel, share, channels),
        in_specs=[IN_VMEM] * 2, out_specs=pl.BlockSpec(memory_space=pl.ANY),
        out_shape=jax.ShapeDtypeStruct((share * plane, flat), jnp.float32),
        scratch_shapes=[
            pltpu.VMEM((share * LENGTH * KY, flat), jnp.float32), pltpu.SemaphoreType.DMA((tiles, 2)),
        ],
        compiler_params=params(24),
        cost_estimate=pl.CostEstimate(
            flops=4 * share * plane * flat * wide, transcendentals=0, bytes_accessed=4 * share * plane * flat
        ),
        name="outer",
    )(on_chip(modes_in), on_chip(modes_back))
    grad_input = pl.pallas_call(
        functools.partial(final_kernel, cells, channels, inner),
        in_specs=[IN_VMEM] * 4, out_specs=IN_VMEM, out_shape=jax.ShapeDtypeStruct((lanes, depth), jnp.bfloat16),
        compiler_params=params(8), name="final",
    )(arrived, table, on_chip(slope), point)
    return grad_input.reshape(inputs.shape), grad_spectral.reshape(spectral_weight.shape)


def kept_angles(positions, kept_count, length):
    index = jnp.arange(kept_count, dtype=jnp.int32)
    frequency = jnp.where(index < kept_count // 2, index, index - kept_count)
    turns = positions[:, None] * frequency[None, :] % length
    return turns.astype(jnp.float32) * (2.0 * math.pi / length)


def axis_tables(positions, kept_count, length):
    angles = kept_angles(positions, kept_count, length)
    return (jnp.cos(angles), jnp.sin(angles))


def depth_tables():
    angle_depth = kept_angles(jnp.arange(NZ, dtype=jnp.int32), KZ, NZ)
    angle_time = kept_angles(jnp.arange(NT, dtype=jnp.int32), KT, NT)
    angles = (angle_depth[:, None, :, None] + angle_time[None, :, None, :]).reshape(
        NZ * NT, KZ * KT
    )
    return (jnp.cos(angles), jnp.sin(angles))


def settle(values):
    return lax.optimization_barrier(values.astype(jnp.bfloat16))


def rotate(spectra, cosine_table, sine_table, pattern, turn_sign):
    half_width = spectra.shape[-1] // 2
    with_cosine = jnp.einsum(pattern, spectra, cosine_table, precision=lax.Precision.HIGHEST)
    with_sine = jnp.einsum(pattern, spectra, sine_table, precision=lax.Precision.HIGHEST)
    real_part = with_cosine[..., :half_width] + turn_sign * with_sine[..., half_width:]
    imag_part = with_cosine[..., half_width:] - turn_sign * with_sine[..., :half_width]
    return jnp.concatenate([real_part, imag_part], -1)


def depth_forward(field_in, tables, factor):
    widened = field_in.astype(jnp.float32)
    with_cosine = jnp.einsum("xycs,sk->kxyc", widened, tables[0], precision=lax.Precision.HIGHEST)
    with_sine = jnp.einsum("xycs,sk->kxyc", widened, tables[1], precision=lax.Precision.HIGHEST)
    return jnp.concatenate([with_cosine, -with_sine], -1) * factor


def depth_inverse(spectra, tables, factor):
    half_width = spectra.shape[-1] // 2
    with_cosine = jnp.einsum(
        "kxyc,sk->xycs", spectra[..., :half_width], tables[0], precision=lax.Precision.HIGHEST
    )
    with_sine = jnp.einsum(
        "kxyc,sk->xycs", spectra[..., half_width:], tables[1], precision=lax.Precision.HIGHEST
    )
    return (with_cosine - with_sine) * factor


def contract_in(left, right):
    return jnp.einsum("mkc,mkco->mko", left, right, precision=lax.Precision.HIGHEST)


def contract_out(left, right):
    return jnp.einsum("mko,mkco->mkc", left, right, precision=lax.Precision.HIGHEST)


def partial_outer(left, right):
    return jnp.einsum("mkc,mko->mkco", left, right, precision=lax.Precision.HIGHEST)


def mix_modes(spectra, weight):
    half_width = spectra.shape[-1] // 2
    weight_wide = weight.astype(jnp.float32)
    weight_real, weight_imag = (weight_wide[..., :half_width], weight_wide[..., half_width:])
    real_in, imag_in = (spectra[..., :half_width], spectra[..., half_width:])
    real_out = contract_in(real_in, weight_real) - contract_in(imag_in, weight_imag)
    imag_out = contract_in(real_in, weight_imag) + contract_in(imag_in, weight_real)
    return jnp.concatenate([real_out, imag_out], -1)


def adjoint_modes(spectra, weight):
    half_width = spectra.shape[-1] // 2
    weight_wide = weight.astype(jnp.float32)
    weight_real, weight_imag = (weight_wide[..., :half_width], weight_wide[..., half_width:])
    real_in, imag_in = (spectra[..., :half_width], spectra[..., half_width:])
    real_out = contract_out(real_in, weight_real) + contract_out(imag_in, weight_imag)
    imag_out = contract_out(imag_in, weight_real) - contract_out(real_in, weight_imag)
    return jnp.concatenate([real_out, imag_out], -1)


def weight_grad(spectra_in, spectra_back):
    half_width = spectra_in.shape[-1] // 2
    real_in, imag_in = (spectra_in[..., :half_width], spectra_in[..., half_width:])
    real_back, imag_back = (spectra_back[..., :half_width], spectra_back[..., half_width:])
    real_part = partial_outer(real_in, real_back) + partial_outer(imag_in, imag_back)
    imag_part = partial_outer(real_in, imag_back) - partial_outer(imag_in, real_back)
    return jnp.concatenate([real_part, imag_part], -1)


def exact_gelu(values):
    return jax.nn.gelu(values, approximate=False)


def general_per_device(inputs, cotangent, point_weight, spectral_weight):
    rows_x, rows_y, channels, cells = inputs.shape
    mode_rows, mode_cols, flat_width = spectral_weight.shape
    weight_blocks = spectral_weight.reshape(mode_rows, mode_cols, channels, 2 * channels)
    count_gx = lax.axis_size("gx")
    count_gy = lax.axis_size("gy")
    length_x = rows_x * count_gx
    length_y = rows_y * count_gy
    depth_pair = depth_tables()
    own_x = lax.axis_index("gx") * rows_x + jnp.arange(rows_x, dtype=jnp.int32)
    local_x = axis_tables(own_x, KX, length_x)
    whole_y = axis_tables(jnp.arange(length_y, dtype=jnp.int32), KY, length_y)
    total_cells = length_x * length_y * cells
    kept_total = KX * KY * KZ * KT

    def to_modes(field_in, factor):
        depth_spec = settle(depth_forward(field_in, depth_pair, factor))
        share = depth_spec.shape[0] // count_gx
        first_spectra = lax.psum_scatter(
            rotate(
                depth_spec.astype(jnp.float32), local_x[0], local_x[1], "rxyc,xk->rkyc", 1.0
            ).astype(jnp.bfloat16),
            "gx",
            scatter_dimension=0,
            tiled=True,
        ).astype(jnp.float32)
        first_spectra = settle(first_spectra).reshape(share * KX, rows_y, 2 * channels)
        arrived_modes = lax.all_to_all(first_spectra, "gy", split_axis=0, concat_axis=1, tiled=True)
        return rotate(arrived_modes.astype(jnp.float32), whole_y[0], whole_y[1], "myc,yk->mkc", 1.0)

    def to_space(spectra, factor):
        back_rows = settle(rotate(spectra, whole_y[0], whole_y[1], "mkc,yk->myc", -1.0))
        returned = lax.all_to_all(back_rows, "gy", split_axis=1, concat_axis=0, tiled=True)
        share = returned.shape[0] // KX
        returned = returned.reshape(share, KX, rows_y, 2 * channels)
        back_depth = settle(
            rotate(
                lax.all_gather(returned, "gx", axis=0, tiled=True).astype(jnp.float32),
                local_x[0],
                local_x[1],
                "rkyc,xk->rxyc",
                -1.0,
            )
        )
        return depth_inverse(back_depth.astype(jnp.float32), depth_pair, factor)

    spectra_in = to_modes(inputs, 1.0 / math.sqrt(total_cells))
    mixed = mix_modes(spectra_in, weight_blocks)
    spectral_out = to_space(mixed, 1.0 / math.sqrt(kept_total))
    pointwise = jnp.einsum(
        "xycs,co->xyos", inputs, point_weight, preferred_element_type=jnp.float32
    )
    before = spectral_out + pointwise
    unused_out, pullback = jax.vjp(exact_gelu, before)
    slope = settle(pullback(cotangent.astype(jnp.float32))[0])
    spectra_back = to_modes(slope, 1.0 / math.sqrt(kept_total))
    grad_spectral = weight_grad(spectra_in, spectra_back).reshape(mode_rows, mode_cols, flat_width)
    adjoint = adjoint_modes(spectra_back, weight_blocks)
    spectral_grad = to_space(adjoint, 1.0 / math.sqrt(total_cells))
    pointwise_grad = jnp.einsum(
        "xyos,co->xycs", slope, point_weight, preferred_element_type=jnp.float32
    )
    grad_input = (pointwise_grad + spectral_grad).astype(jnp.bfloat16)
    return (grad_input, grad_spectral)


def solution(mesh):
    count_gx, count_gy = mesh.shape["gx"], mesh.shape["gy"]
    placed = (
        P("gx", "gy", None, None),
        P("gx", "gy", None, None),
        P(),
        P(("gx", "gy"), None, None),
    )

    def program(inputs, cotangent, point_weight, spectral_weight):
        cells = inputs.shape[0] * inputs.shape[1] // (count_gx * count_gy)
        whole_modes = KZ * KT % (count_gx * count_gy) == 0
        fits = whole_modes and 2 * KZ * KT // (count_gx * count_gy) <= SLOTS
        fits = fits and inputs.shape[2] == 32 and cells * inputs.shape[2] == 256 and inputs.shape[0] == inputs.shape[1] == LENGTH
        return jax.shard_map(
            per_device if fits else general_per_device,
            mesh=mesh,
            in_specs=placed,
            out_specs=(P("gx", "gy", None, None), P(("gx", "gy"), None, None)),
            check_vma=False,
        )(inputs, cotangent, point_weight, spectral_weight)

    return program
```

```python
import functools
import math

import jax
import jax.numpy as jnp
import numpy as np
from jax import lax
from jax.experimental import pallas as pl
from jax.experimental.pallas import tpu as pltpu
from jax.sharding import PartitionSpec as P

NZ = 64
NT = 8
KX = 24
KY = 24
KZ = 12
KT = 8
LANES = 128
LENGTH = 16
GROUP = 4
READ_AHEAD_FLOPS = 10**11
GRID_AXES = ("gx", "gy")


def table_angles(positions, kept_count, length):
    index = np.arange(kept_count)
    frequency = np.where(index < kept_count // 2, index, index - kept_count)
    turns = (np.asarray(positions)[:, None] * frequency[None, :]) % length
    return 2.0 * np.pi * turns / length


def depth_table(share):
    angles = (
        table_angles(np.arange(NZ), KZ, NZ)[:, None, :, None]
        + table_angles(np.arange(NT), KT, NT)[None, :, None, :]
    ).reshape(NZ * NT, KZ * KT)
    parts = np.stack([np.cos(angles), -np.sin(angles)], -1)
    owners = KZ * KT // share
    rows = parts.reshape(NZ * NT, owners, 2 * share).transpose(2, 1, 0)
    return rows.reshape(2 * share * owners, NZ * NT).astype(jnp.bfloat16)


def plane_tables(count_gx, count_gy, rows_x, rows_y):
    length_x, length_y = count_gx * rows_x, count_gy * rows_y
    turns_x = np.outer(np.arange(length_x), np.arange(length_x)) % length_x / length_x
    turns_y = np.outer(np.arange(length_y), np.arange(length_y)) % length_y / length_y
    turns_x = turns_x.reshape(length_x, 1, count_gx, 1, rows_x, 1)
    turns_y = turns_y.reshape(1, length_y, 1, count_gy, 1, rows_y)
    turns = (turns_x + turns_y).transpose(0, 1, 4, 5, 2, 3).reshape(length_x * length_y, length_x * length_y)
    cosine, sine = np.cos(2.0 * np.pi * turns), np.sin(2.0 * np.pi * turns)
    forward = np.concatenate([cosine.T, sine.T], 0)
    inverse = np.concatenate([cosine.T, sine.T], 1)
    return forward.astype(jnp.bfloat16), inverse.astype(jnp.bfloat16)


def residue_of(mode):
    return (mode if mode < KX // 2 else mode - KX) % LENGTH


def modes_of(residue):
    return [mode for mode in range(KX) if residue_of(mode) == residue]


def dot(left, right, left_dim=1, right_dim=0):
    return lax.dot_general(
        left, right, (((left_dim,), (right_dim,)), ((), ())), preferred_element_type=jnp.float32
    )


def unit_rows(unit, wide_ref, units):
    return pl.ds(unit, wide_ref.shape[0] // units, stride=units)


def send_slots(spectra, units, wide_ref, sent_ref):
    devices = wide_ref.shape[0] // units
    halves = spectra.shape[1] // LANES
    for unit in range(units):
        slot, h = divmod(unit, halves)
        wide_ref[unit_rows(unit, wide_ref, units), :] = spectra[
            slot * devices : (slot + 1) * devices, h * LANES : (h + 1) * LANES
        ]
    sent_ref[...] = wide_ref[...].astype(jnp.bfloat16)


def received_slots(arrived_ref, halves, units, wide_ref):
    wide_ref[...] = arrived_ref[...].astype(jnp.float32)
    slots = []
    for slot in range(units // halves):
        pieces = [wide_ref[unit_rows(slot * halves + h, wide_ref, units), :] for h in range(halves)]
        slots.append(jnp.concatenate(pieces, 1))
    return jnp.concatenate(slots, 0)


def depth_kernel(factor, units, table_ref, field_ref, sent_ref, wide_ref):
    spectra = dot(table_ref[...], field_ref[...], 1, 1)
    send_slots(spectra * factor, units, wide_ref, sent_ref)


def to_plane_modes(share, channels, halves, arrived_ref, forward_ref, wide_ref, modes_ref):
    slots = received_slots(arrived_ref, halves, 2 * share * halves, wide_ref)
    devices = wide_ref.shape[0] // (2 * share * halves)
    lanes = slots.shape[1]
    turned = slots.T
    blocks = []
    for slot in range(2 * share):
        pieces = [
            turned[c * channels : (c + 1) * channels, slot * devices : (slot + 1) * devices]
            for c in range(lanes // channels)
        ]
        blocks.append(jnp.concatenate(pieces, 1))
    rows = []
    for k in range(share):
        real, imag = blocks[2 * k], blocks[2 * k + 1]
        rows += [jnp.concatenate([real, imag], 1), jnp.concatenate([imag, -real], 1)]
    modes = dot(jnp.concatenate(rows, 0).astype(jnp.bfloat16), forward_ref[...])
    each = modes_ref.shape[0] // share
    for k in range(share):
        for j in range(each):
            modes_ref[k * each + j] = modes[2 * k * channels : (2 * k + 2) * channels, j * LANES : (j + 1) * LANES]


def store_pair(tile, channels, real, imag, pair_ref):
    pair_ref[tile, :channels, :LANES] = real.astype(jnp.bfloat16)
    pair_ref[tile, channels:, :LANES] = imag.astype(jnp.bfloat16)
    pair_ref[tile, :channels, LANES:] = (-imag).astype(jnp.bfloat16)
    pair_ref[tile, channels:, LANES:] = real.astype(jnp.bfloat16)


def to_cells(share, channels, halves, pair_ref, inverse_ref, wide_ref, sent_ref):
    units = 2 * share * halves
    devices = wide_ref.shape[0] // units
    each = pair_ref.shape[0] // share
    spectra = []
    for k in range(share):
        cosine = jnp.concatenate([pair_ref[k * each + j, :, :LANES] for j in range(each)], 1)
        sine = jnp.concatenate([pair_ref[k * each + j, :, LANES:] for j in range(each)], 1)
        spectra.append(jnp.concatenate([cosine, sine], 1))
    total = dot(inverse_ref[...], jnp.concatenate(spectra, 0), 1, 1)
    per_half = LANES // channels
    for unit in range(units):
        slot, h = divmod(unit, halves)
        columns = slice(slot * channels, (slot + 1) * channels)
        pieces = [total[c * devices : (c + 1) * devices, columns] for c in range(h * per_half, (h + 1) * per_half)]
        wide_ref[unit_rows(unit, wide_ref, units), :] = jnp.concatenate(pieces, 1)
    sent_ref[...] = wide_ref[...].astype(jnp.bfloat16)


def fold_rows(weight_ref, mode, first, count, columns):
    row = lax.broadcasted_iota(jnp.int32, (8, LANES), 0)
    low = jnp.where(row < 4, 1.0, 0.0)
    high = 1.0 - low
    folded = []
    for residue in range(first, first + count):
        total = None
        for kx in modes_of(residue):
            rows = pl.ds(pl.multiple_of((mode * KX + kx) * KY, 8), KY)
            block = weight_ref[rows, columns].astype(jnp.float32)
            total = block if total is None else total + block
        folded += [total[:8] + high * total[8:16], total[16:] + low * total[8:16]]
    return jnp.concatenate(folded, 0).astype(jnp.bfloat16)


def mix_kernel(
    share, channels, halves, arrived_ref, weight_ref, forward_ref, inverse_ref, sent_ref, modes_ref, turned_ref,
    wide_ref, pair_ref,
):
    to_plane_modes(share, channels, halves, arrived_ref, forward_ref, wide_ref, modes_ref)
    wide = 2 * channels
    each = modes_ref.shape[0] // share
    per_tile = LANES // LENGTH

    @pl.loop(0, share)
    def _(k):
        for j in range(each):
            tile = k * each + j
            by_real = jnp.zeros((wide, LANES), jnp.float32)
            by_imag = jnp.zeros((wide, LANES), jnp.float32)
            for first in range(0, channels, GROUP):
                real_sum, imag_sum = None, None
                for c in range(first, first + GROUP, LANES // wide):
                    columns = slice(c * wide, c * wide + LANES)
                    block = fold_rows(weight_ref, k, j * per_tile, per_tile, columns).T
                    turned_ref[tile, columns, :] = block
                    for h in range(LANES // wide):
                        weight = block[h * wide : (h + 1) * wide]
                        real = jnp.broadcast_to(modes_ref[tile, c + h : c + h + 1, :], (wide, LANES))
                        imag = jnp.broadcast_to(
                            modes_ref[tile, channels + c + h : channels + c + h + 1, :], (wide, LANES)
                        )
                        real, imag = real.astype(jnp.bfloat16) * weight, imag.astype(jnp.bfloat16) * weight
                        real_sum = real if real_sum is None else real_sum + real
                        imag_sum = imag if imag_sum is None else imag_sum + imag
                by_real += real_sum.astype(jnp.float32)
                by_imag += imag_sum.astype(jnp.float32)
            store_pair(
                tile, channels, by_real[:channels] - by_imag[channels:],
                by_real[channels:] + by_imag[:channels], pair_ref,
            )

    to_cells(share, channels, halves, pair_ref, inverse_ref, wide_ref, sent_ref)


def row_sums(blocks):
    row = lax.broadcasted_iota(jnp.int32, (8, LANES), 0)
    for shift in (4, 2, 1):
        merged = []
        clear = row % (2 * shift) < shift
        for i in range(shift):
            first, second = blocks[i], blocks[i + shift]
            merged.append(
                jnp.where(clear, first + pltpu.roll(first, 8 - shift, 0), second + pltpu.roll(second, shift, 0))
            )
        blocks = merged
    return blocks[0]


def adjoint_kernel(
    share, channels, halves, arrived_ref, turned_ref, forward_ref, inverse_ref, sent_ref, modes_ref, wide_ref,
    pair_ref,
):
    to_plane_modes(share, channels, halves, arrived_ref, forward_ref, wide_ref, modes_ref)
    wide = 2 * channels

    @pl.loop(0, modes_ref.shape[0])
    def _(tile):
        real, imag = modes_ref[tile, :channels, :], modes_ref[tile, channels:, :]
        here = jnp.concatenate([real, imag], 0).astype(jnp.bfloat16)
        turn = jnp.concatenate([imag, -real], 0).astype(jnp.bfloat16)
        sums = ([], [])
        for first in range(0, channels, 8):
            blocks = ([], [])
            for c in range(first, first + 8):
                weight = turned_ref[tile, c * wide : (c + 1) * wide, :]
                for part, factor in enumerate((here, turn)):
                    product = factor * weight
                    product = product[: wide // 2] + product[wide // 2 :]
                    product = (product[: wide // 4] + product[wide // 4 :]).astype(jnp.float32)
                    blocks[part].append(product[:8] + product[8:])
            for part in range(2):
                sums[part].append(row_sums(blocks[part]))
        store_pair(tile, channels, jnp.concatenate(sums[0], 0), jnp.concatenate(sums[1], 0), pair_ref)

    to_cells(share, channels, halves, pair_ref, inverse_ref, wide_ref, sent_ref)


def outer_kernel(share, channels, in_ref, back_ref, slope_ref, point_ref, grad_ref, pointwise_ref, held_ref, sems):
    wide = 2 * channels
    each = in_ref.shape[0] // share
    per_block = LANES // wide
    per_tile = LANES // LENGTH

    def runs(j):
        inside = [kx for kx in range(KX) if residue_of(kx) // per_tile == j]
        found = []
        for kx in inside:
            if found and found[-1][0] + found[-1][2] == kx and found[-1][1] + found[-1][2] == residue_of(kx):
                found[-1][2] += 1
            else:
                found.append([kx, residue_of(kx), 1])
        return found

    def copies(k, j):
        made = []
        for place, (mode, residue, count) in enumerate(runs(j)):
            source = pl.ds(pl.multiple_of((k * LENGTH + residue) * KY, 8), count * KY)
            target = pl.ds(pl.multiple_of((k * KX + mode) * KY, 8), count * KY)
            made.append(
                pltpu.make_async_copy(held_ref.at[source], grad_ref.at[target], sems.at[k * each + j, place])
            )
        return made

    low = lax.broadcasted_iota(jnp.int32, (8, LANES), 0) < 4

    @pl.loop(0, share)
    def _(k):
        for j in range(each):
            tile = k * each + j
            real, imag = back_ref[tile, :channels, :], back_ref[tile, channels:, :]
            here = jnp.concatenate([real, imag], 0)
            turn = jnp.concatenate([imag, -real], 0)
            for c in range(0, channels, per_block):
                parts = [
                    in_ref[tile, c + h : c + h + 1, :] * here
                    + in_ref[tile, channels + c + h : channels + c + h + 1, :] * turn
                    for h in range(per_block)
                ]
                block = jnp.concatenate(parts, 0).T
                for i in range(per_tile):
                    first = block[i * LENGTH : i * LENGTH + 8]
                    second = block[i * LENGTH + 8 : (i + 1) * LENGTH]
                    rows = pl.ds(pl.multiple_of((k * LENGTH + j * per_tile + i) * KY, 8), KY)
                    held_ref[rows, c * wide : c * wide + LANES] = jnp.concatenate(
                        [first, jnp.where(low, second, first), second], 0
                    )
            for copy in copies(k, j):
                copy.start()

    for first in range(0, slope_ref.shape[0], channels):
        rows = slice(first, first + channels)
        pointwise_ref[rows, :] = dot(point_ref[...], slope_ref[rows, :])

    @pl.loop(0, share)
    def _(k):
        for j in range(each):
            for copy in copies(k, j):
                copy.wait()


def slope_kernel(
    cells, channels, factor, units, arrived_ref, table_ref, field_ref, cotangent_ref, point_ref, slope_ref, sent_ref,
    wide_ref,
):
    arrived = received_slots(arrived_ref, cells * channels // LANES, units, wide_ref)
    spectral = dot(arrived.astype(jnp.bfloat16), table_ref[...], 0, 0)
    for c in range(cells):
        rows = slice(c * channels, (c + 1) * channels)
        before = spectral[rows] * factor + dot(point_ref[...], field_ref[rows, :], 0, 0)
        cumulative = 0.5 + 0.5 * lax.erf(before * math.sqrt(0.5))
        density = jnp.exp(-0.5 * before * before) * (1.0 / math.sqrt(2.0 * math.pi))
        slope = cotangent_ref[rows, :].astype(jnp.float32) * (cumulative + before * density)
        slope_ref[rows, :] = slope.astype(jnp.bfloat16)
    sent = dot(table_ref[...], slope_ref[...], 1, 1)
    send_slots(sent * factor, units, wide_ref, sent_ref)


def final_kernel(factor, halves, units, arrived_ref, table_ref, pointwise_ref, grad_ref, wide_ref):
    arrived = received_slots(arrived_ref, halves, units, wide_ref)
    spectral = dot(arrived.astype(jnp.bfloat16), table_ref[...], 0, 0)
    grad_ref[...] = (pointwise_ref[...] + spectral * factor).astype(jnp.bfloat16)


def params(mebibytes, semantics=None):
    return pltpu.CompilerParams(dimension_semantics=semantics, vmem_limit_bytes=mebibytes * 1024 * 1024)


def on_chip(value):
    return pltpu.with_memory_space_constraint(value, pltpu.VMEM)


def off_chip(value):
    return pltpu.with_memory_space_constraint(value, pltpu.HBM)


IN_VMEM = pl.BlockSpec(memory_space=pltpu.VMEM)


def per_device(inputs, cotangent, point_weight, spectral_weight):
    rows_x, rows_y, channels, depth = inputs.shape
    mode_rows, mode_cols, flat = spectral_weight.shape
    count_gx, count_gy = lax.axis_size("gx"), lax.axis_size("gy")
    devices = count_gx * count_gy
    share = mode_rows // KX
    cells = rows_x * rows_y
    lanes = cells * channels
    wide = 2 * channels
    plane = KX * KY
    points = cells * devices
    each = points // LANES
    tiles = share * each
    halves = lanes // LANES
    units = 2 * share * halves
    inner = 1.0 / math.sqrt(points * depth)
    outer = 1.0 / math.sqrt(plane * KZ * KT)

    table = on_chip(jnp.asarray(depth_table(share)))
    forward, inverse = (on_chip(jnp.asarray(t)) for t in plane_tables(count_gx, count_gy, rows_x, rows_y))
    field = on_chip(inputs.reshape(lanes, depth))
    seed = on_chip(cotangent.reshape(lanes, depth))
    point = on_chip(point_weight)

    def exchange(sent):
        blocks = sent.reshape(devices * units // 4, 4, LANES)
        arrived = lax.all_to_all(blocks, GRID_AXES, split_axis=0, concat_axis=0, tiled=True)
        return on_chip(arrived.reshape(devices * units, LANES))

    packet = pltpu.VMEM((devices * units, LANES), jnp.bfloat16)
    unpacked = pltpu.VMEM((devices * units, LANES), jnp.float32)
    spectra = pltpu.VMEM((tiles, wide, LANES), jnp.float32)

    sent = pl.pallas_call(
        functools.partial(depth_kernel, inner, units),
        in_specs=[IN_VMEM] * 2, out_specs=IN_VMEM, out_shape=packet, scratch_shapes=[unpacked],
        compiler_params=params(2),
        cost_estimate=pl.CostEstimate(flops=READ_AHEAD_FLOPS, transcendentals=0, bytes_accessed=0),
        name="depth",
    )(off_chip(jnp.asarray(depth_table(share))), off_chip(inputs.reshape(lanes, depth)))
    arrived = exchange(sent)
    scratch = [unpacked, pltpu.VMEM((tiles, wide, 2 * LANES), jnp.bfloat16)]
    sent, modes_in, turned = pl.pallas_call(
        functools.partial(mix_kernel, share, channels, halves),
        in_specs=[IN_VMEM] * 4, out_specs=[IN_VMEM] * 3,
        out_shape=[packet, spectra, pltpu.VMEM((tiles, flat, LANES), jnp.bfloat16)],
        scratch_shapes=scratch, compiler_params=params(6), name="mix",
    )(arrived, on_chip(spectral_weight.reshape(share * plane, flat)), forward, inverse)
    arrived = exchange(sent)
    slope, sent = pl.pallas_call(
        functools.partial(slope_kernel, cells, channels, outer, units),
        in_specs=[IN_VMEM] * 5, out_specs=[IN_VMEM] * 2, out_shape=[pltpu.VMEM((lanes, depth), jnp.bfloat16), packet],
        scratch_shapes=[unpacked],
        compiler_params=params(8), name="slope",
    )(arrived, table, field, seed, point)
    arrived = exchange(sent)
    sent, modes_back = pl.pallas_call(
        functools.partial(adjoint_kernel, share, channels, halves),
        in_specs=[IN_VMEM] * 4, out_specs=[IN_VMEM] * 2, out_shape=[packet, spectra],
        scratch_shapes=scratch,
        compiler_params=params(12), name="adjoint",
    )(arrived, on_chip(turned), forward, inverse)
    arrived = exchange(sent)
    grad_spectral, pointwise = pl.pallas_call(
        functools.partial(outer_kernel, share, channels),
        in_specs=[IN_VMEM] * 4, out_specs=[pl.BlockSpec(memory_space=pl.ANY), IN_VMEM],
        out_shape=[
            jax.ShapeDtypeStruct((share * plane, flat), jnp.float32), pltpu.VMEM((lanes, depth), jnp.float32),
        ],
        scratch_shapes=[
            pltpu.VMEM((share * LENGTH * KY, flat), jnp.float32), pltpu.SemaphoreType.DMA((tiles, 2)),
        ],
        compiler_params=params(24),
        cost_estimate=pl.CostEstimate(
            flops=4 * share * plane * flat * wide, transcendentals=0, bytes_accessed=4 * share * plane * flat
        ),
        name="outer",
    )(on_chip(modes_in), on_chip(modes_back), on_chip(slope), point)
    grad_input = pl.pallas_call(
        functools.partial(final_kernel, inner, halves, units),
        in_specs=[IN_VMEM] * 3, out_specs=IN_VMEM, out_shape=jax.ShapeDtypeStruct((lanes, depth), jnp.bfloat16),
        scratch_shapes=[unpacked],
        compiler_params=params(8), name="final",
    )(arrived, table, on_chip(pointwise))
    return grad_input.reshape(inputs.shape), grad_spectral.reshape(spectral_weight.shape)


def kept_angles(positions, kept_count, length):
    index = jnp.arange(kept_count, dtype=jnp.int32)
    frequency = jnp.where(index < kept_count // 2, index, index - kept_count)
    turns = positions[:, None] * frequency[None, :] % length
    return turns.astype(jnp.float32) * (2.0 * math.pi / length)


def axis_tables(positions, kept_count, length):
    angles = kept_angles(positions, kept_count, length)
    return (jnp.cos(angles), jnp.sin(angles))


def depth_tables():
    angle_depth = kept_angles(jnp.arange(NZ, dtype=jnp.int32), KZ, NZ)
    angle_time = kept_angles(jnp.arange(NT, dtype=jnp.int32), KT, NT)
    angles = (angle_depth[:, None, :, None] + angle_time[None, :, None, :]).reshape(
        NZ * NT, KZ * KT
    )
    return (jnp.cos(angles), jnp.sin(angles))


def settle(values):
    return lax.optimization_barrier(values.astype(jnp.bfloat16))


def rotate(spectra, cosine_table, sine_table, pattern, turn_sign):
    half_width = spectra.shape[-1] // 2
    with_cosine = jnp.einsum(pattern, spectra, cosine_table, precision=lax.Precision.HIGHEST)
    with_sine = jnp.einsum(pattern, spectra, sine_table, precision=lax.Precision.HIGHEST)
    real_part = with_cosine[..., :half_width] + turn_sign * with_sine[..., half_width:]
    imag_part = with_cosine[..., half_width:] - turn_sign * with_sine[..., :half_width]
    return jnp.concatenate([real_part, imag_part], -1)


def depth_forward(field_in, tables, factor):
    widened = field_in.astype(jnp.float32)
    with_cosine = jnp.einsum("xycs,sk->kxyc", widened, tables[0], precision=lax.Precision.HIGHEST)
    with_sine = jnp.einsum("xycs,sk->kxyc", widened, tables[1], precision=lax.Precision.HIGHEST)
    return jnp.concatenate([with_cosine, -with_sine], -1) * factor


def depth_inverse(spectra, tables, factor):
    half_width = spectra.shape[-1] // 2
    with_cosine = jnp.einsum(
        "kxyc,sk->xycs", spectra[..., :half_width], tables[0], precision=lax.Precision.HIGHEST
    )
    with_sine = jnp.einsum(
        "kxyc,sk->xycs", spectra[..., half_width:], tables[1], precision=lax.Precision.HIGHEST
    )
    return (with_cosine - with_sine) * factor


def contract_in(left, right):
    return jnp.einsum("mkc,mkco->mko", left, right, precision=lax.Precision.HIGHEST)


def contract_out(left, right):
    return jnp.einsum("mko,mkco->mkc", left, right, precision=lax.Precision.HIGHEST)


def partial_outer(left, right):
    return jnp.einsum("mkc,mko->mkco", left, right, precision=lax.Precision.HIGHEST)


def mix_modes(spectra, weight):
    half_width = spectra.shape[-1] // 2
    weight_wide = weight.astype(jnp.float32)
    weight_real, weight_imag = (weight_wide[..., :half_width], weight_wide[..., half_width:])
    real_in, imag_in = (spectra[..., :half_width], spectra[..., half_width:])
    real_out = contract_in(real_in, weight_real) - contract_in(imag_in, weight_imag)
    imag_out = contract_in(real_in, weight_imag) + contract_in(imag_in, weight_real)
    return jnp.concatenate([real_out, imag_out], -1)


def adjoint_modes(spectra, weight):
    half_width = spectra.shape[-1] // 2
    weight_wide = weight.astype(jnp.float32)
    weight_real, weight_imag = (weight_wide[..., :half_width], weight_wide[..., half_width:])
    real_in, imag_in = (spectra[..., :half_width], spectra[..., half_width:])
    real_out = contract_out(real_in, weight_real) + contract_out(imag_in, weight_imag)
    imag_out = contract_out(imag_in, weight_real) - contract_out(real_in, weight_imag)
    return jnp.concatenate([real_out, imag_out], -1)


def weight_grad(spectra_in, spectra_back):
    half_width = spectra_in.shape[-1] // 2
    real_in, imag_in = (spectra_in[..., :half_width], spectra_in[..., half_width:])
    real_back, imag_back = (spectra_back[..., :half_width], spectra_back[..., half_width:])
    real_part = partial_outer(real_in, real_back) + partial_outer(imag_in, imag_back)
    imag_part = partial_outer(real_in, imag_back) - partial_outer(imag_in, real_back)
    return jnp.concatenate([real_part, imag_part], -1)


def exact_gelu(values):
    return jax.nn.gelu(values, approximate=False)


def general_per_device(inputs, cotangent, point_weight, spectral_weight):
    rows_x, rows_y, channels, cells = inputs.shape
    mode_rows, mode_cols, flat_width = spectral_weight.shape
    weight_blocks = spectral_weight.reshape(mode_rows, mode_cols, channels, 2 * channels)
    count_gx = lax.axis_size("gx")
    count_gy = lax.axis_size("gy")
    length_x = rows_x * count_gx
    length_y = rows_y * count_gy
    depth_pair = depth_tables()
    own_x = lax.axis_index("gx") * rows_x + jnp.arange(rows_x, dtype=jnp.int32)
    local_x = axis_tables(own_x, KX, length_x)
    whole_y = axis_tables(jnp.arange(length_y, dtype=jnp.int32), KY, length_y)
    total_cells = length_x * length_y * cells
    kept_total = KX * KY * KZ * KT

    def to_modes(field_in, factor):
        depth_spec = settle(depth_forward(field_in, depth_pair, factor))
        share = depth_spec.shape[0] // count_gx
        first_spectra = lax.psum_scatter(
            rotate(
                depth_spec.astype(jnp.float32), local_x[0], local_x[1], "rxyc,xk->rkyc", 1.0
            ).astype(jnp.bfloat16),
            "gx",
            scatter_dimension=0,
            tiled=True,
        ).astype(jnp.float32)
        first_spectra = settle(first_spectra).reshape(share * KX, rows_y, 2 * channels)
        arrived_modes = lax.all_to_all(first_spectra, "gy", split_axis=0, concat_axis=1, tiled=True)
        return rotate(arrived_modes.astype(jnp.float32), whole_y[0], whole_y[1], "myc,yk->mkc", 1.0)

    def to_space(spectra, factor):
        back_rows = settle(rotate(spectra, whole_y[0], whole_y[1], "mkc,yk->myc", -1.0))
        returned = lax.all_to_all(back_rows, "gy", split_axis=1, concat_axis=0, tiled=True)
        share = returned.shape[0] // KX
        returned = returned.reshape(share, KX, rows_y, 2 * channels)
        back_depth = settle(
            rotate(
                lax.all_gather(returned, "gx", axis=0, tiled=True).astype(jnp.float32),
                local_x[0],
                local_x[1],
                "rkyc,xk->rxyc",
                -1.0,
            )
        )
        return depth_inverse(back_depth.astype(jnp.float32), depth_pair, factor)

    spectra_in = to_modes(inputs, 1.0 / math.sqrt(total_cells))
    mixed = mix_modes(spectra_in, weight_blocks)
    spectral_out = to_space(mixed, 1.0 / math.sqrt(kept_total))
    pointwise = jnp.einsum(
        "xycs,co->xyos", inputs, point_weight, preferred_element_type=jnp.float32
    )
    before = spectral_out + pointwise
    unused_out, pullback = jax.vjp(exact_gelu, before)
    slope = settle(pullback(cotangent.astype(jnp.float32))[0])
    spectra_back = to_modes(slope, 1.0 / math.sqrt(kept_total))
    grad_spectral = weight_grad(spectra_in, spectra_back).reshape(mode_rows, mode_cols, flat_width)
    adjoint = adjoint_modes(spectra_back, weight_blocks)
    spectral_grad = to_space(adjoint, 1.0 / math.sqrt(total_cells))
    pointwise_grad = jnp.einsum(
        "xyos,co->xycs", slope, point_weight, preferred_element_type=jnp.float32
    )
    grad_input = (pointwise_grad + spectral_grad).astype(jnp.bfloat16)
    return (grad_input, grad_spectral)


def solution(mesh):
    count_gx, count_gy = mesh.shape["gx"], mesh.shape["gy"]
    placed = (
        P("gx", "gy", None, None),
        P("gx", "gy", None, None),
        P(),
        P(("gx", "gy"), None, None),
    )

    def program(inputs, cotangent, point_weight, spectral_weight):
        cells = inputs.shape[0] * inputs.shape[1] // (count_gx * count_gy)
        whole_modes = KZ * KT % (count_gx * count_gy) == 0
        fits = whole_modes and KZ * KT // (count_gx * count_gy) == 3
        fits = fits and inputs.shape[2] == 32 and cells * inputs.shape[2] == 256 and inputs.shape[0] == inputs.shape[1] == LENGTH
        return jax.shard_map(
            per_device if fits else general_per_device,
            mesh=mesh,
            in_specs=placed,
            out_specs=(P("gx", "gy", None, None), P(("gx", "gy"), None, None)),
            check_vma=False,
        )(inputs, cotangent, point_weight, spectral_weight)

    return program
```

```python
import functools
import math

import jax
import jax.numpy as jnp
import numpy as np
from jax import lax
from jax.experimental import pallas as pl
from jax.experimental.pallas import tpu as pltpu
from jax.sharding import PartitionSpec as P

NZ = 64
NT = 8
KX = 24
KY = 24
KZ = 12
KT = 8
LANES = 128
LENGTH = 16
GROUP = 4
READ_AHEAD_FLOPS = 10**11
GRID_AXES = ("gx", "gy")


def table_angles(positions, kept_count, length):
    index = np.arange(kept_count)
    frequency = np.where(index < kept_count // 2, index, index - kept_count)
    turns = (np.asarray(positions)[:, None] * frequency[None, :]) % length
    return 2.0 * np.pi * turns / length


def depth_table(share):
    angles = (
        table_angles(np.arange(NZ), KZ, NZ)[:, None, :, None]
        + table_angles(np.arange(NT), KT, NT)[None, :, None, :]
    ).reshape(NZ * NT, KZ * KT)
    parts = np.stack([np.cos(angles), -np.sin(angles)], -1)
    owners = KZ * KT // share
    rows = parts.reshape(NZ * NT, owners, 2 * share).transpose(2, 1, 0)
    return rows.reshape(2 * share * owners, NZ * NT).astype(jnp.bfloat16)


def plane_tables(count_gx, count_gy, rows_x, rows_y):
    length_x, length_y = count_gx * rows_x, count_gy * rows_y
    turns_x = np.outer(np.arange(length_x), np.arange(length_x)) % length_x / length_x
    turns_y = np.outer(np.arange(length_y), np.arange(length_y)) % length_y / length_y
    turns_x = turns_x.reshape(length_x, 1, count_gx, 1, rows_x, 1)
    turns_y = turns_y.reshape(1, length_y, 1, count_gy, 1, rows_y)
    turns = (turns_x + turns_y).transpose(0, 1, 4, 5, 2, 3).reshape(length_x * length_y, length_x * length_y)
    cosine, sine = np.cos(2.0 * np.pi * turns), np.sin(2.0 * np.pi * turns)
    forward = np.concatenate([cosine.T, sine.T], 0)
    inverse = np.concatenate([cosine.T, sine.T], 1)
    return forward.astype(jnp.bfloat16), inverse.astype(jnp.bfloat16)


def residue_of(mode):
    return (mode if mode < KX // 2 else mode - KX) % LENGTH


def modes_of(residue):
    return [mode for mode in range(KX) if residue_of(mode) == residue]


def dot(left, right, left_dim=1, right_dim=0):
    return lax.dot_general(
        left, right, (((left_dim,), (right_dim,)), ((), ())), preferred_element_type=jnp.float32
    )


def unit_rows(unit, wide_ref, units):
    return pl.ds(unit, wide_ref.shape[0] // units, stride=units)


def send_slots(spectra, units, wide_ref, sent_ref):
    devices = wide_ref.shape[0] // units
    halves = spectra.shape[1] // LANES
    for unit in range(units):
        slot, h = divmod(unit, halves)
        wide_ref[unit_rows(unit, wide_ref, units), :] = spectra[
            slot * devices : (slot + 1) * devices, h * LANES : (h + 1) * LANES
        ]
    sent_ref[...] = wide_ref[...].astype(jnp.bfloat16)


def received_slots(arrived_ref, halves, units, wide_ref):
    wide_ref[...] = arrived_ref[...].astype(jnp.float32)
    slots = []
    for slot in range(units // halves):
        pieces = [wide_ref[unit_rows(slot * halves + h, wide_ref, units), :] for h in range(halves)]
        slots.append(jnp.concatenate(pieces, 1))
    return jnp.concatenate(slots, 0)


def depth_kernel(factor, units, table_ref, field_ref, sent_ref, wide_ref):
    spectra = dot(table_ref[...], field_ref[...], 1, 1)
    send_slots(spectra * factor, units, wide_ref, sent_ref)


def to_plane_modes(share, channels, halves, arrived_ref, forward_ref, wide_ref, modes_ref):
    slots = received_slots(arrived_ref, halves, 2 * share * halves, wide_ref)
    devices = wide_ref.shape[0] // (2 * share * halves)
    lanes = slots.shape[1]
    turned = slots.astype(jnp.bfloat16).T
    blocks = []
    for slot in range(2 * share):
        pieces = [
            turned[c * channels : (c + 1) * channels, slot * devices : (slot + 1) * devices]
            for c in range(lanes // channels)
        ]
        blocks.append(jnp.concatenate(pieces, 1))
    rows = []
    for k in range(share):
        real, imag = blocks[2 * k], blocks[2 * k + 1]
        rows += [jnp.concatenate([real, imag], 1), jnp.concatenate([imag, -real], 1)]
    modes = dot(jnp.concatenate(rows, 0), forward_ref[...])
    each = modes_ref.shape[0] // share
    for k in range(share):
        for j in range(each):
            modes_ref[k * each + j] = modes[2 * k * channels : (2 * k + 2) * channels, j * LANES : (j + 1) * LANES]


def store_pair(tile, channels, real, imag, pair_ref):
    pair_ref[tile, :channels, :LANES] = real.astype(jnp.bfloat16)
    pair_ref[tile, channels:, :LANES] = imag.astype(jnp.bfloat16)
    pair_ref[tile, :channels, LANES:] = (-imag).astype(jnp.bfloat16)
    pair_ref[tile, channels:, LANES:] = real.astype(jnp.bfloat16)


def to_cells(share, channels, halves, pair_ref, inverse_ref, wide_ref, sent_ref):
    units = 2 * share * halves
    devices = wide_ref.shape[0] // units
    each = pair_ref.shape[0] // share
    spectra = []
    for k in range(share):
        cosine = jnp.concatenate([pair_ref[k * each + j, :, :LANES] for j in range(each)], 1)
        sine = jnp.concatenate([pair_ref[k * each + j, :, LANES:] for j in range(each)], 1)
        spectra.append(jnp.concatenate([cosine, sine], 1))
    total = dot(inverse_ref[...], jnp.concatenate(spectra, 0), 1, 1)
    per_half = LANES // channels
    for unit in range(units):
        slot, h = divmod(unit, halves)
        columns = slice(slot * channels, (slot + 1) * channels)
        pieces = [total[c * devices : (c + 1) * devices, columns] for c in range(h * per_half, (h + 1) * per_half)]
        wide_ref[unit_rows(unit, wide_ref, units), :] = jnp.concatenate(pieces, 1)
    sent_ref[...] = wide_ref[...].astype(jnp.bfloat16)


def fold_rows(weight_ref, mode, first, count, columns):
    row = lax.broadcasted_iota(jnp.int32, (8, LANES), 0)
    low = jnp.where(row < 4, 1.0, 0.0).astype(jnp.bfloat16)
    high = jnp.bfloat16(1) - low
    folded = []
    for residue in range(first, first + count):
        total = None
        for kx in modes_of(residue):
            rows = pl.ds(pl.multiple_of((mode * KX + kx) * KY, 8), KY)
            block = weight_ref[rows, columns]
            total = block if total is None else total + block
        folded += [total[:8] + high * total[8:16], total[16:] + low * total[8:16]]
    return jnp.concatenate(folded, 0)


def mix_kernel(
    share, channels, halves, arrived_ref, weight_ref, forward_ref, inverse_ref, sent_ref, modes_ref, turned_ref,
    wide_ref, pair_ref,
):
    to_plane_modes(share, channels, halves, arrived_ref, forward_ref, wide_ref, modes_ref)
    wide = 2 * channels
    each = modes_ref.shape[0] // share
    per_tile = LANES // LENGTH

    for k in range(share):
        for j in range(each):
            tile = k * each + j
            by_real = jnp.zeros((wide, LANES), jnp.float32)
            by_imag = jnp.zeros((wide, LANES), jnp.float32)
            for first in range(0, channels, GROUP):
                real_sum, imag_sum = None, None
                for c in range(first, first + GROUP, LANES // wide):
                    columns = slice(c * wide, c * wide + LANES)
                    block = fold_rows(weight_ref, k, j * per_tile, per_tile, columns).T
                    turned_ref[tile, columns, :] = block
                    for h in range(LANES // wide):
                        weight = block[h * wide : (h + 1) * wide]
                        real = jnp.broadcast_to(modes_ref[tile, c + h : c + h + 1, :], (wide, LANES))
                        imag = jnp.broadcast_to(
                            modes_ref[tile, channels + c + h : channels + c + h + 1, :], (wide, LANES)
                        )
                        real, imag = real.astype(jnp.bfloat16) * weight, imag.astype(jnp.bfloat16) * weight
                        real_sum = real if real_sum is None else real_sum + real
                        imag_sum = imag if imag_sum is None else imag_sum + imag
                by_real += real_sum.astype(jnp.float32)
                by_imag += imag_sum.astype(jnp.float32)
            store_pair(
                tile, channels, by_real[:channels] - by_imag[channels:],
                by_real[channels:] + by_imag[:channels], pair_ref,
            )

    to_cells(share, channels, halves, pair_ref, inverse_ref, wide_ref, sent_ref)


def row_sums(blocks):
    row = lax.broadcasted_iota(jnp.int32, (8, LANES), 0)
    for shift in (4, 2, 1):
        merged = []
        clear = row % (2 * shift) < shift
        for i in range(shift):
            first, second = blocks[i], blocks[i + shift]
            merged.append(
                jnp.where(clear, first + pltpu.roll(first, 8 - shift, 0), second + pltpu.roll(second, shift, 0))
            )
        blocks = merged
    return blocks[0]


def adjoint_kernel(
    share, channels, halves, arrived_ref, turned_ref, forward_ref, inverse_ref, sent_ref, modes_ref, wide_ref,
    pair_ref,
):
    to_plane_modes(share, channels, halves, arrived_ref, forward_ref, wide_ref, modes_ref)
    wide = 2 * channels

    for tile in range(modes_ref.shape[0]):
        real, imag = modes_ref[tile, :channels, :], modes_ref[tile, channels:, :]
        here = jnp.concatenate([real, imag], 0).astype(jnp.bfloat16)
        turn = jnp.concatenate([imag, -real], 0).astype(jnp.bfloat16)
        sums = ([], [])
        for first in range(0, channels, 8):
            blocks = ([], [])
            for c in range(first, first + 8):
                weight = turned_ref[tile, c * wide : (c + 1) * wide, :]
                for part, factor in enumerate((here, turn)):
                    product = factor * weight
                    product = product[: wide // 2] + product[wide // 2 :]
                    product = (product[: wide // 4] + product[wide // 4 :]).astype(jnp.float32)
                    blocks[part].append(product[:8] + product[8:])
            for part in range(2):
                sums[part].append(row_sums(blocks[part]))
        store_pair(tile, channels, jnp.concatenate(sums[0], 0), jnp.concatenate(sums[1], 0), pair_ref)

    to_cells(share, channels, halves, pair_ref, inverse_ref, wide_ref, sent_ref)


def outer_kernel(share, channels, in_ref, back_ref, slope_ref, point_ref, grad_ref, pointwise_ref, held_ref, sems):
    wide = 2 * channels
    each = in_ref.shape[0] // share
    per_block = LANES // wide
    per_tile = LANES // LENGTH

    def runs(j):
        inside = [kx for kx in range(KX) if residue_of(kx) // per_tile == j]
        found = []
        for kx in inside:
            if found and found[-1][0] + found[-1][2] == kx and found[-1][1] + found[-1][2] == residue_of(kx):
                found[-1][2] += 1
            else:
                found.append([kx, residue_of(kx), 1])
        return found

    def copies(k, j):
        made = []
        for place, (mode, residue, count) in enumerate(runs(j)):
            source = pl.ds(pl.multiple_of((k * LENGTH + residue) * KY, 8), count * KY)
            target = pl.ds(pl.multiple_of((k * KX + mode) * KY, 8), count * KY)
            made.append(
                pltpu.make_async_copy(held_ref.at[source], grad_ref.at[target], sems.at[k * each + j, place])
            )
        return made

    low = lax.broadcasted_iota(jnp.int32, (8, LANES), 0) < 4

    @pl.loop(0, share)
    def _(k):
        for j in range(each):
            tile = k * each + j
            real, imag = back_ref[tile, :channels, :], back_ref[tile, channels:, :]
            here = jnp.concatenate([real, imag], 0)
            turn = jnp.concatenate([imag, -real], 0)
            for c in range(0, channels, per_block):
                parts = [
                    in_ref[tile, c + h : c + h + 1, :] * here
                    + in_ref[tile, channels + c + h : channels + c + h + 1, :] * turn
                    for h in range(per_block)
                ]
                block = jnp.concatenate(parts, 0).T
                for i in range(per_tile):
                    first = block[i * LENGTH : i * LENGTH + 8]
                    second = block[i * LENGTH + 8 : (i + 1) * LENGTH]
                    rows = pl.ds(pl.multiple_of((k * LENGTH + j * per_tile + i) * KY, 8), KY)
                    held_ref[rows, c * wide : c * wide + LANES] = jnp.concatenate(
                        [first, jnp.where(low, second, first), second], 0
                    )
            for copy in copies(k, j):
                copy.start()

    for first in range(0, slope_ref.shape[0], channels):
        rows = slice(first, first + channels)
        pointwise_ref[rows, :] = dot(point_ref[...], slope_ref[rows, :])

    @pl.loop(0, share)
    def _(k):
        for j in range(each):
            for copy in copies(k, j):
                copy.wait()


def slope_kernel(
    cells, channels, factor, units, arrived_ref, table_ref, field_ref, cotangent_ref, point_ref, slope_ref, sent_ref,
    wide_ref,
):
    arrived = received_slots(arrived_ref, cells * channels // LANES, units, wide_ref)
    spectral = dot(arrived.astype(jnp.bfloat16), table_ref[...], 0, 0)
    for c in range(cells):
        rows = slice(c * channels, (c + 1) * channels)
        before = spectral[rows] * factor + dot(point_ref[...], field_ref[rows, :], 0, 0)
        cumulative = 0.5 + 0.5 * lax.erf(before * math.sqrt(0.5))
        density = jnp.exp(-0.5 * before * before) * (1.0 / math.sqrt(2.0 * math.pi))
        slope = cotangent_ref[rows, :].astype(jnp.float32) * (cumulative + before * density)
        slope_ref[rows, :] = slope.astype(jnp.bfloat16)
    sent = dot(table_ref[...], slope_ref[...], 1, 1)
    send_slots(sent * factor, units, wide_ref, sent_ref)


def final_kernel(factor, halves, units, arrived_ref, table_ref, pointwise_ref, grad_ref, wide_ref):
    arrived = received_slots(arrived_ref, halves, units, wide_ref)
    spectral = dot(arrived.astype(jnp.bfloat16), table_ref[...], 0, 0)
    grad_ref[...] = (pointwise_ref[...] + spectral * factor).astype(jnp.bfloat16)


def params(mebibytes, semantics=None):
    return pltpu.CompilerParams(dimension_semantics=semantics, vmem_limit_bytes=mebibytes * 1024 * 1024)


def on_chip(value):
    return pltpu.with_memory_space_constraint(value, pltpu.VMEM)


def off_chip(value):
    return pltpu.with_memory_space_constraint(value, pltpu.HBM)


IN_VMEM = pl.BlockSpec(memory_space=pltpu.VMEM)


def per_device(inputs, cotangent, point_weight, spectral_weight):
    rows_x, rows_y, channels, depth = inputs.shape
    mode_rows, mode_cols, flat = spectral_weight.shape
    count_gx, count_gy = lax.axis_size("gx"), lax.axis_size("gy")
    devices = count_gx * count_gy
    share = mode_rows // KX
    cells = rows_x * rows_y
    lanes = cells * channels
    wide = 2 * channels
    plane = KX * KY
    points = cells * devices
    each = points // LANES
    tiles = share * each
    halves = lanes // LANES
    units = 2 * share * halves
    inner = 1.0 / math.sqrt(points * depth)
    outer = 1.0 / math.sqrt(plane * KZ * KT)

    table = on_chip(jnp.asarray(depth_table(share)))
    forward, inverse = (on_chip(jnp.asarray(t)) for t in plane_tables(count_gx, count_gy, rows_x, rows_y))
    field = on_chip(inputs.reshape(lanes, depth))
    seed = on_chip(cotangent.reshape(lanes, depth))
    point = on_chip(point_weight)

    def exchange(sent):
        blocks = sent.reshape(devices * units // 4, 4, LANES)
        arrived = lax.all_to_all(blocks, GRID_AXES, split_axis=0, concat_axis=0, tiled=True)
        return on_chip(arrived.reshape(devices * units, LANES))

    packet = pltpu.VMEM((devices * units, LANES), jnp.bfloat16)
    unpacked = pltpu.VMEM((devices * units, LANES), jnp.float32)
    spectra = pltpu.VMEM((tiles, wide, LANES), jnp.float32)

    sent = pl.pallas_call(
        functools.partial(depth_kernel, inner, units),
        in_specs=[IN_VMEM] * 2, out_specs=IN_VMEM, out_shape=packet, scratch_shapes=[unpacked],
        compiler_params=params(2),
        cost_estimate=pl.CostEstimate(flops=READ_AHEAD_FLOPS, transcendentals=0, bytes_accessed=0),
        name="depth",
    )(off_chip(jnp.asarray(depth_table(share))), off_chip(inputs.reshape(lanes, depth)))
    arrived = exchange(sent)
    scratch = [unpacked, pltpu.VMEM((tiles, wide, 2 * LANES), jnp.bfloat16)]
    sent, modes_in, turned = pl.pallas_call(
        functools.partial(mix_kernel, share, channels, halves),
        in_specs=[IN_VMEM] * 4, out_specs=[IN_VMEM] * 3,
        out_shape=[packet, spectra, pltpu.VMEM((tiles, flat, LANES), jnp.bfloat16)],
        scratch_shapes=scratch, compiler_params=params(6), name="mix",
    )(arrived, on_chip(spectral_weight.reshape(share * plane, flat)), forward, inverse)
    arrived = exchange(sent)
    slope, sent = pl.pallas_call(
        functools.partial(slope_kernel, cells, channels, outer, units),
        in_specs=[IN_VMEM] * 5, out_specs=[IN_VMEM] * 2, out_shape=[pltpu.VMEM((lanes, depth), jnp.bfloat16), packet],
        scratch_shapes=[unpacked],
        compiler_params=params(8), name="slope",
    )(arrived, table, field, seed, point)
    arrived = exchange(sent)
    sent, modes_back = pl.pallas_call(
        functools.partial(adjoint_kernel, share, channels, halves),
        in_specs=[IN_VMEM] * 4, out_specs=[IN_VMEM] * 2, out_shape=[packet, spectra],
        scratch_shapes=scratch,
        compiler_params=params(12), name="adjoint",
    )(arrived, on_chip(turned), forward, inverse)
    arrived = exchange(sent)
    grad_spectral, pointwise = pl.pallas_call(
        functools.partial(outer_kernel, share, channels),
        in_specs=[IN_VMEM] * 4, out_specs=[pl.BlockSpec(memory_space=pl.ANY), IN_VMEM],
        out_shape=[
            jax.ShapeDtypeStruct((share * plane, flat), jnp.float32), pltpu.VMEM((lanes, depth), jnp.float32),
        ],
        scratch_shapes=[
            pltpu.VMEM((share * LENGTH * KY, flat), jnp.float32), pltpu.SemaphoreType.DMA((tiles, 2)),
        ],
        compiler_params=params(24),
        cost_estimate=pl.CostEstimate(
            flops=4 * share * plane * flat * wide, transcendentals=0, bytes_accessed=4 * share * plane * flat
        ),
        name="outer",
    )(on_chip(modes_in), on_chip(modes_back), on_chip(slope), point)
    grad_input = pl.pallas_call(
        functools.partial(final_kernel, inner, halves, units),
        in_specs=[IN_VMEM] * 3, out_specs=IN_VMEM, out_shape=jax.ShapeDtypeStruct((lanes, depth), jnp.bfloat16),
        scratch_shapes=[unpacked],
        compiler_params=params(8), name="final",
    )(arrived, table, on_chip(pointwise))
    return grad_input.reshape(inputs.shape), grad_spectral.reshape(spectral_weight.shape)


def kept_angles(positions, kept_count, length):
    index = jnp.arange(kept_count, dtype=jnp.int32)
    frequency = jnp.where(index < kept_count // 2, index, index - kept_count)
    turns = positions[:, None] * frequency[None, :] % length
    return turns.astype(jnp.float32) * (2.0 * math.pi / length)


def axis_tables(positions, kept_count, length):
    angles = kept_angles(positions, kept_count, length)
    return (jnp.cos(angles), jnp.sin(angles))


def depth_tables():
    angle_depth = kept_angles(jnp.arange(NZ, dtype=jnp.int32), KZ, NZ)
    angle_time = kept_angles(jnp.arange(NT, dtype=jnp.int32), KT, NT)
    angles = (angle_depth[:, None, :, None] + angle_time[None, :, None, :]).reshape(
        NZ * NT, KZ * KT
    )
    return (jnp.cos(angles), jnp.sin(angles))


def settle(values):
    return lax.optimization_barrier(values.astype(jnp.bfloat16))


def rotate(spectra, cosine_table, sine_table, pattern, turn_sign):
    half_width = spectra.shape[-1] // 2
    with_cosine = jnp.einsum(pattern, spectra, cosine_table, precision=lax.Precision.HIGHEST)
    with_sine = jnp.einsum(pattern, spectra, sine_table, precision=lax.Precision.HIGHEST)
    real_part = with_cosine[..., :half_width] + turn_sign * with_sine[..., half_width:]
    imag_part = with_cosine[..., half_width:] - turn_sign * with_sine[..., :half_width]
    return jnp.concatenate([real_part, imag_part], -1)


def depth_forward(field_in, tables, factor):
    widened = field_in.astype(jnp.float32)
    with_cosine = jnp.einsum("xycs,sk->kxyc", widened, tables[0], precision=lax.Precision.HIGHEST)
    with_sine = jnp.einsum("xycs,sk->kxyc", widened, tables[1], precision=lax.Precision.HIGHEST)
    return jnp.concatenate([with_cosine, -with_sine], -1) * factor


def depth_inverse(spectra, tables, factor):
    half_width = spectra.shape[-1] // 2
    with_cosine = jnp.einsum(
        "kxyc,sk->xycs", spectra[..., :half_width], tables[0], precision=lax.Precision.HIGHEST
    )
    with_sine = jnp.einsum(
        "kxyc,sk->xycs", spectra[..., half_width:], tables[1], precision=lax.Precision.HIGHEST
    )
    return (with_cosine - with_sine) * factor


def contract_in(left, right):
    return jnp.einsum("mkc,mkco->mko", left, right, precision=lax.Precision.HIGHEST)


def contract_out(left, right):
    return jnp.einsum("mko,mkco->mkc", left, right, precision=lax.Precision.HIGHEST)


def partial_outer(left, right):
    return jnp.einsum("mkc,mko->mkco", left, right, precision=lax.Precision.HIGHEST)


def mix_modes(spectra, weight):
    half_width = spectra.shape[-1] // 2
    weight_wide = weight.astype(jnp.float32)
    weight_real, weight_imag = (weight_wide[..., :half_width], weight_wide[..., half_width:])
    real_in, imag_in = (spectra[..., :half_width], spectra[..., half_width:])
    real_out = contract_in(real_in, weight_real) - contract_in(imag_in, weight_imag)
    imag_out = contract_in(real_in, weight_imag) + contract_in(imag_in, weight_real)
    return jnp.concatenate([real_out, imag_out], -1)


def adjoint_modes(spectra, weight):
    half_width = spectra.shape[-1] // 2
    weight_wide = weight.astype(jnp.float32)
    weight_real, weight_imag = (weight_wide[..., :half_width], weight_wide[..., half_width:])
    real_in, imag_in = (spectra[..., :half_width], spectra[..., half_width:])
    real_out = contract_out(real_in, weight_real) + contract_out(imag_in, weight_imag)
    imag_out = contract_out(imag_in, weight_real) - contract_out(real_in, weight_imag)
    return jnp.concatenate([real_out, imag_out], -1)


def weight_grad(spectra_in, spectra_back):
    half_width = spectra_in.shape[-1] // 2
    real_in, imag_in = (spectra_in[..., :half_width], spectra_in[..., half_width:])
    real_back, imag_back = (spectra_back[..., :half_width], spectra_back[..., half_width:])
    real_part = partial_outer(real_in, real_back) + partial_outer(imag_in, imag_back)
    imag_part = partial_outer(real_in, imag_back) - partial_outer(imag_in, real_back)
    return jnp.concatenate([real_part, imag_part], -1)


def exact_gelu(values):
    return jax.nn.gelu(values, approximate=False)


def general_per_device(inputs, cotangent, point_weight, spectral_weight):
    rows_x, rows_y, channels, cells = inputs.shape
    mode_rows, mode_cols, flat_width = spectral_weight.shape
    weight_blocks = spectral_weight.reshape(mode_rows, mode_cols, channels, 2 * channels)
    count_gx = lax.axis_size("gx")
    count_gy = lax.axis_size("gy")
    length_x = rows_x * count_gx
    length_y = rows_y * count_gy
    depth_pair = depth_tables()
    own_x = lax.axis_index("gx") * rows_x + jnp.arange(rows_x, dtype=jnp.int32)
    local_x = axis_tables(own_x, KX, length_x)
    whole_y = axis_tables(jnp.arange(length_y, dtype=jnp.int32), KY, length_y)
    total_cells = length_x * length_y * cells
    kept_total = KX * KY * KZ * KT

    def to_modes(field_in, factor):
        depth_spec = settle(depth_forward(field_in, depth_pair, factor))
        share = depth_spec.shape[0] // count_gx
        first_spectra = lax.psum_scatter(
            rotate(
                depth_spec.astype(jnp.float32), local_x[0], local_x[1], "rxyc,xk->rkyc", 1.0
            ).astype(jnp.bfloat16),
            "gx",
            scatter_dimension=0,
            tiled=True,
        ).astype(jnp.float32)
        first_spectra = settle(first_spectra).reshape(share * KX, rows_y, 2 * channels)
        arrived_modes = lax.all_to_all(first_spectra, "gy", split_axis=0, concat_axis=1, tiled=True)
        return rotate(arrived_modes.astype(jnp.float32), whole_y[0], whole_y[1], "myc,yk->mkc", 1.0)

    def to_space(spectra, factor):
        back_rows = settle(rotate(spectra, whole_y[0], whole_y[1], "mkc,yk->myc", -1.0))
        returned = lax.all_to_all(back_rows, "gy", split_axis=1, concat_axis=0, tiled=True)
        share = returned.shape[0] // KX
        returned = returned.reshape(share, KX, rows_y, 2 * channels)
        back_depth = settle(
            rotate(
                lax.all_gather(returned, "gx", axis=0, tiled=True).astype(jnp.float32),
                local_x[0],
                local_x[1],
                "rkyc,xk->rxyc",
                -1.0,
            )
        )
        return depth_inverse(back_depth.astype(jnp.float32), depth_pair, factor)

    spectra_in = to_modes(inputs, 1.0 / math.sqrt(total_cells))
    mixed = mix_modes(spectra_in, weight_blocks)
    spectral_out = to_space(mixed, 1.0 / math.sqrt(kept_total))
    pointwise = jnp.einsum(
        "xycs,co->xyos", inputs, point_weight, preferred_element_type=jnp.float32
    )
    before = spectral_out + pointwise
    unused_out, pullback = jax.vjp(exact_gelu, before)
    slope = settle(pullback(cotangent.astype(jnp.float32))[0])
    spectra_back = to_modes(slope, 1.0 / math.sqrt(kept_total))
    grad_spectral = weight_grad(spectra_in, spectra_back).reshape(mode_rows, mode_cols, flat_width)
    adjoint = adjoint_modes(spectra_back, weight_blocks)
    spectral_grad = to_space(adjoint, 1.0 / math.sqrt(total_cells))
    pointwise_grad = jnp.einsum(
        "xyos,co->xycs", slope, point_weight, preferred_element_type=jnp.float32
    )
    grad_input = (pointwise_grad + spectral_grad).astype(jnp.bfloat16)
    return (grad_input, grad_spectral)


def solution(mesh):
    count_gx, count_gy = mesh.shape["gx"], mesh.shape["gy"]
    placed = (
        P("gx", "gy", None, None),
        P("gx", "gy", None, None),
        P(),
        P(("gx", "gy"), None, None),
    )

    def program(inputs, cotangent, point_weight, spectral_weight):
        cells = inputs.shape[0] * inputs.shape[1] // (count_gx * count_gy)
        whole_modes = KZ * KT % (count_gx * count_gy) == 0
        fits = whole_modes and KZ * KT // (count_gx * count_gy) == 3
        fits = fits and inputs.shape[2] == 32 and cells * inputs.shape[2] == 256 and inputs.shape[0] == inputs.shape[1] == LENGTH
        return jax.shard_map(
            per_device if fits else general_per_device,
            mesh=mesh,
            in_specs=placed,
            out_specs=(P("gx", "gy", None, None), P(("gx", "gy"), None, None)),
            check_vma=False,
        )(inputs, cotangent, point_weight, spectral_weight)

    return program
```

```python
import functools
import math

import jax
import jax.numpy as jnp
import numpy as np
from jax import lax
from jax.experimental import pallas as pl
from jax.experimental.pallas import tpu as pltpu
from jax.sharding import PartitionSpec as P

NZ = 64
NT = 8
KX = 24
KY = 24
KZ = 12
KT = 8
LANES = 128
LENGTH = 16
GROUP = 4
READ_AHEAD_FLOPS = 10**10
GRID_AXES = ("gx", "gy")


def table_angles(positions, kept_count, length):
    index = np.arange(kept_count)
    frequency = np.where(index < kept_count // 2, index, index - kept_count)
    turns = (np.asarray(positions)[:, None] * frequency[None, :]) % length
    return 2.0 * np.pi * turns / length


def depth_table(share):
    angles = (
        table_angles(np.arange(NZ), KZ, NZ)[:, None, :, None]
        + table_angles(np.arange(NT), KT, NT)[None, :, None, :]
    ).reshape(NZ * NT, KZ * KT)
    parts = np.stack([np.cos(angles), -np.sin(angles)], -1)
    owners = KZ * KT // share
    rows = parts.reshape(NZ * NT, owners, 2 * share).transpose(2, 1, 0)
    return rows.reshape(2 * share * owners, NZ * NT).astype(jnp.bfloat16)


def plane_tables(count_gx, count_gy, rows_x, rows_y):
    length_x, length_y = count_gx * rows_x, count_gy * rows_y
    turns_x = np.outer(np.arange(length_x), np.arange(length_x)) % length_x / length_x
    turns_y = np.outer(np.arange(length_y), np.arange(length_y)) % length_y / length_y
    turns_x = turns_x.reshape(length_x, 1, count_gx, 1, rows_x, 1)
    turns_y = turns_y.reshape(1, length_y, 1, count_gy, 1, rows_y)
    turns = (turns_x + turns_y).transpose(0, 1, 4, 5, 2, 3).reshape(length_x * length_y, length_x * length_y)
    cosine, sine = np.cos(2.0 * np.pi * turns), np.sin(2.0 * np.pi * turns)
    forward = np.concatenate([cosine.T, sine.T], 0)
    inverse = np.concatenate([cosine.T, sine.T], 1)
    return forward.astype(jnp.bfloat16), inverse.astype(jnp.bfloat16)


def residue_of(mode):
    return (mode if mode < KX // 2 else mode - KX) % LENGTH


def modes_of(residue):
    return [mode for mode in range(KX) if residue_of(mode) == residue]


def dot(left, right, left_dim=1, right_dim=0):
    return lax.dot_general(
        left, right, (((left_dim,), (right_dim,)), ((), ())), preferred_element_type=jnp.float32
    )


def unit_rows(unit, wide_ref, units):
    return pl.ds(unit, wide_ref.shape[0] // units, stride=units)


def send_slots(spectra, units, wide_ref, sent_ref):
    devices = wide_ref.shape[0] // units
    halves = spectra.shape[1] // LANES
    for unit in range(units):
        slot, h = divmod(unit, halves)
        wide_ref[unit_rows(unit, wide_ref, units), :] = spectra[
            slot * devices : (slot + 1) * devices, h * LANES : (h + 1) * LANES
        ]
    sent_ref[...] = wide_ref[...].astype(jnp.bfloat16)


def received_slots(arrived_ref, halves, units, wide_ref):
    wide_ref[...] = arrived_ref[...].astype(jnp.float32)
    slots = []
    for slot in range(units // halves):
        pieces = [wide_ref[unit_rows(slot * halves + h, wide_ref, units), :] for h in range(halves)]
        slots.append(jnp.concatenate(pieces, 1))
    return jnp.concatenate(slots, 0)


def depth_kernel(factor, units, table_ref, field_ref, sent_ref, wide_ref):
    spectra = dot(table_ref[...], field_ref[...], 1, 1)
    send_slots(spectra * factor, units, wide_ref, sent_ref)


def to_plane_modes(share, channels, halves, arrived_ref, forward_ref, wide_ref, modes_ref):
    slots = received_slots(arrived_ref, halves, 2 * share * halves, wide_ref)
    devices = wide_ref.shape[0] // (2 * share * halves)
    lanes = slots.shape[1]
    turned = slots.astype(jnp.bfloat16).T
    blocks = []
    for slot in range(2 * share):
        pieces = [
            turned[c * channels : (c + 1) * channels, slot * devices : (slot + 1) * devices]
            for c in range(lanes // channels)
        ]
        blocks.append(jnp.concatenate(pieces, 1))
    rows = []
    for k in range(share):
        real, imag = blocks[2 * k], blocks[2 * k + 1]
        rows += [jnp.concatenate([real, imag], 1), jnp.concatenate([imag, -real], 1)]
    modes = dot(jnp.concatenate(rows, 0), forward_ref[...])
    each = modes_ref.shape[0] // share
    for k in range(share):
        for j in range(each):
            modes_ref[k * each + j] = modes[2 * k * channels : (2 * k + 2) * channels, j * LANES : (j + 1) * LANES]


def store_pair(tile, channels, real, imag, pair_ref):
    pair_ref[tile, :channels, :LANES] = real.astype(jnp.bfloat16)
    pair_ref[tile, channels:, :LANES] = imag.astype(jnp.bfloat16)
    pair_ref[tile, :channels, LANES:] = (-imag).astype(jnp.bfloat16)
    pair_ref[tile, channels:, LANES:] = real.astype(jnp.bfloat16)


def to_cells(k, share, channels, halves, pair_ref, inverse_ref, out_ref):
    units = 2 * share * halves
    devices = out_ref.shape[0] // units
    each = pair_ref.shape[0] // share
    cosine = jnp.concatenate([pair_ref[k * each + j, :, :LANES] for j in range(each)], 1)
    sine = jnp.concatenate([pair_ref[k * each + j, :, LANES:] for j in range(each)], 1)
    total = dot(inverse_ref[...], jnp.concatenate([cosine, sine], 1), 1, 1)
    per_half = LANES // channels
    for part in range(2):
        columns = slice(part * channels, (part + 1) * channels)
        for h in range(halves):
            pieces = [total[c * devices : (c + 1) * devices, columns] for c in range(h * per_half, (h + 1) * per_half)]
            unit = (2 * k + part) * halves + h
            out_ref[unit_rows(unit, out_ref, units), :] = jnp.concatenate(pieces, 1)


def fold_rows(weight_ref, mode, first, count, columns):
    row = lax.broadcasted_iota(jnp.int32, (8, LANES), 0)
    folded = []
    for residue in range(first, first + count):
        total = None
        for kx in modes_of(residue):
            rows = pl.ds(pl.multiple_of((mode * KX + kx) * KY, 8), KY)
            block = weight_ref[rows, columns]
            total = block if total is None else total + block
        folded += [total[:8] + jnp.where(row < 4, jnp.bfloat16(0), total[8:16]), total[16:] + jnp.where(row < 4, total[8:16], jnp.bfloat16(0))]
    return jnp.concatenate(folded, 0)


def mix_kernel(
    share, channels, halves, arrived_ref, weight_ref, forward_ref, inverse_ref, sent_ref, modes_ref, turned_ref,
    wide_ref, out_ref, pair_ref,
):
    to_plane_modes(share, channels, halves, arrived_ref, forward_ref, wide_ref, modes_ref)
    wide = 2 * channels
    each = modes_ref.shape[0] // share
    per_tile = LANES // LENGTH

    for k in range(share):
        for j in range(each):
            tile = k * each + j
            by_real = jnp.zeros((wide, LANES), jnp.float32)
            by_imag = jnp.zeros((wide, LANES), jnp.float32)
            for first in range(0, channels, GROUP):
                real_sum, imag_sum = None, None
                for c in range(first, first + GROUP, LANES // wide):
                    columns = slice(c * wide, c * wide + LANES)
                    block = fold_rows(weight_ref, k, j * per_tile, per_tile, columns).T
                    turned_ref[tile, columns, :] = block
                    for h in range(LANES // wide):
                        weight = block[h * wide : (h + 1) * wide]
                        real = jnp.broadcast_to(modes_ref[tile, c + h : c + h + 1, :], (wide, LANES))
                        imag = jnp.broadcast_to(
                            modes_ref[tile, channels + c + h : channels + c + h + 1, :], (wide, LANES)
                        )
                        real, imag = real.astype(jnp.bfloat16) * weight, imag.astype(jnp.bfloat16) * weight
                        real_sum = real if real_sum is None else real_sum + real
                        imag_sum = imag if imag_sum is None else imag_sum + imag
                by_real += real_sum.astype(jnp.float32)
                by_imag += imag_sum.astype(jnp.float32)
            store_pair(
                tile, channels, by_real[:channels] - by_imag[channels:],
                by_real[channels:] + by_imag[:channels], pair_ref,
            )
        to_cells(k, share, channels, halves, pair_ref, inverse_ref, out_ref)

    sent_ref[...] = out_ref[...].astype(jnp.bfloat16)


def row_sums(blocks):
    row = lax.broadcasted_iota(jnp.int32, (8, LANES), 0)
    for shift in (4, 2, 1):
        merged = []
        clear = row % (2 * shift) < shift
        for i in range(shift):
            first, second = blocks[i], blocks[i + shift]
            merged.append(
                jnp.where(clear, first + pltpu.roll(first, 8 - shift, 0), second + pltpu.roll(second, shift, 0))
            )
        blocks = merged
    return blocks[0]


def adjoint_kernel(
    share, channels, halves, arrived_ref, turned_ref, forward_ref, inverse_ref, sent_ref, modes_ref, wide_ref,
    out_ref, pair_ref,
):
    to_plane_modes(share, channels, halves, arrived_ref, forward_ref, wide_ref, modes_ref)
    wide = 2 * channels
    each = modes_ref.shape[0] // share

    for tile in range(modes_ref.shape[0]):
        real, imag = modes_ref[tile, :channels, :], modes_ref[tile, channels:, :]
        here = jnp.concatenate([real, imag], 0).astype(jnp.bfloat16)
        turn = jnp.concatenate([imag, -real], 0).astype(jnp.bfloat16)
        sums = ([], [])
        for first in range(0, channels, 8):
            blocks = ([], [])
            for c in range(first, first + 8):
                weight = turned_ref[tile, c * wide : (c + 1) * wide, :]
                for part, factor in enumerate((here, turn)):
                    product = factor * weight
                    product = product[: wide // 2] + product[wide // 2 :]
                    product = (product[: wide // 4] + product[wide // 4 :]).astype(jnp.float32)
                    blocks[part].append(product[:8] + product[8:])
            for part in range(2):
                sums[part].append(row_sums(blocks[part]))
        store_pair(tile, channels, jnp.concatenate(sums[0], 0), jnp.concatenate(sums[1], 0), pair_ref)
        if (tile + 1) % each == 0:
            to_cells(tile // each, share, channels, halves, pair_ref, inverse_ref, out_ref)

    sent_ref[...] = out_ref[...].astype(jnp.bfloat16)


def outer_kernel(share, channels, in_ref, back_ref, slope_ref, point_ref, grad_ref, pointwise_ref, held_ref, sems):
    wide = 2 * channels
    each = in_ref.shape[0] // share
    per_block = LANES // wide
    per_tile = LANES // LENGTH

    def runs(j):
        inside = [kx for kx in range(KX) if residue_of(kx) // per_tile == j]
        found = []
        for kx in inside:
            if found and found[-1][0] + found[-1][2] == kx and found[-1][1] + found[-1][2] == residue_of(kx):
                found[-1][2] += 1
            else:
                found.append([kx, residue_of(kx), 1])
        return found

    def copies(k, j):
        made = []
        for place, (mode, residue, count) in enumerate(runs(j)):
            source = pl.ds(pl.multiple_of((k * LENGTH + residue) * KY, 8), count * KY)
            target = pl.ds(pl.multiple_of((k * KX + mode) * KY, 8), count * KY)
            made.append(
                pltpu.make_async_copy(held_ref.at[source], grad_ref.at[target], sems.at[k * each + j, place])
            )
        return made

    low = lax.broadcasted_iota(jnp.int32, (8, LANES), 0) < 4

    @pl.loop(0, share)
    def _(k):
        for j in range(each):
            tile = k * each + j
            real, imag = back_ref[tile, :channels, :], back_ref[tile, channels:, :]
            here = jnp.concatenate([real, imag], 0)
            turn = jnp.concatenate([imag, -real], 0)
            for c in range(0, channels, per_block):
                parts = [
                    in_ref[tile, c + h : c + h + 1, :] * here
                    + in_ref[tile, channels + c + h : channels + c + h + 1, :] * turn
                    for h in range(per_block)
                ]
                block = jnp.concatenate(parts, 0).T
                for i in range(per_tile):
                    first = block[i * LENGTH : i * LENGTH + 8]
                    second = block[i * LENGTH + 8 : (i + 1) * LENGTH]
                    rows = pl.ds(pl.multiple_of((k * LENGTH + j * per_tile + i) * KY, 8), KY)
                    held_ref[rows, c * wide : c * wide + LANES] = jnp.concatenate(
                        [first, jnp.where(low, second, first), second], 0
                    )
            for copy in copies(k, j):
                copy.start()

    for first in range(0, slope_ref.shape[0], channels):
        rows = slice(first, first + channels)
        pointwise_ref[rows, :] = dot(point_ref[...], slope_ref[rows, :])

    @pl.loop(0, share)
    def _(k):
        for j in range(each):
            for copy in copies(k, j):
                copy.wait()


def slope_kernel(
    cells, channels, factor, units, arrived_ref, table_ref, field_ref, cotangent_ref, point_ref, slope_ref, sent_ref,
    wide_ref,
):
    arrived = received_slots(arrived_ref, cells * channels // LANES, units, wide_ref)
    spectral = dot(arrived.astype(jnp.bfloat16), table_ref[...], 0, 0)
    for c in range(cells):
        rows = slice(c * channels, (c + 1) * channels)
        before = spectral[rows] * factor + dot(point_ref[...], field_ref[rows, :], 0, 0)
        cumulative = 0.5 + 0.5 * lax.erf(before * math.sqrt(0.5))
        density = jnp.exp(-0.5 * before * before) * (1.0 / math.sqrt(2.0 * math.pi))
        slope = cotangent_ref[rows, :].astype(jnp.float32) * (cumulative + before * density)
        slope_ref[rows, :] = slope.astype(jnp.bfloat16)
    sent = dot(table_ref[...], slope_ref[...], 1, 1)
    send_slots(sent * factor, units, wide_ref, sent_ref)


def final_kernel(factor, halves, units, arrived_ref, table_ref, pointwise_ref, grad_ref, wide_ref):
    arrived = received_slots(arrived_ref, halves, units, wide_ref)
    spectral = dot(arrived.astype(jnp.bfloat16), table_ref[...], 0, 0)
    grad_ref[...] = (pointwise_ref[...] + spectral * factor).astype(jnp.bfloat16)


def params(mebibytes, semantics=None):
    return pltpu.CompilerParams(dimension_semantics=semantics, vmem_limit_bytes=mebibytes * 1024 * 1024)


def on_chip(value):
    return pltpu.with_memory_space_constraint(value, pltpu.VMEM)


def off_chip(value):
    return pltpu.with_memory_space_constraint(value, pltpu.HBM)


IN_VMEM = pl.BlockSpec(memory_space=pltpu.VMEM)


def per_device(inputs, cotangent, point_weight, spectral_weight):
    rows_x, rows_y, channels, depth = inputs.shape
    mode_rows, mode_cols, flat = spectral_weight.shape
    count_gx, count_gy = lax.axis_size("gx"), lax.axis_size("gy")
    devices = count_gx * count_gy
    share = mode_rows // KX
    cells = rows_x * rows_y
    lanes = cells * channels
    wide = 2 * channels
    plane = KX * KY
    points = cells * devices
    each = points // LANES
    tiles = share * each
    halves = lanes // LANES
    units = 2 * share * halves
    inner = 1.0 / math.sqrt(points * depth)
    outer = 1.0 / math.sqrt(plane * KZ * KT)

    table = on_chip(jnp.asarray(depth_table(share)))
    forward, inverse = (on_chip(jnp.asarray(t)) for t in plane_tables(count_gx, count_gy, rows_x, rows_y))
    field = on_chip(inputs.reshape(lanes, depth))
    seed = on_chip(cotangent.reshape(lanes, depth))
    point = on_chip(point_weight)

    def exchange(sent):
        blocks = sent.reshape(devices * units // 4, 4, LANES)
        arrived = lax.all_to_all(blocks, GRID_AXES, split_axis=0, concat_axis=0, tiled=True)
        return on_chip(arrived.reshape(devices * units, LANES))

    packet = pltpu.VMEM((devices * units, LANES), jnp.bfloat16)
    unpacked = pltpu.VMEM((devices * units, LANES), jnp.float32)
    spectra = pltpu.VMEM((tiles, wide, LANES), jnp.float32)

    sent = pl.pallas_call(
        functools.partial(depth_kernel, inner, units),
        in_specs=[IN_VMEM] * 2, out_specs=IN_VMEM, out_shape=packet, scratch_shapes=[unpacked],
        compiler_params=params(2),
        cost_estimate=pl.CostEstimate(flops=READ_AHEAD_FLOPS, transcendentals=0, bytes_accessed=0),
        name="depth",
    )(off_chip(jnp.asarray(depth_table(share))), off_chip(inputs.reshape(lanes, depth)))
    arrived = exchange(sent)
    scratch = [unpacked, unpacked, pltpu.VMEM((tiles, wide, 2 * LANES), jnp.bfloat16)]
    sent, modes_in, turned = pl.pallas_call(
        functools.partial(mix_kernel, share, channels, halves),
        in_specs=[IN_VMEM] * 4, out_specs=[IN_VMEM] * 3,
        out_shape=[packet, spectra, pltpu.VMEM((tiles, flat, LANES), jnp.bfloat16)],
        scratch_shapes=scratch, compiler_params=params(6), name="mix",
    )(arrived, on_chip(spectral_weight.reshape(share * plane, flat)), forward, inverse)
    arrived = exchange(sent)
    slope, sent = pl.pallas_call(
        functools.partial(slope_kernel, cells, channels, outer, units),
        in_specs=[IN_VMEM] * 5, out_specs=[IN_VMEM] * 2, out_shape=[pltpu.VMEM((lanes, depth), jnp.bfloat16), packet],
        scratch_shapes=[unpacked],
        compiler_params=params(8), name="slope",
    )(arrived, table, field, seed, point)
    arrived = exchange(sent)
    sent, modes_back = pl.pallas_call(
        functools.partial(adjoint_kernel, share, channels, halves),
        in_specs=[IN_VMEM] * 4, out_specs=[IN_VMEM] * 2, out_shape=[packet, spectra],
        scratch_shapes=scratch,
        compiler_params=params(12), name="adjoint",
    )(arrived, on_chip(turned), forward, inverse)
    arrived = exchange(sent)
    grad_spectral, pointwise = pl.pallas_call(
        functools.partial(outer_kernel, share, channels),
        in_specs=[IN_VMEM] * 4, out_specs=[pl.BlockSpec(memory_space=pl.ANY), IN_VMEM],
        out_shape=[
            jax.ShapeDtypeStruct((share * plane, flat), jnp.float32), pltpu.VMEM((lanes, depth), jnp.float32),
        ],
        scratch_shapes=[
            pltpu.VMEM((share * LENGTH * KY, flat), jnp.float32), pltpu.SemaphoreType.DMA((tiles, 2)),
        ],
        compiler_params=params(24),
        cost_estimate=pl.CostEstimate(
            flops=4 * share * plane * flat * wide, transcendentals=0, bytes_accessed=4 * share * plane * flat
        ),
        name="outer",
    )(on_chip(modes_in), on_chip(modes_back), on_chip(slope), point)
    grad_input = pl.pallas_call(
        functools.partial(final_kernel, inner, halves, units),
        in_specs=[IN_VMEM] * 3, out_specs=IN_VMEM, out_shape=jax.ShapeDtypeStruct((lanes, depth), jnp.bfloat16),
        scratch_shapes=[unpacked],
        compiler_params=params(8), name="final",
    )(arrived, table, on_chip(pointwise))
    return grad_input.reshape(inputs.shape), grad_spectral.reshape(spectral_weight.shape)


def kept_angles(positions, kept_count, length):
    index = jnp.arange(kept_count, dtype=jnp.int32)
    frequency = jnp.where(index < kept_count // 2, index, index - kept_count)
    turns = positions[:, None] * frequency[None, :] % length
    return turns.astype(jnp.float32) * (2.0 * math.pi / length)


def axis_tables(positions, kept_count, length):
    angles = kept_angles(positions, kept_count, length)
    return (jnp.cos(angles), jnp.sin(angles))


def depth_tables():
    angle_depth = kept_angles(jnp.arange(NZ, dtype=jnp.int32), KZ, NZ)
    angle_time = kept_angles(jnp.arange(NT, dtype=jnp.int32), KT, NT)
    angles = (angle_depth[:, None, :, None] + angle_time[None, :, None, :]).reshape(
        NZ * NT, KZ * KT
    )
    return (jnp.cos(angles), jnp.sin(angles))


def settle(values):
    return lax.optimization_barrier(values.astype(jnp.bfloat16))


def rotate(spectra, cosine_table, sine_table, pattern, turn_sign):
    half_width = spectra.shape[-1] // 2
    with_cosine = jnp.einsum(pattern, spectra, cosine_table, precision=lax.Precision.HIGHEST)
    with_sine = jnp.einsum(pattern, spectra, sine_table, precision=lax.Precision.HIGHEST)
    real_part = with_cosine[..., :half_width] + turn_sign * with_sine[..., half_width:]
    imag_part = with_cosine[..., half_width:] - turn_sign * with_sine[..., :half_width]
    return jnp.concatenate([real_part, imag_part], -1)


def depth_forward(field_in, tables, factor):
    widened = field_in.astype(jnp.float32)
    with_cosine = jnp.einsum("xycs,sk->kxyc", widened, tables[0], precision=lax.Precision.HIGHEST)
    with_sine = jnp.einsum("xycs,sk->kxyc", widened, tables[1], precision=lax.Precision.HIGHEST)
    return jnp.concatenate([with_cosine, -with_sine], -1) * factor


def depth_inverse(spectra, tables, factor):
    half_width = spectra.shape[-1] // 2
    with_cosine = jnp.einsum(
        "kxyc,sk->xycs", spectra[..., :half_width], tables[0], precision=lax.Precision.HIGHEST
    )
    with_sine = jnp.einsum(
        "kxyc,sk->xycs", spectra[..., half_width:], tables[1], precision=lax.Precision.HIGHEST
    )
    return (with_cosine - with_sine) * factor


def contract_in(left, right):
    return jnp.einsum("mkc,mkco->mko", left, right, precision=lax.Precision.HIGHEST)


def contract_out(left, right):
    return jnp.einsum("mko,mkco->mkc", left, right, precision=lax.Precision.HIGHEST)


def partial_outer(left, right):
    return jnp.einsum("mkc,mko->mkco", left, right, precision=lax.Precision.HIGHEST)


def mix_modes(spectra, weight):
    half_width = spectra.shape[-1] // 2
    weight_wide = weight.astype(jnp.float32)
    weight_real, weight_imag = (weight_wide[..., :half_width], weight_wide[..., half_width:])
    real_in, imag_in = (spectra[..., :half_width], spectra[..., half_width:])
    real_out = contract_in(real_in, weight_real) - contract_in(imag_in, weight_imag)
    imag_out = contract_in(real_in, weight_imag) + contract_in(imag_in, weight_real)
    return jnp.concatenate([real_out, imag_out], -1)


def adjoint_modes(spectra, weight):
    half_width = spectra.shape[-1] // 2
    weight_wide = weight.astype(jnp.float32)
    weight_real, weight_imag = (weight_wide[..., :half_width], weight_wide[..., half_width:])
    real_in, imag_in = (spectra[..., :half_width], spectra[..., half_width:])
    real_out = contract_out(real_in, weight_real) + contract_out(imag_in, weight_imag)
    imag_out = contract_out(imag_in, weight_real) - contract_out(real_in, weight_imag)
    return jnp.concatenate([real_out, imag_out], -1)


def weight_grad(spectra_in, spectra_back):
    half_width = spectra_in.shape[-1] // 2
    real_in, imag_in = (spectra_in[..., :half_width], spectra_in[..., half_width:])
    real_back, imag_back = (spectra_back[..., :half_width], spectra_back[..., half_width:])
    real_part = partial_outer(real_in, real_back) + partial_outer(imag_in, imag_back)
    imag_part = partial_outer(real_in, imag_back) - partial_outer(imag_in, real_back)
    return jnp.concatenate([real_part, imag_part], -1)


def exact_gelu(values):
    return jax.nn.gelu(values, approximate=False)


def general_per_device(inputs, cotangent, point_weight, spectral_weight):
    rows_x, rows_y, channels, cells = inputs.shape
    mode_rows, mode_cols, flat_width = spectral_weight.shape
    weight_blocks = spectral_weight.reshape(mode_rows, mode_cols, channels, 2 * channels)
    count_gx = lax.axis_size("gx")
    count_gy = lax.axis_size("gy")
    length_x = rows_x * count_gx
    length_y = rows_y * count_gy
    depth_pair = depth_tables()
    own_x = lax.axis_index("gx") * rows_x + jnp.arange(rows_x, dtype=jnp.int32)
    local_x = axis_tables(own_x, KX, length_x)
    whole_y = axis_tables(jnp.arange(length_y, dtype=jnp.int32), KY, length_y)
    total_cells = length_x * length_y * cells
    kept_total = KX * KY * KZ * KT

    def to_modes(field_in, factor):
        depth_spec = settle(depth_forward(field_in, depth_pair, factor))
        share = depth_spec.shape[0] // count_gx
        first_spectra = lax.psum_scatter(
            rotate(
                depth_spec.astype(jnp.float32), local_x[0], local_x[1], "rxyc,xk->rkyc", 1.0
            ).astype(jnp.bfloat16),
            "gx",
            scatter_dimension=0,
            tiled=True,
        ).astype(jnp.float32)
        first_spectra = settle(first_spectra).reshape(share * KX, rows_y, 2 * channels)
        arrived_modes = lax.all_to_all(first_spectra, "gy", split_axis=0, concat_axis=1, tiled=True)
        return rotate(arrived_modes.astype(jnp.float32), whole_y[0], whole_y[1], "myc,yk->mkc", 1.0)

    def to_space(spectra, factor):
        back_rows = settle(rotate(spectra, whole_y[0], whole_y[1], "mkc,yk->myc", -1.0))
        returned = lax.all_to_all(back_rows, "gy", split_axis=1, concat_axis=0, tiled=True)
        share = returned.shape[0] // KX
        returned = returned.reshape(share, KX, rows_y, 2 * channels)
        back_depth = settle(
            rotate(
                lax.all_gather(returned, "gx", axis=0, tiled=True).astype(jnp.float32),
                local_x[0],
                local_x[1],
                "rkyc,xk->rxyc",
                -1.0,
            )
        )
        return depth_inverse(back_depth.astype(jnp.float32), depth_pair, factor)

    spectra_in = to_modes(inputs, 1.0 / math.sqrt(total_cells))
    mixed = mix_modes(spectra_in, weight_blocks)
    spectral_out = to_space(mixed, 1.0 / math.sqrt(kept_total))
    pointwise = jnp.einsum(
        "xycs,co->xyos", inputs, point_weight, preferred_element_type=jnp.float32
    )
    before = spectral_out + pointwise
    unused_out, pullback = jax.vjp(exact_gelu, before)
    slope = settle(pullback(cotangent.astype(jnp.float32))[0])
    spectra_back = to_modes(slope, 1.0 / math.sqrt(kept_total))
    grad_spectral = weight_grad(spectra_in, spectra_back).reshape(mode_rows, mode_cols, flat_width)
    adjoint = adjoint_modes(spectra_back, weight_blocks)
    spectral_grad = to_space(adjoint, 1.0 / math.sqrt(total_cells))
    pointwise_grad = jnp.einsum(
        "xyos,co->xycs", slope, point_weight, preferred_element_type=jnp.float32
    )
    grad_input = (pointwise_grad + spectral_grad).astype(jnp.bfloat16)
    return (grad_input, grad_spectral)


def solution(mesh):
    count_gx, count_gy = mesh.shape["gx"], mesh.shape["gy"]
    placed = (
        P("gx", "gy", None, None),
        P("gx", "gy", None, None),
        P(),
        P(("gx", "gy"), None, None),
    )

    def program(inputs, cotangent, point_weight, spectral_weight):
        cells = inputs.shape[0] * inputs.shape[1] // (count_gx * count_gy)
        whole_modes = KZ * KT % (count_gx * count_gy) == 0
        fits = whole_modes and KZ * KT // (count_gx * count_gy) == 3
        fits = fits and inputs.shape[2] == 32 and cells * inputs.shape[2] == 256 and inputs.shape[0] == inputs.shape[1] == LENGTH
        return jax.shard_map(
            per_device if fits else general_per_device,
            mesh=mesh,
            in_specs=placed,
            out_specs=(P("gx", "gy", None, None), P(("gx", "gy"), None, None)),
            check_vma=False,
        )(inputs, cotangent, point_weight, spectral_weight)

    return program
```

```python
import functools
import math

import jax
import jax.numpy as jnp
import numpy as np
from jax import lax
from jax.experimental import pallas as pl
from jax.experimental.pallas import tpu as pltpu
from jax.sharding import PartitionSpec as P

NZ = 64
NT = 8
KX = 24
KY = 24
KZ = 12
KT = 8
LANES = 128
LENGTH = 16
GROUP = 8
READ_AHEAD_FLOPS = 10**10
GRID_AXES = ("gx", "gy")


def table_angles(positions, kept_count, length):
    index = np.arange(kept_count)
    frequency = np.where(index < kept_count // 2, index, index - kept_count)
    turns = (np.asarray(positions)[:, None] * frequency[None, :]) % length
    return 2.0 * np.pi * turns / length


def depth_table(share):
    angles = (
        table_angles(np.arange(NZ), KZ, NZ)[:, None, :, None]
        + table_angles(np.arange(NT), KT, NT)[None, :, None, :]
    ).reshape(NZ * NT, KZ * KT)
    parts = np.stack([np.cos(angles), -np.sin(angles)], -1)
    owners = KZ * KT // share
    rows = parts.reshape(NZ * NT, owners, 2 * share).transpose(2, 1, 0)
    return rows.reshape(2 * share * owners, NZ * NT).astype(jnp.bfloat16)


def plane_tables(count_gx, count_gy, rows_x, rows_y):
    length_x, length_y = count_gx * rows_x, count_gy * rows_y
    turns_x = np.outer(np.arange(length_x), np.arange(length_x)) % length_x / length_x
    turns_y = np.outer(np.arange(length_y), np.arange(length_y)) % length_y / length_y
    turns_x = turns_x.reshape(length_x, 1, count_gx, 1, rows_x, 1)
    turns_y = turns_y.reshape(1, length_y, 1, count_gy, 1, rows_y)
    turns = (turns_x + turns_y).transpose(0, 1, 4, 5, 2, 3).reshape(length_x * length_y, length_x * length_y)
    cosine, sine = np.cos(2.0 * np.pi * turns), np.sin(2.0 * np.pi * turns)
    forward = np.concatenate([cosine.T, sine.T], 0)
    inverse = np.concatenate([cosine.T, sine.T], 1)
    return forward.astype(jnp.bfloat16), inverse.astype(jnp.bfloat16)


def residue_of(mode):
    return (mode if mode < KX // 2 else mode - KX) % LENGTH


def modes_of(residue):
    return [mode for mode in range(KX) if residue_of(mode) == residue]


def dot(left, right, left_dim=1, right_dim=0):
    return lax.dot_general(
        left, right, (((left_dim,), (right_dim,)), ((), ())), preferred_element_type=jnp.float32
    )


def unit_rows(unit, wide_ref, units):
    return pl.ds(unit, wide_ref.shape[0] // units, stride=units)


def send_slots(spectra, units, wide_ref, sent_ref):
    devices = wide_ref.shape[0] // units
    halves = spectra.shape[1] // LANES
    for unit in range(units):
        slot, h = divmod(unit, halves)
        wide_ref[unit_rows(unit, wide_ref, units), :] = spectra[
            slot * devices : (slot + 1) * devices, h * LANES : (h + 1) * LANES
        ]
    sent_ref[...] = wide_ref[...].astype(jnp.bfloat16)


def received_slots(arrived_ref, halves, units, wide_ref):
    wide_ref[...] = arrived_ref[...].astype(jnp.float32)
    slots = []
    for slot in range(units // halves):
        pieces = [wide_ref[unit_rows(slot * halves + h, wide_ref, units), :] for h in range(halves)]
        slots.append(jnp.concatenate(pieces, 1))
    return jnp.concatenate(slots, 0)


def depth_kernel(factor, units, table_ref, field_ref, sent_ref, wide_ref):
    spectra = dot(table_ref[...], field_ref[...], 1, 1)
    send_slots(spectra * factor, units, wide_ref, sent_ref)


def to_plane_modes(share, channels, halves, arrived_ref, forward_ref, wide_ref, modes_ref):
    slots = received_slots(arrived_ref, halves, 2 * share * halves, wide_ref)
    devices = wide_ref.shape[0] // (2 * share * halves)
    lanes = slots.shape[1]
    turned = slots.astype(jnp.bfloat16).T
    blocks = []
    for slot in range(2 * share):
        pieces = [
            turned[c * channels : (c + 1) * channels, slot * devices : (slot + 1) * devices]
            for c in range(lanes // channels)
        ]
        blocks.append(jnp.concatenate(pieces, 1))
    rows = []
    for k in range(share):
        real, imag = blocks[2 * k], blocks[2 * k + 1]
        rows += [jnp.concatenate([real, imag], 1), jnp.concatenate([imag, -real], 1)]
    modes = dot(jnp.concatenate(rows, 0), forward_ref[...])
    each = modes_ref.shape[0] // share
    for k in range(share):
        for j in range(each):
            modes_ref[k * each + j] = modes[2 * k * channels : (2 * k + 2) * channels, j * LANES : (j + 1) * LANES]


def store_pair(tile, channels, real, imag, pair_ref):
    pair_ref[tile, :channels, :LANES] = real.astype(jnp.bfloat16)
    pair_ref[tile, channels:, :LANES] = imag.astype(jnp.bfloat16)
    pair_ref[tile, :channels, LANES:] = (-imag).astype(jnp.bfloat16)
    pair_ref[tile, channels:, LANES:] = real.astype(jnp.bfloat16)


def to_cells(k, share, channels, halves, pair_ref, inverse_ref, out_ref):
    units = 2 * share * halves
    devices = out_ref.shape[0] // units
    each = pair_ref.shape[0] // share
    cosine = jnp.concatenate([pair_ref[k * each + j, :, :LANES] for j in range(each)], 1)
    sine = jnp.concatenate([pair_ref[k * each + j, :, LANES:] for j in range(each)], 1)
    total = dot(inverse_ref[...], jnp.concatenate([cosine, sine], 1), 1, 1)
    per_half = LANES // channels
    for part in range(2):
        columns = slice(part * channels, (part + 1) * channels)
        for h in range(halves):
            pieces = [total[c * devices : (c + 1) * devices, columns] for c in range(h * per_half, (h + 1) * per_half)]
            unit = (2 * k + part) * halves + h
            out_ref[unit_rows(unit, out_ref, units), :] = jnp.concatenate(pieces, 1)


def fold_rows(weight_ref, mode, first, count, columns):
    row = lax.broadcasted_iota(jnp.int32, (8, LANES), 0)
    folded = []
    for residue in range(first, first + count):
        total = None
        for kx in modes_of(residue):
            rows = pl.ds(pl.multiple_of((mode * KX + kx) * KY, 8), KY)
            block = weight_ref[rows, columns]
            total = block if total is None else total + block
        folded += [total[:8] + jnp.where(row < 4, jnp.bfloat16(0), total[8:16]), total[16:] + jnp.where(row < 4, total[8:16], jnp.bfloat16(0))]
    return jnp.concatenate(folded, 0)


def mix_kernel(
    share, channels, halves, arrived_ref, weight_ref, forward_ref, inverse_ref, sent_ref, modes_ref, turned_ref,
    wide_ref, out_ref, pair_ref,
):
    to_plane_modes(share, channels, halves, arrived_ref, forward_ref, wide_ref, modes_ref)
    wide = 2 * channels
    each = modes_ref.shape[0] // share
    per_tile = LANES // LENGTH

    for k in range(share):
        for j in range(each):
            tile = k * each + j
            by_real = jnp.zeros((wide, LANES), jnp.float32)
            by_imag = jnp.zeros((wide, LANES), jnp.float32)
            for first in range(0, channels, GROUP):
                real_sum, imag_sum = None, None
                for c in range(first, first + GROUP, LANES // wide):
                    columns = slice(c * wide, c * wide + LANES)
                    block = fold_rows(weight_ref, k, j * per_tile, per_tile, columns).T
                    turned_ref[tile, columns, :] = block
                    for h in range(LANES // wide):
                        weight = block[h * wide : (h + 1) * wide]
                        real = jnp.broadcast_to(modes_ref[tile, c + h : c + h + 1, :], (wide, LANES))
                        imag = jnp.broadcast_to(
                            modes_ref[tile, channels + c + h : channels + c + h + 1, :], (wide, LANES)
                        )
                        real, imag = real.astype(jnp.bfloat16) * weight, imag.astype(jnp.bfloat16) * weight
                        real_sum = real if real_sum is None else real_sum + real
                        imag_sum = imag if imag_sum is None else imag_sum + imag
                by_real += real_sum.astype(jnp.float32)
                by_imag += imag_sum.astype(jnp.float32)
            store_pair(
                tile, channels, by_real[:channels] - by_imag[channels:],
                by_real[channels:] + by_imag[:channels], pair_ref,
            )
        to_cells(k, share, channels, halves, pair_ref, inverse_ref, out_ref)

    sent_ref[...] = out_ref[...].astype(jnp.bfloat16)


def row_sums(blocks):
    row = lax.broadcasted_iota(jnp.int32, (8, LANES), 0)
    for shift in (4, 2, 1):
        merged = []
        clear = row % (2 * shift) < shift
        for i in range(shift):
            first, second = blocks[i], blocks[i + shift]
            merged.append(
                jnp.where(clear, first + pltpu.roll(first, 8 - shift, 0), second + pltpu.roll(second, shift, 0))
            )
        blocks = merged
    return blocks[0]


def adjoint_kernel(
    share, channels, halves, arrived_ref, turned_ref, forward_ref, inverse_ref, sent_ref, modes_ref, wide_ref,
    out_ref, pair_ref,
):
    to_plane_modes(share, channels, halves, arrived_ref, forward_ref, wide_ref, modes_ref)
    wide = 2 * channels
    each = modes_ref.shape[0] // share

    for tile in range(modes_ref.shape[0]):
        real, imag = modes_ref[tile, :channels, :], modes_ref[tile, channels:, :]
        here = jnp.concatenate([real, imag], 0).astype(jnp.bfloat16)
        turn = jnp.concatenate([imag, -real], 0).astype(jnp.bfloat16)
        sums = ([], [])
        for first in range(0, channels, 8):
            blocks = ([], [])
            for c in range(first, first + 8):
                weight = turned_ref[tile, c * wide : (c + 1) * wide, :]
                for part, factor in enumerate((here, turn)):
                    product = factor * weight
                    product = product[: wide // 2] + product[wide // 2 :]
                    product = (product[: wide // 4] + product[wide // 4 :]).astype(jnp.float32)
                    blocks[part].append(product[:8] + product[8:])
            for part in range(2):
                sums[part].append(row_sums(blocks[part]))
        store_pair(tile, channels, jnp.concatenate(sums[0], 0), jnp.concatenate(sums[1], 0), pair_ref)
        if (tile + 1) % each == 0:
            to_cells(tile // each, share, channels, halves, pair_ref, inverse_ref, out_ref)

    sent_ref[...] = out_ref[...].astype(jnp.bfloat16)


def outer_kernel(share, channels, in_ref, back_ref, slope_ref, point_ref, grad_ref, pointwise_ref, held_ref, sems):
    wide = 2 * channels
    each = in_ref.shape[0] // share
    per_block = LANES // wide
    per_tile = LANES // LENGTH

    def runs(j):
        inside = [kx for kx in range(KX) if residue_of(kx) // per_tile == j]
        found = []
        for kx in inside:
            if found and found[-1][0] + found[-1][2] == kx and found[-1][1] + found[-1][2] == residue_of(kx):
                found[-1][2] += 1
            else:
                found.append([kx, residue_of(kx), 1])
        return found

    def copies(k, j):
        made = []
        for place, (mode, residue, count) in enumerate(runs(j)):
            source = pl.ds(pl.multiple_of((k * LENGTH + residue) * KY, 8), count * KY)
            target = pl.ds(pl.multiple_of((k * KX + mode) * KY, 8), count * KY)
            made.append(
                pltpu.make_async_copy(held_ref.at[source], grad_ref.at[target], sems.at[k * each + j, place])
            )
        return made

    low = lax.broadcasted_iota(jnp.int32, (8, LANES), 0) < 4

    @pl.loop(0, share)
    def _(k):
        for j in range(each):
            tile = k * each + j
            real, imag = back_ref[tile, :channels, :], back_ref[tile, channels:, :]
            here = jnp.concatenate([real, imag], 0)
            turn = jnp.concatenate([imag, -real], 0)
            for c in range(0, channels, per_block):
                parts = [
                    in_ref[tile, c + h : c + h + 1, :] * here
                    + in_ref[tile, channels + c + h : channels + c + h + 1, :] * turn
                    for h in range(per_block)
                ]
                block = jnp.concatenate(parts, 0).T
                for i in range(per_tile):
                    first = block[i * LENGTH : i * LENGTH + 8]
                    second = block[i * LENGTH + 8 : (i + 1) * LENGTH]
                    rows = pl.ds(pl.multiple_of((k * LENGTH + j * per_tile + i) * KY, 8), KY)
                    held_ref[rows, c * wide : c * wide + LANES] = jnp.concatenate(
                        [first, jnp.where(low, second, first), second], 0
                    )
            for copy in copies(k, j):
                copy.start()

    for first in range(0, slope_ref.shape[0], channels):
        rows = slice(first, first + channels)
        pointwise_ref[rows, :] = dot(point_ref[...], slope_ref[rows, :])

    @pl.loop(0, share)
    def _(k):
        for j in range(each):
            for copy in copies(k, j):
                copy.wait()


def slope_kernel(
    cells, channels, factor, units, arrived_ref, table_ref, field_ref, cotangent_ref, point_ref, slope_ref, sent_ref,
    wide_ref,
):
    arrived = received_slots(arrived_ref, cells * channels // LANES, units, wide_ref)
    spectral = dot(arrived.astype(jnp.bfloat16), table_ref[...], 0, 0)
    for c in range(cells):
        rows = slice(c * channels, (c + 1) * channels)
        before = spectral[rows] * factor + dot(point_ref[...], field_ref[rows, :], 0, 0)
        cumulative = 0.5 + 0.5 * lax.erf(before * math.sqrt(0.5))
        density = jnp.exp(-0.5 * before * before) * (1.0 / math.sqrt(2.0 * math.pi))
        slope = cotangent_ref[rows, :].astype(jnp.float32) * (cumulative + before * density)
        slope_ref[rows, :] = slope.astype(jnp.bfloat16)
    sent = dot(table_ref[...], slope_ref[...], 1, 1)
    send_slots(sent * factor, units, wide_ref, sent_ref)


def final_kernel(factor, halves, units, arrived_ref, table_ref, pointwise_ref, grad_ref, wide_ref):
    arrived = received_slots(arrived_ref, halves, units, wide_ref)
    spectral = dot(arrived.astype(jnp.bfloat16), table_ref[...], 0, 0)
    grad_ref[...] = (pointwise_ref[...] + spectral * factor).astype(jnp.bfloat16)


def params(mebibytes, semantics=None):
    return pltpu.CompilerParams(dimension_semantics=semantics, vmem_limit_bytes=mebibytes * 1024 * 1024)


def on_chip(value):
    return pltpu.with_memory_space_constraint(value, pltpu.VMEM)


def off_chip(value):
    return pltpu.with_memory_space_constraint(value, pltpu.HBM)


IN_VMEM = pl.BlockSpec(memory_space=pltpu.VMEM)


def per_device(inputs, cotangent, point_weight, spectral_weight):
    rows_x, rows_y, channels, depth = inputs.shape
    mode_rows, mode_cols, flat = spectral_weight.shape
    count_gx, count_gy = lax.axis_size("gx"), lax.axis_size("gy")
    devices = count_gx * count_gy
    share = mode_rows // KX
    cells = rows_x * rows_y
    lanes = cells * channels
    wide = 2 * channels
    plane = KX * KY
    points = cells * devices
    each = points // LANES
    tiles = share * each
    halves = lanes // LANES
    units = 2 * share * halves
    inner = 1.0 / math.sqrt(points * depth)
    outer = 1.0 / math.sqrt(plane * KZ * KT)

    table = on_chip(jnp.asarray(depth_table(share)))
    forward, inverse = (on_chip(jnp.asarray(t)) for t in plane_tables(count_gx, count_gy, rows_x, rows_y))
    field = on_chip(inputs.reshape(lanes, depth))
    seed = on_chip(cotangent.reshape(lanes, depth))
    point = on_chip(point_weight)

    def exchange(sent):
        blocks = sent.reshape(devices * units // 4, 4, LANES)
        arrived = lax.all_to_all(blocks, GRID_AXES, split_axis=0, concat_axis=0, tiled=True)
        return on_chip(arrived.reshape(devices * units, LANES))

    packet = pltpu.VMEM((devices * units, LANES), jnp.bfloat16)
    unpacked = pltpu.VMEM((devices * units, LANES), jnp.float32)
    spectra = pltpu.VMEM((tiles, wide, LANES), jnp.float32)

    sent = pl.pallas_call(
        functools.partial(depth_kernel, inner, units),
        in_specs=[IN_VMEM] * 2, out_specs=IN_VMEM, out_shape=packet, scratch_shapes=[unpacked],
        compiler_params=params(2),
        cost_estimate=pl.CostEstimate(flops=READ_AHEAD_FLOPS, transcendentals=0, bytes_accessed=0),
        name="depth",
    )(off_chip(jnp.asarray(depth_table(share))), off_chip(inputs.reshape(lanes, depth)))
    arrived = exchange(sent)
    scratch = [unpacked, unpacked, pltpu.VMEM((tiles, wide, 2 * LANES), jnp.bfloat16)]
    sent, modes_in, turned = pl.pallas_call(
        functools.partial(mix_kernel, share, channels, halves),
        in_specs=[IN_VMEM] * 4, out_specs=[IN_VMEM] * 3,
        out_shape=[packet, spectra, pltpu.VMEM((tiles, flat, LANES), jnp.bfloat16)],
        scratch_shapes=scratch, compiler_params=params(6), name="mix",
    )(arrived, on_chip(spectral_weight.reshape(share * plane, flat)), forward, inverse)
    arrived = exchange(sent)
    slope, sent = pl.pallas_call(
        functools.partial(slope_kernel, cells, channels, outer, units),
        in_specs=[IN_VMEM] * 5, out_specs=[IN_VMEM] * 2, out_shape=[pltpu.VMEM((lanes, depth), jnp.bfloat16), packet],
        scratch_shapes=[unpacked],
        compiler_params=params(8), name="slope",
    )(arrived, table, field, seed, point)
    arrived = exchange(sent)
    sent, modes_back = pl.pallas_call(
        functools.partial(adjoint_kernel, share, channels, halves),
        in_specs=[IN_VMEM] * 4, out_specs=[IN_VMEM] * 2, out_shape=[packet, spectra],
        scratch_shapes=scratch,
        compiler_params=params(12), name="adjoint",
    )(arrived, on_chip(turned), forward, inverse)
    arrived = exchange(sent)
    grad_spectral, pointwise = pl.pallas_call(
        functools.partial(outer_kernel, share, channels),
        in_specs=[IN_VMEM] * 4, out_specs=[pl.BlockSpec(memory_space=pl.ANY), IN_VMEM],
        out_shape=[
            jax.ShapeDtypeStruct((share * plane, flat), jnp.float32), pltpu.VMEM((lanes, depth), jnp.float32),
        ],
        scratch_shapes=[
            pltpu.VMEM((share * LENGTH * KY, flat), jnp.float32), pltpu.SemaphoreType.DMA((tiles, 2)),
        ],
        compiler_params=params(24),
        cost_estimate=pl.CostEstimate(
            flops=4 * share * plane * flat * wide, transcendentals=0, bytes_accessed=4 * share * plane * flat
        ),
        name="outer",
    )(on_chip(modes_in), on_chip(modes_back), on_chip(slope), point)
    grad_input = pl.pallas_call(
        functools.partial(final_kernel, inner, halves, units),
        in_specs=[IN_VMEM] * 3, out_specs=IN_VMEM, out_shape=jax.ShapeDtypeStruct((lanes, depth), jnp.bfloat16),
        scratch_shapes=[unpacked],
        compiler_params=params(8), name="final",
    )(arrived, table, on_chip(pointwise))
    return grad_input.reshape(inputs.shape), grad_spectral.reshape(spectral_weight.shape)


def kept_angles(positions, kept_count, length):
    index = jnp.arange(kept_count, dtype=jnp.int32)
    frequency = jnp.where(index < kept_count // 2, index, index - kept_count)
    turns = positions[:, None] * frequency[None, :] % length
    return turns.astype(jnp.float32) * (2.0 * math.pi / length)


def axis_tables(positions, kept_count, length):
    angles = kept_angles(positions, kept_count, length)
    return (jnp.cos(angles), jnp.sin(angles))


def depth_tables():
    angle_depth = kept_angles(jnp.arange(NZ, dtype=jnp.int32), KZ, NZ)
    angle_time = kept_angles(jnp.arange(NT, dtype=jnp.int32), KT, NT)
    angles = (angle_depth[:, None, :, None] + angle_time[None, :, None, :]).reshape(
        NZ * NT, KZ * KT
    )
    return (jnp.cos(angles), jnp.sin(angles))


def settle(values):
    return lax.optimization_barrier(values.astype(jnp.bfloat16))


def rotate(spectra, cosine_table, sine_table, pattern, turn_sign):
    half_width = spectra.shape[-1] // 2
    with_cosine = jnp.einsum(pattern, spectra, cosine_table, precision=lax.Precision.HIGHEST)
    with_sine = jnp.einsum(pattern, spectra, sine_table, precision=lax.Precision.HIGHEST)
    real_part = with_cosine[..., :half_width] + turn_sign * with_sine[..., half_width:]
    imag_part = with_cosine[..., half_width:] - turn_sign * with_sine[..., :half_width]
    return jnp.concatenate([real_part, imag_part], -1)


def depth_forward(field_in, tables, factor):
    widened = field_in.astype(jnp.float32)
    with_cosine = jnp.einsum("xycs,sk->kxyc", widened, tables[0], precision=lax.Precision.HIGHEST)
    with_sine = jnp.einsum("xycs,sk->kxyc", widened, tables[1], precision=lax.Precision.HIGHEST)
    return jnp.concatenate([with_cosine, -with_sine], -1) * factor


def depth_inverse(spectra, tables, factor):
    half_width = spectra.shape[-1] // 2
    with_cosine = jnp.einsum(
        "kxyc,sk->xycs", spectra[..., :half_width], tables[0], precision=lax.Precision.HIGHEST
    )
    with_sine = jnp.einsum(
        "kxyc,sk->xycs", spectra[..., half_width:], tables[1], precision=lax.Precision.HIGHEST
    )
    return (with_cosine - with_sine) * factor


def contract_in(left, right):
    return jnp.einsum("mkc,mkco->mko", left, right, precision=lax.Precision.HIGHEST)


def contract_out(left, right):
    return jnp.einsum("mko,mkco->mkc", left, right, precision=lax.Precision.HIGHEST)


def partial_outer(left, right):
    return jnp.einsum("mkc,mko->mkco", left, right, precision=lax.Precision.HIGHEST)


def mix_modes(spectra, weight):
    half_width = spectra.shape[-1] // 2
    weight_wide = weight.astype(jnp.float32)
    weight_real, weight_imag = (weight_wide[..., :half_width], weight_wide[..., half_width:])
    real_in, imag_in = (spectra[..., :half_width], spectra[..., half_width:])
    real_out = contract_in(real_in, weight_real) - contract_in(imag_in, weight_imag)
    imag_out = contract_in(real_in, weight_imag) + contract_in(imag_in, weight_real)
    return jnp.concatenate([real_out, imag_out], -1)


def adjoint_modes(spectra, weight):
    half_width = spectra.shape[-1] // 2
    weight_wide = weight.astype(jnp.float32)
    weight_real, weight_imag = (weight_wide[..., :half_width], weight_wide[..., half_width:])
    real_in, imag_in = (spectra[..., :half_width], spectra[..., half_width:])
    real_out = contract_out(real_in, weight_real) + contract_out(imag_in, weight_imag)
    imag_out = contract_out(imag_in, weight_real) - contract_out(real_in, weight_imag)
    return jnp.concatenate([real_out, imag_out], -1)


def weight_grad(spectra_in, spectra_back):
    half_width = spectra_in.shape[-1] // 2
    real_in, imag_in = (spectra_in[..., :half_width], spectra_in[..., half_width:])
    real_back, imag_back = (spectra_back[..., :half_width], spectra_back[..., half_width:])
    real_part = partial_outer(real_in, real_back) + partial_outer(imag_in, imag_back)
    imag_part = partial_outer(real_in, imag_back) - partial_outer(imag_in, real_back)
    return jnp.concatenate([real_part, imag_part], -1)


def exact_gelu(values):
    return jax.nn.gelu(values, approximate=False)


def general_per_device(inputs, cotangent, point_weight, spectral_weight):
    rows_x, rows_y, channels, cells = inputs.shape
    mode_rows, mode_cols, flat_width = spectral_weight.shape
    weight_blocks = spectral_weight.reshape(mode_rows, mode_cols, channels, 2 * channels)
    count_gx = lax.axis_size("gx")
    count_gy = lax.axis_size("gy")
    length_x = rows_x * count_gx
    length_y = rows_y * count_gy
    depth_pair = depth_tables()
    own_x = lax.axis_index("gx") * rows_x + jnp.arange(rows_x, dtype=jnp.int32)
    local_x = axis_tables(own_x, KX, length_x)
    whole_y = axis_tables(jnp.arange(length_y, dtype=jnp.int32), KY, length_y)
    total_cells = length_x * length_y * cells
    kept_total = KX * KY * KZ * KT

    def to_modes(field_in, factor):
        depth_spec = settle(depth_forward(field_in, depth_pair, factor))
        share = depth_spec.shape[0] // count_gx
        first_spectra = lax.psum_scatter(
            rotate(
                depth_spec.astype(jnp.float32), local_x[0], local_x[1], "rxyc,xk->rkyc", 1.0
            ).astype(jnp.bfloat16),
            "gx",
            scatter_dimension=0,
            tiled=True,
        ).astype(jnp.float32)
        first_spectra = settle(first_spectra).reshape(share * KX, rows_y, 2 * channels)
        arrived_modes = lax.all_to_all(first_spectra, "gy", split_axis=0, concat_axis=1, tiled=True)
        return rotate(arrived_modes.astype(jnp.float32), whole_y[0], whole_y[1], "myc,yk->mkc", 1.0)

    def to_space(spectra, factor):
        back_rows = settle(rotate(spectra, whole_y[0], whole_y[1], "mkc,yk->myc", -1.0))
        returned = lax.all_to_all(back_rows, "gy", split_axis=1, concat_axis=0, tiled=True)
        share = returned.shape[0] // KX
        returned = returned.reshape(share, KX, rows_y, 2 * channels)
        back_depth = settle(
            rotate(
                lax.all_gather(returned, "gx", axis=0, tiled=True).astype(jnp.float32),
                local_x[0],
                local_x[1],
                "rkyc,xk->rxyc",
                -1.0,
            )
        )
        return depth_inverse(back_depth.astype(jnp.float32), depth_pair, factor)

    spectra_in = to_modes(inputs, 1.0 / math.sqrt(total_cells))
    mixed = mix_modes(spectra_in, weight_blocks)
    spectral_out = to_space(mixed, 1.0 / math.sqrt(kept_total))
    pointwise = jnp.einsum(
        "xycs,co->xyos", inputs, point_weight, preferred_element_type=jnp.float32
    )
    before = spectral_out + pointwise
    unused_out, pullback = jax.vjp(exact_gelu, before)
    slope = settle(pullback(cotangent.astype(jnp.float32))[0])
    spectra_back = to_modes(slope, 1.0 / math.sqrt(kept_total))
    grad_spectral = weight_grad(spectra_in, spectra_back).reshape(mode_rows, mode_cols, flat_width)
    adjoint = adjoint_modes(spectra_back, weight_blocks)
    spectral_grad = to_space(adjoint, 1.0 / math.sqrt(total_cells))
    pointwise_grad = jnp.einsum(
        "xyos,co->xycs", slope, point_weight, preferred_element_type=jnp.float32
    )
    grad_input = (pointwise_grad + spectral_grad).astype(jnp.bfloat16)
    return (grad_input, grad_spectral)


def solution(mesh):
    count_gx, count_gy = mesh.shape["gx"], mesh.shape["gy"]
    placed = (
        P("gx", "gy", None, None),
        P("gx", "gy", None, None),
        P(),
        P(("gx", "gy"), None, None),
    )

    def program(inputs, cotangent, point_weight, spectral_weight):
        cells = inputs.shape[0] * inputs.shape[1] // (count_gx * count_gy)
        whole_modes = KZ * KT % (count_gx * count_gy) == 0
        fits = whole_modes and KZ * KT // (count_gx * count_gy) == 3
        fits = fits and inputs.shape[2] == 32 and cells * inputs.shape[2] == 256 and inputs.shape[0] == inputs.shape[1] == LENGTH
        return jax.shard_map(
            per_device if fits else general_per_device,
            mesh=mesh,
            in_specs=placed,
            out_specs=(P("gx", "gy", None, None), P(("gx", "gy"), None, None)),
            check_vma=False,
        )(inputs, cotangent, point_weight, spectral_weight)

    return program
```

```python
import functools
import math

import jax
import jax.numpy as jnp
import numpy as np
from jax import lax
from jax.experimental import pallas as pl
from jax.experimental.pallas import tpu as pltpu
from jax.sharding import PartitionSpec as P

NZ = 64
NT = 8
KX = 24
KY = 24
KZ = 12
KT = 8
LANES = 128
LENGTH = 16
GROUP = 4
READ_AHEAD_FLOPS = 10**10
GRID_AXES = ("gx", "gy")


def table_angles(positions, kept_count, length):
    index = np.arange(kept_count)
    frequency = np.where(index < kept_count // 2, index, index - kept_count)
    turns = (np.asarray(positions)[:, None] * frequency[None, :]) % length
    return 2.0 * np.pi * turns / length


def depth_table(share):
    angles = (
        table_angles(np.arange(NZ), KZ, NZ)[:, None, :, None]
        + table_angles(np.arange(NT), KT, NT)[None, :, None, :]
    ).reshape(NZ * NT, KZ * KT)
    parts = np.stack([np.cos(angles), -np.sin(angles)], -1)
    owners = KZ * KT // share
    rows = parts.reshape(NZ * NT, owners, 2 * share).transpose(2, 1, 0)
    return rows.reshape(2 * share * owners, NZ * NT).astype(jnp.bfloat16)


def plane_tables(count_gx, count_gy, rows_x, rows_y):
    length_x, length_y = count_gx * rows_x, count_gy * rows_y
    turns_x = np.outer(np.arange(length_x), np.arange(length_x)) % length_x / length_x
    turns_y = np.outer(np.arange(length_y), np.arange(length_y)) % length_y / length_y
    turns_x = turns_x.reshape(length_x, 1, count_gx, 1, rows_x, 1)
    turns_y = turns_y.reshape(1, length_y, 1, count_gy, 1, rows_y)
    turns = (turns_x + turns_y).transpose(0, 1, 4, 5, 2, 3).reshape(length_x * length_y, length_x * length_y)
    cosine, sine = np.cos(2.0 * np.pi * turns), np.sin(2.0 * np.pi * turns)
    forward = np.concatenate([cosine.T, sine.T], 0)
    inverse = np.concatenate([cosine.T, sine.T], 1)
    return forward.astype(jnp.bfloat16), inverse.astype(jnp.bfloat16)


def residue_of(mode):
    return (mode if mode < KX // 2 else mode - KX) % LENGTH


def modes_of(residue):
    return [mode for mode in range(KX) if residue_of(mode) == residue]


def dot(left, right, left_dim=1, right_dim=0):
    return lax.dot_general(
        left, right, (((left_dim,), (right_dim,)), ((), ())), preferred_element_type=jnp.float32
    )


def unit_rows(unit, wide_ref, units):
    return pl.ds(unit, wide_ref.shape[0] // units, stride=units)


def send_slots(spectra, units, wide_ref, sent_ref):
    devices = wide_ref.shape[0] // units
    halves = spectra.shape[1] // LANES
    for unit in range(units):
        slot, h = divmod(unit, halves)
        wide_ref[unit_rows(unit, wide_ref, units), :] = spectra[
            slot * devices : (slot + 1) * devices, h * LANES : (h + 1) * LANES
        ]
    sent_ref[...] = wide_ref[...].astype(jnp.bfloat16)


def received_slots(arrived_ref, halves, units, wide_ref):
    wide_ref[...] = arrived_ref[...].astype(jnp.float32)
    slots = []
    for slot in range(units // halves):
        pieces = [wide_ref[unit_rows(slot * halves + h, wide_ref, units), :] for h in range(halves)]
        slots.append(jnp.concatenate(pieces, 1))
    return jnp.concatenate(slots, 0)


def depth_kernel(factor, units, table_ref, field_ref, sent_ref, wide_ref):
    spectra = dot(table_ref[...], field_ref[...], 1, 1)
    send_slots(spectra * factor, units, wide_ref, sent_ref)


def to_plane_modes(share, channels, halves, arrived_ref, forward_ref, wide_ref, modes_ref):
    slots = received_slots(arrived_ref, halves, 2 * share * halves, wide_ref)
    devices = wide_ref.shape[0] // (2 * share * halves)
    lanes = slots.shape[1]
    turned = slots.astype(jnp.bfloat16).T
    blocks = []
    for slot in range(2 * share):
        pieces = [
            turned[c * channels : (c + 1) * channels, slot * devices : (slot + 1) * devices]
            for c in range(lanes // channels)
        ]
        blocks.append(jnp.concatenate(pieces, 1))
    rows = []
    for k in range(share):
        real, imag = blocks[2 * k], blocks[2 * k + 1]
        rows += [jnp.concatenate([real, imag], 1), jnp.concatenate([imag, -real], 1)]
    modes = dot(jnp.concatenate(rows, 0), forward_ref[...])
    each = modes_ref.shape[0] // share
    for k in range(share):
        for j in range(each):
            modes_ref[k * each + j] = modes[2 * k * channels : (2 * k + 2) * channels, j * LANES : (j + 1) * LANES]


def store_pair(tile, channels, real, imag, pair_ref):
    pair_ref[tile, :channels, :LANES] = real.astype(jnp.bfloat16)
    pair_ref[tile, channels:, :LANES] = imag.astype(jnp.bfloat16)
    pair_ref[tile, :channels, LANES:] = (-imag).astype(jnp.bfloat16)
    pair_ref[tile, channels:, LANES:] = real.astype(jnp.bfloat16)


def to_cells(k, share, channels, halves, pair_ref, inverse_ref, out_ref):
    units = 2 * share * halves
    devices = out_ref.shape[0] // units
    each = pair_ref.shape[0] // share
    cosine = jnp.concatenate([pair_ref[k * each + j, :, :LANES] for j in range(each)], 1)
    sine = jnp.concatenate([pair_ref[k * each + j, :, LANES:] for j in range(each)], 1)
    total = dot(inverse_ref[...], jnp.concatenate([cosine, sine], 1), 1, 1)
    per_half = LANES // channels
    for part in range(2):
        columns = slice(part * channels, (part + 1) * channels)
        for h in range(halves):
            pieces = [total[c * devices : (c + 1) * devices, columns] for c in range(h * per_half, (h + 1) * per_half)]
            unit = (2 * k + part) * halves + h
            out_ref[unit_rows(unit, out_ref, units), :] = jnp.concatenate(pieces, 1)


def fold_rows(weight_ref, mode, first, count, columns):
    row = lax.broadcasted_iota(jnp.int32, (8, LANES), 0)
    folded = []
    for residue in range(first, first + count):
        total = None
        for kx in modes_of(residue):
            rows = pl.ds(pl.multiple_of((mode * KX + kx) * KY, 8), KY)
            block = weight_ref[rows, columns]
            total = block if total is None else total + block
        folded += [total[:8] + jnp.where(row < 4, jnp.bfloat16(0), total[8:16]), total[16:] + jnp.where(row < 4, total[8:16], jnp.bfloat16(0))]
    return jnp.concatenate(folded, 0)


def mix_kernel(
    share, channels, halves, arrived_ref, weight_ref, forward_ref, inverse_ref, sent_ref, modes_ref, turned_ref,
    wide_ref, out_ref, pair_ref,
):
    to_plane_modes(share, channels, halves, arrived_ref, forward_ref, wide_ref, modes_ref)
    wide = 2 * channels
    each = modes_ref.shape[0] // share
    per_tile = LANES // LENGTH

    for k in range(share):
        for j in range(each):
            tile = k * each + j
            by_real = jnp.zeros((wide, LANES), jnp.float32)
            by_imag = jnp.zeros((wide, LANES), jnp.float32)
            for first in range(0, channels, GROUP):
                real_sum, imag_sum = None, None
                for c in range(first, first + GROUP, LANES // wide):
                    columns = slice(c * wide, c * wide + LANES)
                    block = fold_rows(weight_ref, k, j * per_tile, per_tile, columns).T
                    turned_ref[tile, columns, :] = block
                    for h in range(LANES // wide):
                        weight = block[h * wide : (h + 1) * wide]
                        real = jnp.broadcast_to(modes_ref[tile, c + h : c + h + 1, :], (wide, LANES))
                        imag = jnp.broadcast_to(
                            modes_ref[tile, channels + c + h : channels + c + h + 1, :], (wide, LANES)
                        )
                        real, imag = real.astype(jnp.bfloat16) * weight, imag.astype(jnp.bfloat16) * weight
                        real_sum = real if real_sum is None else real_sum + real
                        imag_sum = imag if imag_sum is None else imag_sum + imag
                by_real += real_sum.astype(jnp.float32)
                by_imag += imag_sum.astype(jnp.float32)
            store_pair(
                tile, channels, by_real[:channels] - by_imag[channels:],
                by_real[channels:] + by_imag[:channels], pair_ref,
            )
        to_cells(k, share, channels, halves, pair_ref, inverse_ref, out_ref)

    sent_ref[...] = out_ref[...].astype(jnp.bfloat16)


def row_sums(blocks):
    row = lax.broadcasted_iota(jnp.int32, (8, LANES), 0)
    for shift in (4, 2, 1):
        merged = []
        clear = row % (2 * shift) < shift
        for i in range(shift):
            first, second = blocks[i], blocks[i + shift]
            merged.append(
                jnp.where(clear, first + pltpu.roll(first, 8 - shift, 0), second + pltpu.roll(second, shift, 0))
            )
        blocks = merged
    return blocks[0]


def adjoint_kernel(
    share, channels, halves, arrived_ref, turned_ref, forward_ref, inverse_ref, sent_hbm, modes_ref, wide_ref,
    out_ref, pair_ref, sent_ref, sems,
):
    to_plane_modes(share, channels, halves, arrived_ref, forward_ref, wide_ref, modes_ref)
    wide = 2 * channels
    each = modes_ref.shape[0] // share

    for tile in range(modes_ref.shape[0]):
        real, imag = modes_ref[tile, :channels, :], modes_ref[tile, channels:, :]
        here = jnp.concatenate([real, imag], 0).astype(jnp.bfloat16)
        turn = jnp.concatenate([imag, -real], 0).astype(jnp.bfloat16)
        sums = ([], [])
        for first in range(0, channels, 8):
            blocks = ([], [])
            for c in range(first, first + 8):
                weight = turned_ref[tile, c * wide : (c + 1) * wide, :]
                for part, factor in enumerate((here, turn)):
                    product = factor * weight
                    product = product[: wide // 2] + product[wide // 2 :]
                    product = (product[: wide // 4] + product[wide // 4 :]).astype(jnp.float32)
                    blocks[part].append(product[:8] + product[8:])
            for part in range(2):
                sums[part].append(row_sums(blocks[part]))
        store_pair(tile, channels, jnp.concatenate(sums[0], 0), jnp.concatenate(sums[1], 0), pair_ref)
        if (tile + 1) % each == 0:
            to_cells(tile // each, share, channels, halves, pair_ref, inverse_ref, out_ref)

    count = sems.shape[0]
    rows = sent_ref.shape[0] // count
    copies = []
    for part in range(count):
        here = pl.ds(part * rows, rows)
        sent_ref[here, :] = out_ref[here, :].astype(jnp.bfloat16)
        copies.append(pltpu.make_async_copy(sent_ref.at[here], sent_hbm.at[here], sems.at[part]))
        copies[-1].start()
    for copy in copies:
        copy.wait()


def outer_kernel(share, channels, in_ref, back_ref, slope_ref, point_ref, grad_ref, pointwise_ref, held_ref, sems):
    wide = 2 * channels
    each = in_ref.shape[0] // share
    per_block = LANES // wide
    per_tile = LANES // LENGTH

    def runs(j):
        inside = [kx for kx in range(KX) if residue_of(kx) // per_tile == j]
        found = []
        for kx in inside:
            if found and found[-1][0] + found[-1][2] == kx and found[-1][1] + found[-1][2] == residue_of(kx):
                found[-1][2] += 1
            else:
                found.append([kx, residue_of(kx), 1])
        return found

    def copies(k, j):
        made = []
        for place, (mode, residue, count) in enumerate(runs(j)):
            source = pl.ds(pl.multiple_of((k * LENGTH + residue) * KY, 8), count * KY)
            target = pl.ds(pl.multiple_of((k * KX + mode) * KY, 8), count * KY)
            made.append(
                pltpu.make_async_copy(held_ref.at[source], grad_ref.at[target], sems.at[k * each + j, place])
            )
        return made

    low = lax.broadcasted_iota(jnp.int32, (8, LANES), 0) < 4

    @pl.loop(0, share)
    def _(k):
        for j in range(each):
            tile = k * each + j
            real, imag = back_ref[tile, :channels, :], back_ref[tile, channels:, :]
            here = jnp.concatenate([real, imag], 0)
            turn = jnp.concatenate([imag, -real], 0)
            for c in range(0, channels, per_block):
                parts = [
                    in_ref[tile, c + h : c + h + 1, :] * here
                    + in_ref[tile, channels + c + h : channels + c + h + 1, :] * turn
                    for h in range(per_block)
                ]
                block = jnp.concatenate(parts, 0).T
                for i in range(per_tile):
                    first = block[i * LENGTH : i * LENGTH + 8]
                    second = block[i * LENGTH + 8 : (i + 1) * LENGTH]
                    rows = pl.ds(pl.multiple_of((k * LENGTH + j * per_tile + i) * KY, 8), KY)
                    held_ref[rows, c * wide : c * wide + LANES] = jnp.concatenate(
                        [first, jnp.where(low, second, first), second], 0
                    )
            for copy in copies(k, j):
                copy.start()

    for first in range(0, slope_ref.shape[0], channels):
        rows = slice(first, first + channels)
        pointwise_ref[rows, :] = dot(point_ref[...], slope_ref[rows, :])

    @pl.loop(0, share)
    def _(k):
        for j in range(each):
            for copy in copies(k, j):
                copy.wait()


def slope_kernel(
    cells, channels, factor, units, arrived_ref, table_ref, field_ref, cotangent_ref, point_ref, slope_ref, sent_ref,
    wide_ref,
):
    arrived = received_slots(arrived_ref, cells * channels // LANES, units, wide_ref)
    spectral = dot(arrived.astype(jnp.bfloat16), table_ref[...], 0, 0)
    for c in range(cells):
        rows = slice(c * channels, (c + 1) * channels)
        before = spectral[rows] * factor + dot(point_ref[...], field_ref[rows, :], 0, 0)
        cumulative = 0.5 + 0.5 * lax.erf(before * math.sqrt(0.5))
        density = jnp.exp(-0.5 * before * before) * (1.0 / math.sqrt(2.0 * math.pi))
        slope = cotangent_ref[rows, :].astype(jnp.float32) * (cumulative + before * density)
        slope_ref[rows, :] = slope.astype(jnp.bfloat16)
    sent = dot(table_ref[...], slope_ref[...], 1, 1)
    send_slots(sent * factor, units, wide_ref, sent_ref)


def final_kernel(factor, halves, units, arrived_ref, table_ref, pointwise_ref, grad_ref, wide_ref):
    arrived = received_slots(arrived_ref, halves, units, wide_ref)
    spectral = dot(arrived.astype(jnp.bfloat16), table_ref[...], 0, 0)
    grad_ref[...] = (pointwise_ref[...] + spectral * factor).astype(jnp.bfloat16)


def params(mebibytes, semantics=None):
    return pltpu.CompilerParams(dimension_semantics=semantics, vmem_limit_bytes=mebibytes * 1024 * 1024)


def on_chip(value):
    return pltpu.with_memory_space_constraint(value, pltpu.VMEM)


def off_chip(value):
    return pltpu.with_memory_space_constraint(value, pltpu.HBM)


IN_VMEM = pl.BlockSpec(memory_space=pltpu.VMEM)


def per_device(inputs, cotangent, point_weight, spectral_weight):
    rows_x, rows_y, channels, depth = inputs.shape
    mode_rows, mode_cols, flat = spectral_weight.shape
    count_gx, count_gy = lax.axis_size("gx"), lax.axis_size("gy")
    devices = count_gx * count_gy
    share = mode_rows // KX
    cells = rows_x * rows_y
    lanes = cells * channels
    wide = 2 * channels
    plane = KX * KY
    points = cells * devices
    each = points // LANES
    tiles = share * each
    halves = lanes // LANES
    units = 2 * share * halves
    inner = 1.0 / math.sqrt(points * depth)
    outer = 1.0 / math.sqrt(plane * KZ * KT)

    table = on_chip(jnp.asarray(depth_table(share)))
    forward, inverse = (on_chip(jnp.asarray(t)) for t in plane_tables(count_gx, count_gy, rows_x, rows_y))
    field = on_chip(inputs.reshape(lanes, depth))
    seed = on_chip(cotangent.reshape(lanes, depth))
    point = on_chip(point_weight)

    def exchange(sent):
        blocks = sent.reshape(devices * units // 4, 4, LANES)
        arrived = lax.all_to_all(blocks, GRID_AXES, split_axis=0, concat_axis=0, tiled=True)
        return on_chip(arrived.reshape(devices * units, LANES))

    packet = pltpu.VMEM((devices * units, LANES), jnp.bfloat16)
    unpacked = pltpu.VMEM((devices * units, LANES), jnp.float32)
    spectra = pltpu.VMEM((tiles, wide, LANES), jnp.float32)

    sent = pl.pallas_call(
        functools.partial(depth_kernel, inner, units),
        in_specs=[IN_VMEM] * 2, out_specs=IN_VMEM, out_shape=packet, scratch_shapes=[unpacked],
        compiler_params=params(2),
        cost_estimate=pl.CostEstimate(flops=READ_AHEAD_FLOPS, transcendentals=0, bytes_accessed=0),
        name="depth",
    )(off_chip(jnp.asarray(depth_table(share))), off_chip(inputs.reshape(lanes, depth)))
    arrived = exchange(sent)
    scratch = [unpacked, unpacked, pltpu.VMEM((tiles, wide, 2 * LANES), jnp.bfloat16)]
    sent, modes_in, turned = pl.pallas_call(
        functools.partial(mix_kernel, share, channels, halves),
        in_specs=[IN_VMEM] * 4, out_specs=[IN_VMEM] * 3,
        out_shape=[packet, spectra, pltpu.VMEM((tiles, flat, LANES), jnp.bfloat16)],
        scratch_shapes=scratch, compiler_params=params(6), name="mix",
    )(arrived, on_chip(spectral_weight.reshape(share * plane, flat)), forward, inverse)
    arrived = exchange(sent)
    slope, sent = pl.pallas_call(
        functools.partial(slope_kernel, cells, channels, outer, units),
        in_specs=[IN_VMEM] * 5, out_specs=[IN_VMEM] * 2, out_shape=[pltpu.VMEM((lanes, depth), jnp.bfloat16), packet],
        scratch_shapes=[unpacked],
        compiler_params=params(8), name="slope",
    )(arrived, table, field, seed, point)
    arrived = exchange(sent)
    sent, modes_back = pl.pallas_call(
        functools.partial(adjoint_kernel, share, channels, halves),
        in_specs=[IN_VMEM] * 4, out_specs=[pl.BlockSpec(memory_space=pl.ANY), IN_VMEM],
        out_shape=[jax.ShapeDtypeStruct((devices * units, LANES), jnp.bfloat16), spectra],
        scratch_shapes=scratch + [packet, pltpu.SemaphoreType.DMA((2,))],
        compiler_params=params(12), name="adjoint",
    )(arrived, on_chip(turned), forward, inverse)
    arrived = exchange(sent)
    grad_spectral, pointwise = pl.pallas_call(
        functools.partial(outer_kernel, share, channels),
        in_specs=[IN_VMEM] * 4, out_specs=[pl.BlockSpec(memory_space=pl.ANY), IN_VMEM],
        out_shape=[
            jax.ShapeDtypeStruct((share * plane, flat), jnp.float32), pltpu.VMEM((lanes, depth), jnp.float32),
        ],
        scratch_shapes=[
            pltpu.VMEM((share * LENGTH * KY, flat), jnp.float32), pltpu.SemaphoreType.DMA((tiles, 2)),
        ],
        compiler_params=params(24),
        cost_estimate=pl.CostEstimate(
            flops=4 * share * plane * flat * wide, transcendentals=0, bytes_accessed=4 * share * plane * flat
        ),
        name="outer",
    )(on_chip(modes_in), on_chip(modes_back), on_chip(slope), point)
    grad_input = pl.pallas_call(
        functools.partial(final_kernel, inner, halves, units),
        in_specs=[IN_VMEM] * 3, out_specs=IN_VMEM, out_shape=jax.ShapeDtypeStruct((lanes, depth), jnp.bfloat16),
        scratch_shapes=[unpacked],
        compiler_params=params(8), name="final",
    )(arrived, table, on_chip(pointwise))
    return grad_input.reshape(inputs.shape), grad_spectral.reshape(spectral_weight.shape)


def kept_angles(positions, kept_count, length):
    index = jnp.arange(kept_count, dtype=jnp.int32)
    frequency = jnp.where(index < kept_count // 2, index, index - kept_count)
    turns = positions[:, None] * frequency[None, :] % length
    return turns.astype(jnp.float32) * (2.0 * math.pi / length)


def axis_tables(positions, kept_count, length):
    angles = kept_angles(positions, kept_count, length)
    return (jnp.cos(angles), jnp.sin(angles))


def depth_tables():
    angle_depth = kept_angles(jnp.arange(NZ, dtype=jnp.int32), KZ, NZ)
    angle_time = kept_angles(jnp.arange(NT, dtype=jnp.int32), KT, NT)
    angles = (angle_depth[:, None, :, None] + angle_time[None, :, None, :]).reshape(
        NZ * NT, KZ * KT
    )
    return (jnp.cos(angles), jnp.sin(angles))


def settle(values):
    return lax.optimization_barrier(values.astype(jnp.bfloat16))


def rotate(spectra, cosine_table, sine_table, pattern, turn_sign):
    half_width = spectra.shape[-1] // 2
    with_cosine = jnp.einsum(pattern, spectra, cosine_table, precision=lax.Precision.HIGHEST)
    with_sine = jnp.einsum(pattern, spectra, sine_table, precision=lax.Precision.HIGHEST)
    real_part = with_cosine[..., :half_width] + turn_sign * with_sine[..., half_width:]
    imag_part = with_cosine[..., half_width:] - turn_sign * with_sine[..., :half_width]
    return jnp.concatenate([real_part, imag_part], -1)


def depth_forward(field_in, tables, factor):
    widened = field_in.astype(jnp.float32)
    with_cosine = jnp.einsum("xycs,sk->kxyc", widened, tables[0], precision=lax.Precision.HIGHEST)
    with_sine = jnp.einsum("xycs,sk->kxyc", widened, tables[1], precision=lax.Precision.HIGHEST)
    return jnp.concatenate([with_cosine, -with_sine], -1) * factor


def depth_inverse(spectra, tables, factor):
    half_width = spectra.shape[-1] // 2
    with_cosine = jnp.einsum(
        "kxyc,sk->xycs", spectra[..., :half_width], tables[0], precision=lax.Precision.HIGHEST
    )
    with_sine = jnp.einsum(
        "kxyc,sk->xycs", spectra[..., half_width:], tables[1], precision=lax.Precision.HIGHEST
    )
    return (with_cosine - with_sine) * factor


def contract_in(left, right):
    return jnp.einsum("mkc,mkco->mko", left, right, precision=lax.Precision.HIGHEST)


def contract_out(left, right):
    return jnp.einsum("mko,mkco->mkc", left, right, precision=lax.Precision.HIGHEST)


def partial_outer(left, right):
    return jnp.einsum("mkc,mko->mkco", left, right, precision=lax.Precision.HIGHEST)


def mix_modes(spectra, weight):
    half_width = spectra.shape[-1] // 2
    weight_wide = weight.astype(jnp.float32)
    weight_real, weight_imag = (weight_wide[..., :half_width], weight_wide[..., half_width:])
    real_in, imag_in = (spectra[..., :half_width], spectra[..., half_width:])
    real_out = contract_in(real_in, weight_real) - contract_in(imag_in, weight_imag)
    imag_out = contract_in(real_in, weight_imag) + contract_in(imag_in, weight_real)
    return jnp.concatenate([real_out, imag_out], -1)


def adjoint_modes(spectra, weight):
    half_width = spectra.shape[-1] // 2
    weight_wide = weight.astype(jnp.float32)
    weight_real, weight_imag = (weight_wide[..., :half_width], weight_wide[..., half_width:])
    real_in, imag_in = (spectra[..., :half_width], spectra[..., half_width:])
    real_out = contract_out(real_in, weight_real) + contract_out(imag_in, weight_imag)
    imag_out = contract_out(imag_in, weight_real) - contract_out(real_in, weight_imag)
    return jnp.concatenate([real_out, imag_out], -1)


def weight_grad(spectra_in, spectra_back):
    half_width = spectra_in.shape[-1] // 2
    real_in, imag_in = (spectra_in[..., :half_width], spectra_in[..., half_width:])
    real_back, imag_back = (spectra_back[..., :half_width], spectra_back[..., half_width:])
    real_part = partial_outer(real_in, real_back) + partial_outer(imag_in, imag_back)
    imag_part = partial_outer(real_in, imag_back) - partial_outer(imag_in, real_back)
    return jnp.concatenate([real_part, imag_part], -1)


def exact_gelu(values):
    return jax.nn.gelu(values, approximate=False)


def general_per_device(inputs, cotangent, point_weight, spectral_weight):
    rows_x, rows_y, channels, cells = inputs.shape
    mode_rows, mode_cols, flat_width = spectral_weight.shape
    weight_blocks = spectral_weight.reshape(mode_rows, mode_cols, channels, 2 * channels)
    count_gx = lax.axis_size("gx")
    count_gy = lax.axis_size("gy")
    length_x = rows_x * count_gx
    length_y = rows_y * count_gy
    depth_pair = depth_tables()
    own_x = lax.axis_index("gx") * rows_x + jnp.arange(rows_x, dtype=jnp.int32)
    local_x = axis_tables(own_x, KX, length_x)
    whole_y = axis_tables(jnp.arange(length_y, dtype=jnp.int32), KY, length_y)
    total_cells = length_x * length_y * cells
    kept_total = KX * KY * KZ * KT

    def to_modes(field_in, factor):
        depth_spec = settle(depth_forward(field_in, depth_pair, factor))
        share = depth_spec.shape[0] // count_gx
        first_spectra = lax.psum_scatter(
            rotate(
                depth_spec.astype(jnp.float32), local_x[0], local_x[1], "rxyc,xk->rkyc", 1.0
            ).astype(jnp.bfloat16),
            "gx",
            scatter_dimension=0,
            tiled=True,
        ).astype(jnp.float32)
        first_spectra = settle(first_spectra).reshape(share * KX, rows_y, 2 * channels)
        arrived_modes = lax.all_to_all(first_spectra, "gy", split_axis=0, concat_axis=1, tiled=True)
        return rotate(arrived_modes.astype(jnp.float32), whole_y[0], whole_y[1], "myc,yk->mkc", 1.0)

    def to_space(spectra, factor):
        back_rows = settle(rotate(spectra, whole_y[0], whole_y[1], "mkc,yk->myc", -1.0))
        returned = lax.all_to_all(back_rows, "gy", split_axis=1, concat_axis=0, tiled=True)
        share = returned.shape[0] // KX
        returned = returned.reshape(share, KX, rows_y, 2 * channels)
        back_depth = settle(
            rotate(
                lax.all_gather(returned, "gx", axis=0, tiled=True).astype(jnp.float32),
                local_x[0],
                local_x[1],
                "rkyc,xk->rxyc",
                -1.0,
            )
        )
        return depth_inverse(back_depth.astype(jnp.float32), depth_pair, factor)

    spectra_in = to_modes(inputs, 1.0 / math.sqrt(total_cells))
    mixed = mix_modes(spectra_in, weight_blocks)
    spectral_out = to_space(mixed, 1.0 / math.sqrt(kept_total))
    pointwise = jnp.einsum(
        "xycs,co->xyos", inputs, point_weight, preferred_element_type=jnp.float32
    )
    before = spectral_out + pointwise
    unused_out, pullback = jax.vjp(exact_gelu, before)
    slope = settle(pullback(cotangent.astype(jnp.float32))[0])
    spectra_back = to_modes(slope, 1.0 / math.sqrt(kept_total))
    grad_spectral = weight_grad(spectra_in, spectra_back).reshape(mode_rows, mode_cols, flat_width)
    adjoint = adjoint_modes(spectra_back, weight_blocks)
    spectral_grad = to_space(adjoint, 1.0 / math.sqrt(total_cells))
    pointwise_grad = jnp.einsum(
        "xyos,co->xycs", slope, point_weight, preferred_element_type=jnp.float32
    )
    grad_input = (pointwise_grad + spectral_grad).astype(jnp.bfloat16)
    return (grad_input, grad_spectral)


def solution(mesh):
    count_gx, count_gy = mesh.shape["gx"], mesh.shape["gy"]
    placed = (
        P("gx", "gy", None, None),
        P("gx", "gy", None, None),
        P(),
        P(("gx", "gy"), None, None),
    )

    def program(inputs, cotangent, point_weight, spectral_weight):
        cells = inputs.shape[0] * inputs.shape[1] // (count_gx * count_gy)
        whole_modes = KZ * KT % (count_gx * count_gy) == 0
        fits = whole_modes and KZ * KT // (count_gx * count_gy) == 3
        fits = fits and inputs.shape[2] == 32 and cells * inputs.shape[2] == 256 and inputs.shape[0] == inputs.shape[1] == LENGTH
        return jax.shard_map(
            per_device if fits else general_per_device,
            mesh=mesh,
            in_specs=placed,
            out_specs=(P("gx", "gy", None, None), P(("gx", "gy"), None, None)),
            check_vma=False,
        )(inputs, cotangent, point_weight, spectral_weight)

    return program
```

```python
import functools
import math

import jax
import jax.numpy as jnp
import numpy as np
from jax import lax
from jax.experimental import pallas as pl
from jax.experimental.pallas import tpu as pltpu
from jax.sharding import PartitionSpec as P

NZ = 64
NT = 8
KX = 24
KY = 24
KZ = 12
KT = 8
LANES = 128
LENGTH = 16
GROUP = 4
READ_AHEAD_FLOPS = 10**10
GRID_AXES = ("gx", "gy")


def table_angles(positions, kept_count, length):
    index = np.arange(kept_count)
    frequency = np.where(index < kept_count // 2, index, index - kept_count)
    turns = (np.asarray(positions)[:, None] * frequency[None, :]) % length
    return 2.0 * np.pi * turns / length


def depth_table(share):
    angles = (
        table_angles(np.arange(NZ), KZ, NZ)[:, None, :, None]
        + table_angles(np.arange(NT), KT, NT)[None, :, None, :]
    ).reshape(NZ * NT, KZ * KT)
    parts = np.stack([np.cos(angles), -np.sin(angles)], -1)
    owners = KZ * KT // share
    rows = parts.reshape(NZ * NT, owners, 2 * share).transpose(2, 1, 0)
    return rows.reshape(2 * share * owners, NZ * NT).astype(jnp.bfloat16)


def plane_tables(count_gx, count_gy, rows_x, rows_y):
    length_x, length_y = count_gx * rows_x, count_gy * rows_y
    turns_x = np.outer(np.arange(length_x), np.arange(length_x)) % length_x / length_x
    turns_y = np.outer(np.arange(length_y), np.arange(length_y)) % length_y / length_y
    turns_x = turns_x.reshape(length_x, 1, count_gx, 1, rows_x, 1)
    turns_y = turns_y.reshape(1, length_y, 1, count_gy, 1, rows_y)
    turns = (turns_x + turns_y).transpose(0, 1, 4, 5, 2, 3).reshape(length_x * length_y, length_x * length_y)
    cosine, sine = np.cos(2.0 * np.pi * turns), np.sin(2.0 * np.pi * turns)
    forward = np.concatenate([cosine.T, sine.T], 0)
    inverse = np.concatenate([cosine.T, sine.T], 1)
    return forward.astype(jnp.bfloat16), inverse.astype(jnp.bfloat16)


def residue_of(mode):
    return (mode if mode < KX // 2 else mode - KX) % LENGTH


def modes_of(residue):
    return [mode for mode in range(KX) if residue_of(mode) == residue]


def dot(left, right, left_dim=1, right_dim=0):
    return lax.dot_general(
        left, right, (((left_dim,), (right_dim,)), ((), ())), preferred_element_type=jnp.float32
    )


def unit_rows(unit, wide_ref, units):
    return pl.ds(unit, wide_ref.shape[0] // units, stride=units)


def send_slots(spectra, units, wide_ref, sent_ref):
    devices = wide_ref.shape[0] // units
    halves = spectra.shape[1] // LANES
    for unit in range(units):
        slot, h = divmod(unit, halves)
        wide_ref[unit_rows(unit, wide_ref, units), :] = spectra[
            slot * devices : (slot + 1) * devices, h * LANES : (h + 1) * LANES
        ]
    sent_ref[...] = wide_ref[...].astype(jnp.bfloat16)


def received_slots(arrived_ref, halves, units, wide_ref):
    wide_ref[...] = arrived_ref[...].astype(jnp.float32)
    slots = []
    for slot in range(units // halves):
        pieces = [wide_ref[unit_rows(slot * halves + h, wide_ref, units), :] for h in range(halves)]
        slots.append(jnp.concatenate(pieces, 1))
    return jnp.concatenate(slots, 0)


def depth_kernel(factor, units, table_ref, field_ref, sent_ref, wide_ref):
    spectra = dot(table_ref[...], field_ref[...], 1, 1)
    send_slots(spectra * factor, units, wide_ref, sent_ref)


def to_plane_modes(share, channels, halves, arrived_ref, forward_ref, wide_ref, modes_ref):
    slots = received_slots(arrived_ref, halves, 2 * share * halves, wide_ref)
    devices = wide_ref.shape[0] // (2 * share * halves)
    lanes = slots.shape[1]
    turned = slots.astype(jnp.bfloat16).T
    blocks = []
    for slot in range(2 * share):
        pieces = [
            turned[c * channels : (c + 1) * channels, slot * devices : (slot + 1) * devices]
            for c in range(lanes // channels)
        ]
        blocks.append(jnp.concatenate(pieces, 1))
    rows = []
    for k in range(share):
        real, imag = blocks[2 * k], blocks[2 * k + 1]
        rows += [jnp.concatenate([real, imag], 1), jnp.concatenate([imag, -real], 1)]
    modes = dot(jnp.concatenate(rows, 0), forward_ref[...])
    each = modes_ref.shape[0] // share
    for k in range(share):
        for j in range(each):
            modes_ref[k * each + j] = modes[2 * k * channels : (2 * k + 2) * channels, j * LANES : (j + 1) * LANES]


def store_pair(tile, channels, real, imag, pair_ref):
    pair_ref[tile, :channels, :LANES] = real.astype(jnp.bfloat16)
    pair_ref[tile, channels:, :LANES] = imag.astype(jnp.bfloat16)
    pair_ref[tile, :channels, LANES:] = (-imag).astype(jnp.bfloat16)
    pair_ref[tile, channels:, LANES:] = real.astype(jnp.bfloat16)


def to_cells(k, share, channels, halves, pair_ref, inverse_ref, out_ref):
    units = 2 * share * halves
    devices = out_ref.shape[0] // units
    each = pair_ref.shape[0] // share
    cosine = jnp.concatenate([pair_ref[k * each + j, :, :LANES] for j in range(each)], 1)
    sine = jnp.concatenate([pair_ref[k * each + j, :, LANES:] for j in range(each)], 1)
    total = dot(inverse_ref[...], jnp.concatenate([cosine, sine], 1), 1, 1)
    per_half = LANES // channels
    for part in range(2):
        columns = slice(part * channels, (part + 1) * channels)
        for h in range(halves):
            pieces = [total[c * devices : (c + 1) * devices, columns] for c in range(h * per_half, (h + 1) * per_half)]
            unit = (2 * k + part) * halves + h
            out_ref[unit_rows(unit, out_ref, units), :] = jnp.concatenate(pieces, 1)


def fold_rows(weight_ref, mode, first, count, columns):
    row = lax.broadcasted_iota(jnp.int32, (8, LANES), 0)
    folded = []
    for residue in range(first, first + count):
        total = None
        for kx in modes_of(residue):
            rows = pl.ds(pl.multiple_of((mode * KX + kx) * KY, 8), KY)
            block = weight_ref[rows, columns]
            total = block if total is None else total + block
        folded += [total[:8] + jnp.where(row < 4, jnp.bfloat16(0), total[8:16]), total[16:] + jnp.where(row < 4, total[8:16], jnp.bfloat16(0))]
    return jnp.concatenate(folded, 0)


def mix_kernel(
    share, channels, halves, arrived_ref, weight_ref, forward_ref, inverse_ref, sent_ref, modes_ref, turned_ref,
    wide_ref, out_ref, pair_ref,
):
    to_plane_modes(share, channels, halves, arrived_ref, forward_ref, wide_ref, modes_ref)
    wide = 2 * channels
    each = modes_ref.shape[0] // share
    per_tile = LANES // LENGTH

    for k in range(share):
        for j in range(each):
            tile = k * each + j
            by_real = jnp.zeros((wide, LANES), jnp.float32)
            by_imag = jnp.zeros((wide, LANES), jnp.float32)
            for first in range(0, channels, GROUP):
                real_sum, imag_sum = None, None
                for c in range(first, first + GROUP, LANES // wide):
                    columns = slice(c * wide, c * wide + LANES)
                    block = fold_rows(weight_ref, k, j * per_tile, per_tile, columns).T
                    turned_ref[tile, columns, :] = block
                    for h in range(LANES // wide):
                        weight = block[h * wide : (h + 1) * wide]
                        real = jnp.broadcast_to(modes_ref[tile, c + h : c + h + 1, :], (wide, LANES))
                        imag = jnp.broadcast_to(
                            modes_ref[tile, channels + c + h : channels + c + h + 1, :], (wide, LANES)
                        )
                        real, imag = real.astype(jnp.bfloat16) * weight, imag.astype(jnp.bfloat16) * weight
                        real_sum = real if real_sum is None else real_sum + real
                        imag_sum = imag if imag_sum is None else imag_sum + imag
                by_real += real_sum.astype(jnp.float32)
                by_imag += imag_sum.astype(jnp.float32)
            store_pair(
                tile, channels, by_real[:channels] - by_imag[channels:],
                by_real[channels:] + by_imag[:channels], pair_ref,
            )
        to_cells(k, share, channels, halves, pair_ref, inverse_ref, out_ref)

    sent_ref[...] = out_ref[...].astype(jnp.bfloat16)


def row_sums(blocks):
    row = lax.broadcasted_iota(jnp.int32, (8, LANES), 0)
    for shift in (4, 2, 1):
        merged = []
        clear = row % (2 * shift) < shift
        for i in range(shift):
            first, second = blocks[i], blocks[i + shift]
            merged.append(
                jnp.where(clear, first + pltpu.roll(first, 8 - shift, 0), second + pltpu.roll(second, shift, 0))
            )
        blocks = merged
    return blocks[0]


def adjoint_kernel(
    share, channels, halves, arrived_ref, turned_ref, forward_ref, inverse_ref, sent_ref, modes_ref, wide_ref,
    out_ref, pair_ref,
):
    to_plane_modes(share, channels, halves, arrived_ref, forward_ref, wide_ref, modes_ref)
    wide = 2 * channels
    each = modes_ref.shape[0] // share

    for tile in range(modes_ref.shape[0]):
        real, imag = modes_ref[tile, :channels, :], modes_ref[tile, channels:, :]
        here = jnp.concatenate([real, imag], 0).astype(jnp.bfloat16)
        turn = jnp.concatenate([imag, -real], 0).astype(jnp.bfloat16)
        sums = ([], [])
        for first in range(0, channels, 8):
            blocks = ([], [])
            for c in range(first, first + 8):
                weight = turned_ref[tile, c * wide : (c + 1) * wide, :]
                for part, factor in enumerate((here, turn)):
                    product = factor * weight
                    product = product[: wide // 2] + product[wide // 2 :]
                    product = (product[: wide // 4] + product[wide // 4 :]).astype(jnp.float32)
                    blocks[part].append(product[:8] + product[8:])
            for part in range(2):
                sums[part].append(row_sums(blocks[part]))
        store_pair(tile, channels, jnp.concatenate(sums[0], 0), jnp.concatenate(sums[1], 0), pair_ref)
        if (tile + 1) % each == 0:
            to_cells(tile // each, share, channels, halves, pair_ref, inverse_ref, out_ref)

    sent_ref[...] = out_ref[...].astype(jnp.bfloat16)


def outer_kernel(share, channels, in_ref, back_ref, slope_ref, point_ref, grad_ref, pointwise_ref, held_ref, sems):
    wide = 2 * channels
    each = in_ref.shape[0] // share
    per_block = LANES // wide
    per_tile = LANES // LENGTH

    def runs(j):
        inside = [kx for kx in range(KX) if residue_of(kx) // per_tile == j]
        found = []
        for kx in inside:
            if found and found[-1][0] + found[-1][2] == kx and found[-1][1] + found[-1][2] == residue_of(kx):
                found[-1][2] += 1
            else:
                found.append([kx, residue_of(kx), 1])
        return found

    def copies(k, j):
        made = []
        for place, (mode, residue, count) in enumerate(runs(j)):
            source = pl.ds(pl.multiple_of((k * LENGTH + residue) * KY, 8), count * KY)
            target = pl.ds(pl.multiple_of((k * KX + mode) * KY, 8), count * KY)
            made.append(
                pltpu.make_async_copy(held_ref.at[source], grad_ref.at[target], sems.at[k * each + j, place])
            )
        return made

    low = lax.broadcasted_iota(jnp.int32, (8, LANES), 0) < 4

    @pl.loop(0, share)
    def _(k):
        for j in range(each):
            tile = k * each + j
            real, imag = back_ref[tile, :channels, :], back_ref[tile, channels:, :]
            here = jnp.concatenate([real, imag], 0)
            turn = jnp.concatenate([imag, -real], 0)
            for c in range(0, channels, per_block):
                parts = [
                    in_ref[tile, c + h : c + h + 1, :] * here
                    + in_ref[tile, channels + c + h : channels + c + h + 1, :] * turn
                    for h in range(per_block)
                ]
                block = jnp.concatenate(parts, 0).T
                for i in range(per_tile):
                    first = block[i * LENGTH : i * LENGTH + 8]
                    second = block[i * LENGTH + 8 : (i + 1) * LENGTH]
                    rows = pl.ds(pl.multiple_of((k * LENGTH + j * per_tile + i) * KY, 8), KY)
                    held_ref[rows, c * wide : c * wide + LANES] = jnp.concatenate(
                        [first, jnp.where(low, second, first), second], 0
                    )
            for copy in copies(k, j):
                copy.start()

    for first in range(0, slope_ref.shape[0], channels):
        rows = slice(first, first + channels)
        pointwise_ref[rows, :] = dot(point_ref[...], slope_ref[rows, :])

    @pl.loop(0, share)
    def _(k):
        for j in range(each):
            for copy in copies(k, j):
                copy.wait()


def slope_kernel(
    cells, channels, factor, units, arrived_ref, table_ref, field_ref, cotangent_ref, point_ref, slope_ref, sent_ref,
    wide_ref,
):
    arrived = received_slots(arrived_ref, cells * channels // LANES, units, wide_ref)
    spectral = dot(arrived.astype(jnp.bfloat16), table_ref[...], 0, 0)
    for c in range(cells):
        rows = slice(c * channels, (c + 1) * channels)
        before = spectral[rows] * factor + dot(point_ref[...], field_ref[rows, :], 0, 0)
        cumulative = 0.5 + 0.5 * lax.erf(before * math.sqrt(0.5))
        density = jnp.exp(-0.5 * before * before) * (1.0 / math.sqrt(2.0 * math.pi))
        slope = cotangent_ref[rows, :].astype(jnp.float32) * (cumulative + before * density)
        slope_ref[rows, :] = slope.astype(jnp.bfloat16)
    sent = dot(table_ref[...], slope_ref[...], 1, 1)
    send_slots(sent * factor, units, wide_ref, sent_ref)


def final_kernel(factor, halves, units, arrived_ref, table_ref, pointwise_ref, grad_hbm, wide_ref, grad_ref, sems):
    arrived = received_slots(arrived_ref, halves, units, wide_ref).astype(jnp.bfloat16)
    count = sems.shape[0]
    rows = grad_ref.shape[0] // count
    copies = []
    for part in range(count):
        here = slice(part * rows, (part + 1) * rows)
        spectral = dot(arrived[:, here], table_ref[...], 0, 0)
        grad_ref[here, :] = (pointwise_ref[here, :] + spectral * factor).astype(jnp.bfloat16)
        place = pl.ds(part * rows, rows)
        copies.append(pltpu.make_async_copy(grad_ref.at[place], grad_hbm.at[place], sems.at[part]))
        copies[-1].start()
    for copy in copies:
        copy.wait()


def params(mebibytes, semantics=None):
    return pltpu.CompilerParams(dimension_semantics=semantics, vmem_limit_bytes=mebibytes * 1024 * 1024)


def on_chip(value):
    return pltpu.with_memory_space_constraint(value, pltpu.VMEM)


def off_chip(value):
    return pltpu.with_memory_space_constraint(value, pltpu.HBM)


IN_VMEM = pl.BlockSpec(memory_space=pltpu.VMEM)


def per_device(inputs, cotangent, point_weight, spectral_weight):
    rows_x, rows_y, channels, depth = inputs.shape
    mode_rows, mode_cols, flat = spectral_weight.shape
    count_gx, count_gy = lax.axis_size("gx"), lax.axis_size("gy")
    devices = count_gx * count_gy
    share = mode_rows // KX
    cells = rows_x * rows_y
    lanes = cells * channels
    wide = 2 * channels
    plane = KX * KY
    points = cells * devices
    each = points // LANES
    tiles = share * each
    halves = lanes // LANES
    units = 2 * share * halves
    inner = 1.0 / math.sqrt(points * depth)
    outer = 1.0 / math.sqrt(plane * KZ * KT)

    table = on_chip(jnp.asarray(depth_table(share)))
    forward, inverse = (on_chip(jnp.asarray(t)) for t in plane_tables(count_gx, count_gy, rows_x, rows_y))
    field = on_chip(inputs.reshape(lanes, depth))
    seed = on_chip(cotangent.reshape(lanes, depth))
    point = on_chip(point_weight)

    def exchange(sent):
        blocks = sent.reshape(devices * units // 4, 4, LANES)
        arrived = lax.all_to_all(blocks, GRID_AXES, split_axis=0, concat_axis=0, tiled=True)
        return on_chip(arrived.reshape(devices * units, LANES))

    packet = pltpu.VMEM((devices * units, LANES), jnp.bfloat16)
    unpacked = pltpu.VMEM((devices * units, LANES), jnp.float32)
    spectra = pltpu.VMEM((tiles, wide, LANES), jnp.float32)

    sent = pl.pallas_call(
        functools.partial(depth_kernel, inner, units),
        in_specs=[IN_VMEM] * 2, out_specs=IN_VMEM, out_shape=packet, scratch_shapes=[unpacked],
        compiler_params=params(2),
        cost_estimate=pl.CostEstimate(flops=READ_AHEAD_FLOPS, transcendentals=0, bytes_accessed=0),
        name="depth",
    )(off_chip(jnp.asarray(depth_table(share))), off_chip(inputs.reshape(lanes, depth)))
    arrived = exchange(sent)
    scratch = [unpacked, unpacked, pltpu.VMEM((tiles, wide, 2 * LANES), jnp.bfloat16)]
    sent, modes_in, turned = pl.pallas_call(
        functools.partial(mix_kernel, share, channels, halves),
        in_specs=[IN_VMEM] * 4, out_specs=[IN_VMEM] * 3,
        out_shape=[packet, spectra, pltpu.VMEM((tiles, flat, LANES), jnp.bfloat16)],
        scratch_shapes=scratch, compiler_params=params(6), name="mix",
    )(arrived, on_chip(spectral_weight.reshape(share * plane, flat)), forward, inverse)
    arrived = exchange(sent)
    slope, sent = pl.pallas_call(
        functools.partial(slope_kernel, cells, channels, outer, units),
        in_specs=[IN_VMEM] * 5, out_specs=[IN_VMEM] * 2, out_shape=[pltpu.VMEM((lanes, depth), jnp.bfloat16), packet],
        scratch_shapes=[unpacked],
        compiler_params=params(8), name="slope",
    )(arrived, table, field, seed, point)
    arrived = exchange(sent)
    sent, modes_back = pl.pallas_call(
        functools.partial(adjoint_kernel, share, channels, halves),
        in_specs=[IN_VMEM] * 4, out_specs=[IN_VMEM] * 2, out_shape=[packet, spectra],
        scratch_shapes=scratch,
        compiler_params=params(12), name="adjoint",
    )(arrived, on_chip(turned), forward, inverse)
    arrived = exchange(sent)
    grad_spectral, pointwise = pl.pallas_call(
        functools.partial(outer_kernel, share, channels),
        in_specs=[IN_VMEM] * 4, out_specs=[pl.BlockSpec(memory_space=pl.ANY), IN_VMEM],
        out_shape=[
            jax.ShapeDtypeStruct((share * plane, flat), jnp.float32), pltpu.VMEM((lanes, depth), jnp.float32),
        ],
        scratch_shapes=[
            pltpu.VMEM((share * LENGTH * KY, flat), jnp.float32), pltpu.SemaphoreType.DMA((tiles, 2)),
        ],
        compiler_params=params(24),
        cost_estimate=pl.CostEstimate(
            flops=4 * share * plane * flat * wide, transcendentals=0, bytes_accessed=4 * share * plane * flat
        ),
        name="outer",
    )(on_chip(modes_in), on_chip(modes_back), on_chip(slope), point)
    grad_input = pl.pallas_call(
        functools.partial(final_kernel, inner, halves, units),
        in_specs=[IN_VMEM] * 3, out_specs=pl.BlockSpec(memory_space=pl.ANY),
        out_shape=jax.ShapeDtypeStruct((lanes, depth), jnp.bfloat16),
        scratch_shapes=[unpacked, pltpu.VMEM((lanes, depth), jnp.bfloat16), pltpu.SemaphoreType.DMA((2,))],
        compiler_params=params(8), name="final",
    )(arrived, table, on_chip(pointwise))
    return grad_input.reshape(inputs.shape), grad_spectral.reshape(spectral_weight.shape)


def kept_angles(positions, kept_count, length):
    index = jnp.arange(kept_count, dtype=jnp.int32)
    frequency = jnp.where(index < kept_count // 2, index, index - kept_count)
    turns = positions[:, None] * frequency[None, :] % length
    return turns.astype(jnp.float32) * (2.0 * math.pi / length)


def axis_tables(positions, kept_count, length):
    angles = kept_angles(positions, kept_count, length)
    return (jnp.cos(angles), jnp.sin(angles))


def depth_tables():
    angle_depth = kept_angles(jnp.arange(NZ, dtype=jnp.int32), KZ, NZ)
    angle_time = kept_angles(jnp.arange(NT, dtype=jnp.int32), KT, NT)
    angles = (angle_depth[:, None, :, None] + angle_time[None, :, None, :]).reshape(
        NZ * NT, KZ * KT
    )
    return (jnp.cos(angles), jnp.sin(angles))


def settle(values):
    return lax.optimization_barrier(values.astype(jnp.bfloat16))


def rotate(spectra, cosine_table, sine_table, pattern, turn_sign):
    half_width = spectra.shape[-1] // 2
    with_cosine = jnp.einsum(pattern, spectra, cosine_table, precision=lax.Precision.HIGHEST)
    with_sine = jnp.einsum(pattern, spectra, sine_table, precision=lax.Precision.HIGHEST)
    real_part = with_cosine[..., :half_width] + turn_sign * with_sine[..., half_width:]
    imag_part = with_cosine[..., half_width:] - turn_sign * with_sine[..., :half_width]
    return jnp.concatenate([real_part, imag_part], -1)


def depth_forward(field_in, tables, factor):
    widened = field_in.astype(jnp.float32)
    with_cosine = jnp.einsum("xycs,sk->kxyc", widened, tables[0], precision=lax.Precision.HIGHEST)
    with_sine = jnp.einsum("xycs,sk->kxyc", widened, tables[1], precision=lax.Precision.HIGHEST)
    return jnp.concatenate([with_cosine, -with_sine], -1) * factor


def depth_inverse(spectra, tables, factor):
    half_width = spectra.shape[-1] // 2
    with_cosine = jnp.einsum(
        "kxyc,sk->xycs", spectra[..., :half_width], tables[0], precision=lax.Precision.HIGHEST
    )
    with_sine = jnp.einsum(
        "kxyc,sk->xycs", spectra[..., half_width:], tables[1], precision=lax.Precision.HIGHEST
    )
    return (with_cosine - with_sine) * factor


def contract_in(left, right):
    return jnp.einsum("mkc,mkco->mko", left, right, precision=lax.Precision.HIGHEST)


def contract_out(left, right):
    return jnp.einsum("mko,mkco->mkc", left, right, precision=lax.Precision.HIGHEST)


def partial_outer(left, right):
    return jnp.einsum("mkc,mko->mkco", left, right, precision=lax.Precision.HIGHEST)


def mix_modes(spectra, weight):
    half_width = spectra.shape[-1] // 2
    weight_wide = weight.astype(jnp.float32)
    weight_real, weight_imag = (weight_wide[..., :half_width], weight_wide[..., half_width:])
    real_in, imag_in = (spectra[..., :half_width], spectra[..., half_width:])
    real_out = contract_in(real_in, weight_real) - contract_in(imag_in, weight_imag)
    imag_out = contract_in(real_in, weight_imag) + contract_in(imag_in, weight_real)
    return jnp.concatenate([real_out, imag_out], -1)


def adjoint_modes(spectra, weight):
    half_width = spectra.shape[-1] // 2
    weight_wide = weight.astype(jnp.float32)
    weight_real, weight_imag = (weight_wide[..., :half_width], weight_wide[..., half_width:])
    real_in, imag_in = (spectra[..., :half_width], spectra[..., half_width:])
    real_out = contract_out(real_in, weight_real) + contract_out(imag_in, weight_imag)
    imag_out = contract_out(imag_in, weight_real) - contract_out(real_in, weight_imag)
    return jnp.concatenate([real_out, imag_out], -1)


def weight_grad(spectra_in, spectra_back):
    half_width = spectra_in.shape[-1] // 2
    real_in, imag_in = (spectra_in[..., :half_width], spectra_in[..., half_width:])
    real_back, imag_back = (spectra_back[..., :half_width], spectra_back[..., half_width:])
    real_part = partial_outer(real_in, real_back) + partial_outer(imag_in, imag_back)
    imag_part = partial_outer(real_in, imag_back) - partial_outer(imag_in, real_back)
    return jnp.concatenate([real_part, imag_part], -1)


def exact_gelu(values):
    return jax.nn.gelu(values, approximate=False)


def general_per_device(inputs, cotangent, point_weight, spectral_weight):
    rows_x, rows_y, channels, cells = inputs.shape
    mode_rows, mode_cols, flat_width = spectral_weight.shape
    weight_blocks = spectral_weight.reshape(mode_rows, mode_cols, channels, 2 * channels)
    count_gx = lax.axis_size("gx")
    count_gy = lax.axis_size("gy")
    length_x = rows_x * count_gx
    length_y = rows_y * count_gy
    depth_pair = depth_tables()
    own_x = lax.axis_index("gx") * rows_x + jnp.arange(rows_x, dtype=jnp.int32)
    local_x = axis_tables(own_x, KX, length_x)
    whole_y = axis_tables(jnp.arange(length_y, dtype=jnp.int32), KY, length_y)
    total_cells = length_x * length_y * cells
    kept_total = KX * KY * KZ * KT

    def to_modes(field_in, factor):
        depth_spec = settle(depth_forward(field_in, depth_pair, factor))
        share = depth_spec.shape[0] // count_gx
        first_spectra = lax.psum_scatter(
            rotate(
                depth_spec.astype(jnp.float32), local_x[0], local_x[1], "rxyc,xk->rkyc", 1.0
            ).astype(jnp.bfloat16),
            "gx",
            scatter_dimension=0,
            tiled=True,
        ).astype(jnp.float32)
        first_spectra = settle(first_spectra).reshape(share * KX, rows_y, 2 * channels)
        arrived_modes = lax.all_to_all(first_spectra, "gy", split_axis=0, concat_axis=1, tiled=True)
        return rotate(arrived_modes.astype(jnp.float32), whole_y[0], whole_y[1], "myc,yk->mkc", 1.0)

    def to_space(spectra, factor):
        back_rows = settle(rotate(spectra, whole_y[0], whole_y[1], "mkc,yk->myc", -1.0))
        returned = lax.all_to_all(back_rows, "gy", split_axis=1, concat_axis=0, tiled=True)
        share = returned.shape[0] // KX
        returned = returned.reshape(share, KX, rows_y, 2 * channels)
        back_depth = settle(
            rotate(
                lax.all_gather(returned, "gx", axis=0, tiled=True).astype(jnp.float32),
                local_x[0],
                local_x[1],
                "rkyc,xk->rxyc",
                -1.0,
            )
        )
        return depth_inverse(back_depth.astype(jnp.float32), depth_pair, factor)

    spectra_in = to_modes(inputs, 1.0 / math.sqrt(total_cells))
    mixed = mix_modes(spectra_in, weight_blocks)
    spectral_out = to_space(mixed, 1.0 / math.sqrt(kept_total))
    pointwise = jnp.einsum(
        "xycs,co->xyos", inputs, point_weight, preferred_element_type=jnp.float32
    )
    before = spectral_out + pointwise
    unused_out, pullback = jax.vjp(exact_gelu, before)
    slope = settle(pullback(cotangent.astype(jnp.float32))[0])
    spectra_back = to_modes(slope, 1.0 / math.sqrt(kept_total))
    grad_spectral = weight_grad(spectra_in, spectra_back).reshape(mode_rows, mode_cols, flat_width)
    adjoint = adjoint_modes(spectra_back, weight_blocks)
    spectral_grad = to_space(adjoint, 1.0 / math.sqrt(total_cells))
    pointwise_grad = jnp.einsum(
        "xyos,co->xycs", slope, point_weight, preferred_element_type=jnp.float32
    )
    grad_input = (pointwise_grad + spectral_grad).astype(jnp.bfloat16)
    return (grad_input, grad_spectral)


def solution(mesh):
    count_gx, count_gy = mesh.shape["gx"], mesh.shape["gy"]
    placed = (
        P("gx", "gy", None, None),
        P("gx", "gy", None, None),
        P(),
        P(("gx", "gy"), None, None),
    )

    def program(inputs, cotangent, point_weight, spectral_weight):
        cells = inputs.shape[0] * inputs.shape[1] // (count_gx * count_gy)
        whole_modes = KZ * KT % (count_gx * count_gy) == 0
        fits = whole_modes and KZ * KT // (count_gx * count_gy) == 3
        fits = fits and inputs.shape[2] == 32 and cells * inputs.shape[2] == 256 and inputs.shape[0] == inputs.shape[1] == LENGTH
        return jax.shard_map(
            per_device if fits else general_per_device,
            mesh=mesh,
            in_specs=placed,
            out_specs=(P("gx", "gy", None, None), P(("gx", "gy"), None, None)),
            check_vma=False,
        )(inputs, cotangent, point_weight, spectral_weight)

    return program
```
